128 devices in a mesh: blk: 32 (over y, z, core), gz: 4 (over x).
Axes of the slice: x: 4, y: 4, z: 4, core: 2. Of those that a mesh axis runs over, the one named last changes fastest.
Arguments:
- populations: float32 [19, 160, 8192], P(None, 'blk', 'gz'), may hold values from 0 to 1, as said below
- target: bfloat16 [19, 160, 8192], P(None, 'blk', 'gz'), may hold values from -1 to 1
- solid_frac: float32 [160, 8192], P('blk', 'gz'), may hold values from 0 to 0.5
- wall_mask: int32 [160, 8192], P('blk', 'gz'), may hold values 0 or 1
- slot_column: int32 [160], P('blk'), may hold values from -1 to 7, as said below
Outputs:
- solid_gradient: float32 [160, 8192], P('blk', 'gz')
- start_adjoint: float32 [19, 160, 8192], P(None, 'blk', 'gz')
The draws below stay inside these ranges and needn't reach their ends.
Inputs may be any that keep to these rules, and one draw needn't show every extreme that they name: Near-equilibrium populations, positive. `slot_column`: the 5 entries of one row list the column positions it holds in increasing order, then -1; every row holds at least one column and some row holds 5.
All inputs are finite; a program needn't handle non-finite values. No bound on the sum of `wall_mask` on one device may be relied on, other than what follows from the above.
Results may differ from the reference program's by a relative error of at most 0.0003.
Values sent between devices are 32-bit elements; how exact they have to be, the bound alone decides.
No kernel may reach another device: no remote copies, remote signals or barrier semaphores. Data moves between devices by JAX's collectives and lax.ppermute only.
A program may use at most 128 MiB of HBM per device.

```python
import jax
import jax.numpy as jnp
import numpy as np
from jax import lax

EDGE = 16
GY = 8
SLOTS = 5
DZ = 8
ROWS = 32
NS = 160
NZ = 32
N_GZ = 4


def lattice_columns():
    velocity = jnp.array([[0, 0, 0], [1, 0, 0], [-1, 0, 0], [0, 1, 0], [0, -1, 0], [0, 0, 1], [0, 0, -1], [1, 1, 0], [-1, -1, 0], [1, -1, 0], [-1, 1, 0], [1, 0, 1], [-1, 0, -1], [1, 0, -1], [-1, 0, 1], [0, 1, 1], [0, -1, -1], [0, 1, -1], [0, -1, 1]], jnp.float32)
    weights = jnp.array([1.0 / 3.0] + [1.0 / 18.0] * 6 + [1.0 / 36.0] * 12, jnp.float32)
    return (velocity, weights)


def draw_populations(key, part):
    velocity, weights = lattice_columns()
    cells = NZ * EDGE * EDGE
    first, second = jax.random.split(jax.random.fold_in(key, 11), 2)
    flow = jax.random.uniform(first, (3, NS, cells), jnp.float32, -0.05, 0.05)
    noise = 0.4 * jax.random.uniform(second, (19, NS, cells), jnp.float32, -1.0, 1.0)
    projected = velocity[:, 0][:, None, None] * flow[0][None] + velocity[:, 1][:, None, None] * flow[1][None] + velocity[:, 2][:, None, None] * flow[2][None]
    return weights[:, None, None] * (1.0 + 3.0 * projected + noise)


def draw_target(key, part):
    velocity, weights = lattice_columns()
    cells = NZ * EDGE * EDGE
    second = jax.random.fold_in(jax.random.fold_in(key, 23), 1)
    noise = 0.5 * jnp.clip(jax.random.normal(second, (19, NS, cells), jnp.float32), -2.0, 2.0)
    return (weights[:, None, None] * (1.0 + noise)).astype(jnp.bfloat16)


def draw_slot_column(key, part):
    first, second, third = jax.random.split(jax.random.fold_in(key, 37), 3)
    counts = jax.random.randint(first, (ROWS,), 1, SLOTS + 1)
    fullest = jax.random.randint(second, (), 0, ROWS)
    counts = jnp.where(jnp.arange(ROWS) == fullest, SLOTS, counts)
    scores = jax.random.randint(third, (ROWS, GY), 0, 1 << 20) * GY + jnp.arange(GY)[None, :]
    ordering = jnp.argsort(scores, axis=1)
    chosen = ordering[:, :SLOTS]
    keeping = jnp.arange(SLOTS)[None, :] < counts[:, None]
    candidate = jnp.where(keeping, chosen, GY)
    ranked = jnp.sort(candidate, axis=1)
    return jnp.where(ranked == GY, -1, ranked).reshape(NS).astype(jnp.int32)


def place_ends(values, key, least, largest):
    extent = values.shape
    index_at = [jax.random.randint(jax.random.fold_in(key, axis), (), 0, extent[axis]) for axis in range(len(extent))]
    values = values.at[tuple(index_at)].set(least)
    longest = extent.index(max(extent))
    index_at[longest] = (index_at[longest] + 1) % extent[longest]
    return values.at[tuple(index_at)].set(largest)


def steps_of(stream_key, extent, cuts, low, high):
    def one(position, parts):
        heights = jax.random.uniform(jax.random.fold_in(jax.random.fold_in(stream_key, 6), position), (parts,), jnp.float32, low / len(cuts), high / len(cuts))
        return jnp.repeat(jnp.exp(heights), extent[position] // parts).reshape((-1,) + (1,) * (len(extent) - position - 1))

    gain = one(*cuts[0])
    for cut in cuts[1:]:
        gain = gain * one(*cut)
    return gain


def setup_inputs(seed: int = 0) -> dict:
    key_list = jax.random.split(jax.random.key(seed), 6)
    populations = draw_populations(jax.random.fold_in(key_list[5], 71), 0)
    target = draw_target(jax.random.fold_in(key_list[5], 71), 0)
    solid_frac = jnp.clip(0.5 * jax.random.uniform(key_list[2], (NS, NZ * EDGE * EDGE), jnp.float32) ** steps_of(key_list[2], (NS, NZ * EDGE * EDGE), ((0, 32), (1, 4)), -0.2, 0.2), 0.0, 0.5)
    wall_mask = place_ends((jax.random.randint(key_list[3], (NS, NZ * EDGE * EDGE), 0, 8) < 1).astype(jnp.int32), jax.random.fold_in(key_list[3], 1), 0, 1)
    slot_column = draw_slot_column(jax.random.fold_in(key_list[5], 71), 0)
    return {"populations": populations, "target": target, "solid_frac": solid_frac, "wall_mask": wall_mask, "slot_column": slot_column}


HIGH = lax.Precision.HIGHEST

def invert_matrix(square):
    count = len(square)
    augmented = [[float(value) for value in square[line]] + [1.0 if other == line else 0.0 for other in range(count)] for line in range(count)]
    for column_index in range(count):
        pivot_index = max(range(column_index, count), key=lambda candidate: abs(augmented[candidate][column_index]))
        augmented[column_index], augmented[pivot_index] = (augmented[pivot_index], augmented[column_index])
        leader = augmented[column_index][column_index]
        augmented[column_index] = [value / leader for value in augmented[column_index]]
        for line in range(count):
            if line != column_index:
                factor = augmented[line][column_index]
                augmented[line] = [value - factor * pivot_value for value, pivot_value in zip(augmented[line], augmented[column_index])]
    return np.array([entries[count:] for entries in augmented])

def lattice_tables():
    velocity = np.array([[0, 0, 0], [1, 0, 0], [-1, 0, 0], [0, 1, 0], [0, -1, 0], [0, 0, 1], [0, 0, -1], [1, 1, 0], [-1, -1, 0], [1, -1, 0], [-1, 1, 0], [1, 0, 1], [-1, 0, -1], [1, 0, -1], [-1, 0, 1], [0, 1, 1], [0, -1, -1], [0, 1, -1], [0, -1, 1]])
    weights = np.array([1.0 / 3.0] + [1.0 / 18.0] * 6 + [1.0 / 36.0] * 12)
    opposite = [0, 2, 1, 4, 3, 6, 5, 8, 7, 10, 9, 12, 11, 14, 13, 16, 15, 18, 17]
    powers = [(0, 0, 0), (1, 0, 0), (0, 1, 0), (0, 0, 1), (2, 0, 0), (0, 2, 0), (0, 0, 2), (1, 1, 0), (1, 0, 1), (0, 1, 1), (1, 2, 0), (1, 0, 2), (2, 1, 0), (0, 1, 2), (2, 0, 1), (0, 2, 1), (2, 2, 0), (2, 0, 2), (0, 2, 2)]
    moments = np.array([[float(np.prod(velocity[index] ** np.array(power))) for index in range(19)] for power in powers])
    relax_rates = np.array([0.0] * 4 + [1.6] * 6 + [1.2] * 6 + [1.0] * 3)
    relax_matrix = invert_matrix(moments) @ (relax_rates[:, None] * moments)
    return (velocity, weights, opposite, relax_matrix)

def collide(field, fraction):
    velocity, weights, opposite, relax_matrix = lattice_tables()
    initial = field.shape
    flattened = field.reshape(19, -1)
    share = fraction.reshape(-1)
    lattice = jnp.asarray(velocity, jnp.float32)
    density = lax.optimization_barrier(jnp.sum(flattened, axis=0))
    momentum = jnp.dot(lattice.T, flattened, precision=HIGH)
    projected = jnp.dot(lattice, momentum, precision=HIGH)
    speed_sq = lax.optimization_barrier(jnp.sum(momentum * momentum, axis=0))
    equilibrium = jnp.asarray(weights, jnp.float32)[:, None] * (density + 3.0 * projected + 4.5 * projected * projected - 1.5 * speed_sq)
    relaxed = flattened - jnp.dot(jnp.asarray(relax_matrix, jnp.float32), flattened - equilibrium, precision=HIGH)
    result = (1.0 - share) * relaxed + share * flattened[jnp.asarray(opposite)]
    return result.reshape(initial)

def collide_pullback(field, fraction, cotangent):
    primal, pullback = jax.vjp(collide, field, fraction)
    return pullback(cotangent)

def over_depth(func, *arrays):

    def split(array):
        grouped = array.reshape(array.shape[:-3] + (N_GZ, DZ) + array.shape[-2:])
        return jnp.moveaxis(grouped, -4, 0)

    def merge(array):
        joined = jnp.moveaxis(array, 0, -4)
        return joined.reshape(joined.shape[:-4] + (N_GZ * DZ,) + joined.shape[-2:])
    outputs = lax.map(lambda group: func(*group), tuple((split(a) for a in arrays)))
    return jax.tree.map(merge, outputs)

def propagate(field, direction):
    velocity = lattice_tables()[0]
    depth_cells, row_cells, col_cells = (field.shape[1], field.shape[2], field.shape[3])
    padded = jnp.pad(field, ((0, 0), (1, 1), (1, 1), (1, 1)))
    pieces = []
    for index in range(19):
        start_x = 1 - direction * int(velocity[index][0])
        start_y = 1 - direction * int(velocity[index][1])
        start_z = 1 - direction * int(velocity[index][2])
        pieces.append(padded[index, start_z:start_z + depth_cells, start_x:start_x + row_cells, start_y:start_y + col_cells])
    return jnp.stack(pieces)

def reference(populations, target, solid_frac, wall_mask, slot_column):
    weights = lattice_tables()[1]
    layout = slot_column.reshape(ROWS, SLOTS)
    chooser = (layout[:, None, :] == jnp.arange(GY, dtype=jnp.int32)[None, :, None]).astype(jnp.float32)

    def spread(packed):
        leading = packed.shape[:-2]
        blocked = packed.astype(jnp.float32).reshape(leading + (ROWS, SLOTS, NZ, EDGE, EDGE))
        dense_field = jnp.einsum('rgk,...rkzxy->...zrxgy', chooser, blocked, precision=HIGH)
        return dense_field.reshape(leading + (NZ, ROWS * EDGE, GY * EDGE))

    def pack_slots(dense_field):
        leading = dense_field.shape[:-3]
        blocked = dense_field.reshape(leading + (NZ, ROWS, EDGE, GY, EDGE))
        packed = jnp.einsum('rgk,...zrxgy->...rkzxy', chooser, blocked, precision=HIGH)
        return packed.reshape(leading + (NS, NZ * EDGE * EDGE))
    listed = spread(jnp.ones((NS, NZ * EDGE * EDGE), jnp.float32))
    fraction = spread(jnp.where(wall_mask == 1, jnp.float32(1.0), solid_frac))
    field0 = spread(populations)

    def advance(field):
        return listed * propagate(over_depth(collide, field, fraction), 1)
    field1 = advance(field0)
    field2 = advance(field1)
    weight_col = jnp.asarray(weights, jnp.float32)[:, None, None, None]
    cot2 = listed * (field2 - spread(target)) / weight_col

    def retreat(cotangent, field):
        pulled = propagate(cotangent, -1)
        field_cot, frac_cot = over_depth(collide_pullback, field, fraction, pulled)
        return (listed * field_cot, frac_cot)
    cot1, gain2 = retreat(cot2, field1)
    cot0, gain1 = retreat(cot1, field0)
    gradient = jnp.where(wall_mask == 1, jnp.float32(0.0), pack_slots(gain1 + gain2))
    return (gradient, pack_slots(cot0))
```

```python
import functools

import jax
import jax.numpy as jnp
import numpy as np
from jax import lax
from jax.experimental import pallas as pl
from jax.experimental.pallas import tpu as pltpu
from jax.sharding import PartitionSpec as P

EDGE = 16
GY = 8
SLOTS = 5
DZ = 8
CELLS = DZ * EDGE * EDGE

VEL = (
    (0, 0, 0),
    (1, 0, 0), (-1, 0, 0), (0, 1, 0), (0, -1, 0), (0, 0, 1), (0, 0, -1),
    (1, 1, 0), (-1, -1, 0), (1, -1, 0), (-1, 1, 0),
    (1, 0, 1), (-1, 0, -1), (1, 0, -1), (-1, 0, 1),
    (0, 1, 1), (0, -1, -1), (0, 1, -1), (0, -1, 1),
)
OPP = (0, 2, 1, 4, 3, 6, 5, 8, 7, 10, 9, 12, 11, 14, 13, 16, 15, 18, 17)
INV_W = (3.0,) + (18.0,) * 6 + (36.0,) * 12
CX = [v[0] for v in VEL]
CY = [v[1] for v in VEL]
CZ = [v[2] for v in VEL]

NF = 38
ZI = 10
ROWS_STORE = 256


def vel(n):
    return VEL[n % 19]


def z_planes(up):
    sign = 1 if up else -1
    edge, inner = (DZ - 1, DZ - 2) if up else (0, 1)
    ghost, first = (-1, 0) if up else (DZ, DZ - 1)
    planes = []
    for n in range(NF):
        cz = vel(n)[2]
        if cz == 0:
            planes.append((n, edge, ghost))
        elif cz == sign:
            planes.append((n, inner, ghost))
            planes.append((n, edge, first))
    return planes


def x_planes(right):
    sign = 1 if right else -1
    edge, inner = (EDGE - 1, EDGE - 2) if right else (0, 1)
    planes = []
    for n in range(NF):
        cx = vel(n)[0]
        if cx == 0:
            planes.append((n, edge, "ghost"))
        elif cx == sign:
            planes.append((n, inner, "ghost"))
            planes.append((n, edge, "edge"))
    return planes


ZUP, ZDN = z_planes(True), z_planes(False)
XRT, XLT = x_planes(True), x_planes(False)
NP = len(ZUP)
ZROWS = 200
XROWS = 400


def moments(f):
    m = {}

    def pair(a):
        return f[a] + f[a + 1], f[a] - f[a + 1]

    sx, dx = pair(1)
    sy, dy = pair(3)
    sz, dz = pair(5)
    for name, a, t1, t2 in (("xy", 7, "xyy", "xxy"), ("xz", 11, "xzz", "xxz"), ("yz", 15, "yzz", "yyz")):
        sa, da = pair(a)
        sb, db = pair(a + 2)
        m["Q" + name] = sa + sb
        m["P" + name] = sa - sb
        m["T" + t1] = da + db
        m["T" + t2] = da - db
    qa = m["Qxy"] + m["Qxz"]
    m["Pxx"] = sx + qa
    m["Pyy"] = sy + (m["Qxy"] + m["Qyz"])
    m["Pzz"] = sz + (m["Qxz"] + m["Qyz"])
    m["rho"] = (f[0] + sx) + (sy + sz) + (qa + m["Qyz"])
    m["jx"] = dx + (m["Txyy"] + m["Txzz"])
    m["jy"] = dy + (m["Txxy"] + m["Tyzz"])
    m["jz"] = dz + (m["Txxz"] + m["Tyyz"])
    return m


def defects(m):
    ux, uy, uz = m["jx"], m["jy"], m["jz"]
    xx, yy, zz = ux * ux, uy * uy, uz * uz
    third = m["rho"] * (1.0 / 3.0)
    ninth = m["rho"] * (1.0 / 9.0) - (xx + yy + zz) * (1.0 / 6.0)
    d = {}
    d["Pxx"] = third + xx - m["Pxx"]
    d["Pyy"] = third + yy - m["Pyy"]
    d["Pzz"] = third + zz - m["Pzz"]
    d["Pxy"] = ux * uy - m["Pxy"]
    d["Pxz"] = ux * uz - m["Pxz"]
    d["Pyz"] = uy * uz - m["Pyz"]
    d["Qxy"] = ninth + (xx + yy) * 0.5 - m["Qxy"]
    d["Qxz"] = ninth + (xx + zz) * 0.5 - m["Qxz"]
    d["Qyz"] = ninth + (yy + zz) * 0.5 - m["Qyz"]
    return d


P_NAMES = ("Pxx", "Pyy", "Pzz", "Pxy", "Pxz", "Pyz")
Q_NAMES = ("Qxy", "Qxz", "Qyz")
T_OF = {"x": ("Txyy", "Txzz"), "y": ("Txxy", "Tyzz"), "z": ("Txxz", "Tyyz")}


def collide(m, d, s):
    h = 1.0 - s
    h16 = 1.6 * h
    t_keep = 0.8 * h - 1.0
    h04 = 0.4 * h
    j_keep = h - s
    o = {}
    for name in P_NAMES:
        o[name] = m[name] + h16 * d[name]
    for name in Q_NAMES:
        o[name] = m[name] + h * d[name]
    for axis in "xyz":
        j = m["j" + axis]
        o["j" + axis] = j_keep * j
        hj = h04 * j
        for name in T_OF[axis]:
            o[name] = t_keep * m[name] + hj
    f = [None] * 19
    qs = (o["Qxy"] + o["Qxz"]) + o["Qyz"]
    f[0] = (m["rho"] + qs) - ((o["Pxx"] + o["Pyy"]) + o["Pzz"])
    for a, p, q1, q2, axis in ((1, "Pxx", "Qxy", "Qxz", "x"), (3, "Pyy", "Qxy", "Qyz", "y"), (5, "Pzz", "Qxz", "Qyz", "z")):
        s_ = (o[p] - (o[q1] + o[q2])) * 0.5
        d_ = (o["j" + axis] - (o[T_OF[axis][0]] + o[T_OF[axis][1]])) * 0.5
        f[a] = s_ + d_
        f[a + 1] = s_ - d_
    for name, a, t1, t2 in (("xy", 7, "Txyy", "Txxy"), ("xz", 11, "Txzz", "Txxz"), ("yz", 15, "Tyzz", "Tyyz")):
        q = o["Q" + name] * 0.25
        p = o["P" + name] * 0.25
        u = o[t1] * 0.25
        w = o[t2] * 0.25
        sa, sb, da, db = q + p, q - p, u + w, u - w
        f[a] = sa + da
        f[a + 1] = sa - da
        f[a + 2] = sb + db
        f[a + 3] = sb - db
    return f


def adjoint(m, d, s, q):
    h = 1.0 - s
    h16 = 1.6 * h
    t_keep = 0.8 * h - 1.0
    h04 = 0.4 * h
    j_keep = h - s
    t = {}
    half = {}
    for axis, a in (("x", 1), ("y", 3), ("z", 5)):
        half[axis] = (q[a] + q[a + 1]) * 0.5
        t["j" + axis] = (q[a] - q[a + 1]) * 0.5
        t["P" + axis + axis] = half[axis] - q[0]
    for name, a, t1, t2 in (("xy", 7, "Txyy", "Txxy"), ("xz", 11, "Txzz", "Txxz"), ("yz", 15, "Tyzz", "Tyyz")):
        sa, da = q[a] + q[a + 1], q[a] - q[a + 1]
        sb, db = q[a + 2] + q[a + 3], q[a + 2] - q[a + 3]
        t["Q" + name] = (sa + sb) * 0.25 - half[name[0]] - t["P" + name[1] * 2]
        t["P" + name] = (sa - sb) * 0.25
        t[t1] = (da + db) * 0.25 - t["j" + name[0]]
        t[t2] = (da - db) * 0.25 - t["j" + name[1]]
    gp = t["Pxx"] * d["Pxx"]
    for name in P_NAMES[1:]:
        gp = gp + t[name] * d[name]
    gq = t["Qxy"] * d["Qxy"] + t["Qxz"] * d["Qxz"] + t["Qyz"] * d["Qyz"]
    gt = None
    gj = None
    tsum = {}
    for axis in "xyz":
        tsum[axis] = t[T_OF[axis][0]] + t[T_OF[axis][1]]
        term = t[T_OF[axis][0]] * m[T_OF[axis][0]] + t[T_OF[axis][1]] * m[T_OF[axis][1]]
        gt = term if gt is None else gt + term
        term = (2.0 * t["j" + axis] + 0.4 * tsum[axis]) * m["j" + axis]
        gj = term if gj is None else gj + term
    gs = -(1.6 * gp + gq + gj + 0.8 * gt)
    ux, uy, uz = m["jx"], m["jy"], m["jz"]
    p_keep = 1.0 - h16
    qsum = t["Qxy"] + t["Qxz"] + t["Qyz"]
    u = {}
    u["rho"] = q[0] + (h16 * (1.0 / 3.0)) * (t["Pxx"] + t["Pyy"] + t["Pzz"]) + (h * (1.0 / 9.0)) * qsum
    third = qsum * (1.0 / 3.0)
    w16 = {"x": t["Pxy"] * uy + t["Pxz"] * uz, "y": t["Pxy"] * ux + t["Pyz"] * uz, "z": t["Pxz"] * ux + t["Pyz"] * uy}
    other = {"x": "Qyz", "y": "Qxz", "z": "Qxy"}
    for axis, uu in (("x", ux), ("y", uy), ("z", uz)):
        quad = 2.0 * third - t[other[axis]]
        u["j" + axis] = (
            j_keep * t["j" + axis]
            + h04 * tsum[axis]
            + h16 * (w16[axis] + 2.0 * t["P" + axis + axis] * uu)
            + h * (quad * uu)
        )
    for name in P_NAMES:
        u[name] = p_keep * t[name]
    for name in Q_NAMES:
        u[name] = s * t[name]
    for axis in "xyz":
        for name in T_OF[axis]:
            u[name] = t_keep * t[name]
    a_ = [None] * 19
    a_[0] = u["rho"]
    for axis, a in (("x", 1), ("y", 3), ("z", 5)):
        e = u["rho"] + u["P" + axis + axis]
        a_[a] = e + u["j" + axis]
        a_[a + 1] = e - u["j" + axis]
    for name, a, t1, t2 in (("xy", 7, "Txyy", "Txxy"), ("xz", 11, "Txzz", "Txxz"), ("yz", 15, "Tyzz", "Tyyz")):
        e = u["rho"] + u["P" + name[0] * 2] + u["P" + name[1] * 2] + u["Q" + name]
        ea, eb = e + u["P" + name], e - u["P" + name]
        o1, o2 = u["j" + name[0]] + u[t1], u["j" + name[1]] + u[t2]
        oa, ob = o1 + o2, o1 - o2
        a_[a] = ea + oa
        a_[a + 1] = ea - oa
        a_[a + 2] = eb + ob
        a_[a + 3] = eb - ob
    return a_, gs


def misfit(c, arrived):
    q = []
    for i in range(19):
        v = arrived[OPP[i]]
        q.append(jnp.where(v > 0.5, (c[i] - (v - 2.0)) * INV_W[i], 0.0))
    return q


def iota(shape, dim):
    return lax.broadcasted_iota(jnp.int32, shape, dim)


def columns(slots, shape):
    row = iota(shape, 0)
    col = jnp.full(shape, -1, jnp.int32)
    for k in range(SLOTS):
        col = jnp.where(row == k, slots[k], col)
    return col


def fields_of(f_ref, t_ref, s_ref, w_ref, valid, lanes):
    f = [f_ref[i, :, lanes] for i in range(19)]
    s = jnp.where(w_ref[:, lanes] == 1, 1.0, s_ref[:, lanes])
    m = moments(f)
    c = collide(m, defects(m), s)
    out = [jnp.where(valid, c[i], 0.0) for i in range(19)]
    for i in range(19):
        t = t_ref[OPP[i], :, lanes].astype(jnp.float32)
        out.append(jnp.where(valid, t + 2.0, 0.0))
    return out, jnp.where(valid, s + 1.0, 0.0)


def border_kernel(slots, fl, tl, sl, wl, fh, th, sh, wh, up, dn):
    valid = columns(slots, (SLOTS, 128)) >= 0
    for planes, out, (f, t, s, w), base, vz in (
        (ZUP, up, (fh, th, sh, wh), DZ - 2, DZ - 1),
        (ZDN, dn, (fl, tl, sl, wl), 0, 0),
    ):
        for z in (base, base + 1):
            for half in range(2):
                lanes = pl.ds((z - base) * 256 + half * 128, 128)
                dst = pl.ds(half * 128, 128)
                fields, v = fields_of(f, t, s, w, valid, lanes)
                for p, (n, src, _) in enumerate(planes):
                    if src == z:
                        out[pl.ds(p * SLOTS, SLOTS), dst] = fields[n]
                if z == vz:
                    out[pl.ds(NP * SLOTS, SLOTS), dst] = v
        out[pl.ds((NP + 1) * SLOTS, ZROWS - (NP + 1) * SLOTS), :] = jnp.zeros((ZROWS - (NP + 1) * SLOTS, 256), jnp.float32)


def fields_kernel(slots, f, t, s, w, store, vstore):
    valid = columns(slots, (SLOTS, 128)) >= 0

    def body(z, carry):
        for half in range(2):
            lanes = pl.ds(pl.multiple_of(z * 256 + half * 128, 128), 128)
            fields, v = fields_of(f, t, s, w, valid, lanes)
            base = pl.multiple_of((z + 1) * 16 + half * 8, 8)
            for n in range(NF):
                store[n, pl.ds(base + vel(n)[2] * 16, SLOTS), :] = fields[n]
            vstore[pl.ds(base, SLOTS), :] = v
        return carry

    lax.fori_loop(0, DZ, body, 0)


def side_kernel(slots, store_in, vstore_in, rup, rdn, store, vstore, rt, lt):
    del store_in, vstore_in
    lane = iota((8, 128), 1)
    group = lane // EDGE
    for planes, r, zi_v in ((ZUP, rup, 0), (ZDN, rdn, ZI - 1)):
        for half in range(2):
            src = pl.ds(half * 128, 128)
            for p, (n, _, zd) in enumerate(planes):
                store[n, pl.ds((zd + 1) * 16 + half * 8, SLOTS), :] = r[pl.ds(p * SLOTS, SLOTS), src]
            vstore[pl.ds(zi_v * 16 + half * 8, SLOTS), :] = r[pl.ds(NP * SLOTS, SLOTS), src]
    masks = [group == slots[k] for k in range(SLOTS)]
    for planes, out in ((XRT, rt), (XLT, lt)):
        vx = EDGE - 1 if out is rt else 0
        for p, (n, x, _) in enumerate(planes + [(None, vx, None)]):
            half, xl = x // 8, x % 8
            for part in range(2):
                acc = jnp.zeros((8, 128), jnp.float32)
                for k in range(SLOTS):
                    rows = pl.ds(part * 128 + half * 8 + k, 8, stride=16)
                    v = vstore[rows, :] if n is None else store[n, rows, :]
                    shift = lax.rem((slots[k] - xl + 16) * EDGE, 128)
                    acc = jnp.where(masks[k], pltpu.roll(v, shift, 1), acc)
                if part == 0:
                    out[pl.ds(p * ZI, 8), :] = acc
                else:
                    out[pl.ds(p * ZI + 8, 2), :] = acc[0:2]


def final_kernel(slots, f_ref, s_ref, w_ref, store, vstore, rt, lt, from_l, from_r, grad, out,
                 moved, gx, ghost_a, adj):
    lane = iota((8, 128), 1)
    y = lax.rem(lane, EDGE)
    row = iota((8, 128), 0)
    col = columns(slots, (8, 128))
    prev = pltpu.roll(col, 1, 0)
    nxt = pltpu.roll(col, 7, 0)
    edge = {1: y == 0, -1: y == EDGE - 1}
    conn = {
        1: edge[1] & (row >= 1) & (col >= 0) & (prev == col - 1),
        -1: edge[-1] & (row < SLOTS - 1) & (nxt >= 0) & (nxt == col + 1),
    }
    low, high = lane < EDGE, lane >= 128 - EDGE

    def yshift(t, cy):
        if cy == 0:
            return t
        a = pltpu.roll(t, cy % 128, 1)
        b = pltpu.roll(pltpu.roll(t, (-15 * cy) % 128, 1), cy % 8, 0)
        return jnp.where(conn[cy], b, jnp.where(edge[cy], 0.0, a))

    def xyshift(t0, t1, v, ghost):
        t0, t1 = yshift(t0, v[1]), yshift(t1, v[1])
        if v[0] == 1:
            r0, r1 = pltpu.roll(t0, EDGE, 1), pltpu.roll(t1, EDGE, 1)
            return jnp.where(low, ghost, r0), jnp.where(low, r0, r1)
        if v[0] == -1:
            r0, r1 = pltpu.roll(t0, 128 - EDGE, 1), pltpu.roll(t1, 128 - EDGE, 1)
            return jnp.where(high, r1, r0), jnp.where(high, ghost, r1)
        return t0, t1

    lane16 = iota((16, 128), 1)
    first, last = lane16 == 0, lane16 == 127

    def yshift_dense(t, cy):
        if cy == 0:
            return t
        a = pltpu.roll(t, cy % 128, 1)
        return jnp.where(first if cy == 1 else last, 0.0, a)

    def to_packed(t, dst, n, xl):
        for k in range(SLOTS):
            shift = lax.rem((xl - slots[k] + 16) * EDGE, 128)
            r = pltpu.roll(t, shift, 1)
            dst[n, pl.ds(k, 8, stride=8), :] = r[0:8]
            dst[n, pl.ds(64 + k, 8, stride=8), :] = r[8:16]

    for side, (planes, recv, own_planes, own, c_in, xl) in enumerate(
        ((XRT, from_l, XLT, lt, 1, 0), (XLT, from_r, XRT, rt, -1, 7))
    ):
        ghost = [None] * NF
        for p, (n, _, kind) in enumerate(planes):
            t = recv[pl.ds(p * ZI, 16), :]
            if kind == "ghost":
                ghost[n] = t
            else:
                to_packed(yshift_dense(t, vel(n)[1]), gx, n, xl)
        for p, (n, _, kind) in enumerate(own_planes):
            if kind == "edge":
                ghost[n] = own[pl.ds(p * ZI, 16), :]
        v = recv[pl.ds(NP * ZI, 16), :]
        ghost = [yshift_dense(ghost[n], vel(n)[1]) for n in range(NF)]
        m = moments(ghost[:19])
        d = defects(m)
        s = v - 1.0
        a, _ = adjoint(m, d, s, misfit(collide(m, d, s), ghost[19:]))
        for n in range(19):
            if VEL[n][0] == c_in:
                t = jnp.where(v > 0.5, a[OPP[n]], 0.0)
                to_packed(yshift_dense(t, VEL[n][1]), ghost_a, n, xl)

    def shift_fields(zi, carry):
        r0, r1 = pl.multiple_of(zi * 16, 8), pl.multiple_of(zi * 16 + 8, 8)
        for n in range(NF):
            t0 = store[n, pl.ds(r0, 8), :]
            t1 = store[n, pl.ds(r1, 8), :]
            g = gx[n, pl.ds(pl.multiple_of(zi * 8, 8), 8), :] if vel(n)[0] else None
            t0, t1 = xyshift(t0, t1, vel(n), g)
            moved[n, 0] = t0
            moved[n, 1] = t1
        for half in range(2):
            r = r1 if half else r0
            v = vstore[pl.ds(r, 8), :]
            s = v - 1.0
            m = moments([moved[i, half] for i in range(19)])
            d = defects(m)
            a, gs = adjoint(m, d, s, misfit(collide(m, d, s), [moved[19 + i, half] for i in range(19)]))
            listed = (v > 0.5) & (col >= 0)
            for n in range(19):
                adj[n, pl.ds(r, 8), :] = jnp.where(listed, a[OPP[n]], 0.0)
            adj[19, pl.ds(r, 8), :] = gs
        return carry

    lax.fori_loop(0, ZI, shift_fields, 0)

    valid = columns(slots, (SLOTS, 128)) >= 0

    def retreat(z, carry):
        zi = z + 1
        for n in range(19):
            src = zi - VEL[n][2]
            t0 = adj[n, pl.ds(pl.multiple_of(src * 16, 8), 8), :]
            t1 = adj[n, pl.ds(pl.multiple_of(src * 16 + 8, 8), 8), :]
            g = ghost_a[n, pl.ds(pl.multiple_of(src * 8, 8), 8), :] if VEL[n][0] else None
            t0, t1 = xyshift(t0, t1, VEL[n], g)
            moved[n, 0] = t0
            moved[n, 1] = t1
        for half in range(2):
            lanes = pl.ds(pl.multiple_of(z * 256 + half * 128, 128), 128)
            f = [f_ref[i, :, lanes] for i in range(19)]
            wall = w_ref[:, lanes] == 1
            s = jnp.where(wall, 1.0, s_ref[:, lanes])
            m = moments(f)
            q = [moved[OPP[i], half][0:SLOTS] for i in range(19)]
            a, gs = adjoint(m, defects(m), s, q)
            for i in range(19):
                out[i, :, lanes] = jnp.where(valid, a[i], 0.0)
            g2 = adj[19, pl.ds(pl.multiple_of(zi * 16 + half * 8, 8), 8), :][0:SLOTS]
            grad[:, lanes] = jnp.where(valid & jnp.logical_not(wall), gs + g2, 0.0)
        return carry

    lax.fori_loop(0, DZ, retreat, 0)


SMEM = pl.BlockSpec(memory_space=pltpu.SMEM)
VMEM = pl.BlockSpec(memory_space=pltpu.VMEM)


def pairs(count):
    inside = [(i, i ^ 1) for i in range(count)]
    across = []
    for i in range(1, count - 1, 2):
        across += [(i, i + 1), (i + 1, i)]
    return inside, across


def exchange(forward, backward, axis):
    count = lax.axis_size(axis)
    even = lax.axis_index(axis) % 2 == 0
    inside, across = pairs(count)
    del even, inside, across
    up = [(i, i + 1) for i in range(count - 1)]
    low = lax.ppermute(forward, axis, up)
    high = lax.ppermute(backward, axis, [(b, a) for a, b in up])
    return low, high


def per_device(populations, target, solid_frac, wall_mask, slot_column):
    f32 = jnp.float32
    params = pltpu.CompilerParams(vmem_limit_bytes=48 << 20)
    lo3 = pl.BlockSpec((19, SLOTS, 512), lambda i: (0, 0, 0))
    hi3 = pl.BlockSpec((19, SLOTS, 512), lambda i: (0, 0, 3))
    lo2 = pl.BlockSpec((SLOTS, 512), lambda i: (0, 0))
    hi2 = pl.BlockSpec((SLOTS, 512), lambda i: (0, 3))
    zbuf = jax.ShapeDtypeStruct((ZROWS, 256), f32)
    up, dn = pl.pallas_call(
        border_kernel,
        grid=(1,),
        in_specs=[SMEM, lo3, lo3, lo2, lo2, hi3, hi3, hi2, hi2],
        out_specs=[pl.BlockSpec((ZROWS, 256), lambda i: (0, 0))] * 2,
        out_shape=[zbuf, zbuf],
        compiler_params=params,
    )(slot_column, populations, target, solid_frac, wall_mask, populations, target, solid_frac, wall_mask)
    rup, rdn = exchange(up, dn, "gz")
    store_t = jax.ShapeDtypeStruct((NF, ROWS_STORE, 128), f32)
    vstore_t = jax.ShapeDtypeStruct((ROWS_STORE, 128), f32)
    store, vstore = pl.pallas_call(
        fields_kernel,
        in_specs=[SMEM, VMEM, VMEM, VMEM, VMEM],
        out_specs=[VMEM, VMEM],
        out_shape=[store_t, vstore_t],
        compiler_params=params,
    )(slot_column, populations, target, solid_frac, wall_mask)
    xbuf = jax.ShapeDtypeStruct((XROWS, 128), f32)
    store, vstore, rt, lt = pl.pallas_call(
        side_kernel,
        in_specs=[SMEM, VMEM, VMEM, VMEM, VMEM],
        out_specs=[VMEM] * 4,
        out_shape=[store_t, vstore_t, xbuf, xbuf],
        input_output_aliases={1: 0, 2: 1},
        compiler_params=params,
    )(slot_column, store, vstore, rup, rdn)
    from_l, from_r = exchange(rt, lt, "blk")
    grad, adjoint_out = pl.pallas_call(
        final_kernel,
        in_specs=[SMEM] + [VMEM] * 9,
        out_specs=[VMEM, VMEM],
        out_shape=[
            jax.ShapeDtypeStruct((SLOTS, CELLS), f32),
            jax.ShapeDtypeStruct((19, SLOTS, CELLS), f32),
        ],
        scratch_shapes=[
            pltpu.VMEM((NF, 2, 8, 128), f32),
            pltpu.VMEM((NF, 128, 128), f32),
            pltpu.VMEM((19, 128, 128), f32),
            pltpu.VMEM((20, ZI * 16, 128), f32),
        ],
        compiler_params=params,
    )(slot_column, populations, solid_frac, wall_mask, store, vstore, rt, lt, from_l, from_r)
    return grad, adjoint_out


def solution(mesh):
    return jax.shard_map(
        per_device,
        mesh=mesh,
        in_specs=(
            P(None, "blk", "gz"),
            P(None, "blk", "gz"),
            P("blk", "gz"),
            P("blk", "gz"),
            P("blk"),
        ),
        out_specs=(P("blk", "gz"), P(None, "blk", "gz")),
        check_vma=False,
    )
```

```python
import jax
import jax.numpy as jnp
from jax import lax
from jax.experimental import pallas as pl
from jax.experimental.pallas import tpu as pltpu
from jax.sharding import PartitionSpec as P

EDGE = 16
GY = 8
SLOTS = 5
DZ = 8
CELLS = DZ * EDGE * EDGE

VEL = (
    (0, 0, 0),
    (1, 0, 0), (-1, 0, 0), (0, 1, 0), (0, -1, 0), (0, 0, 1), (0, 0, -1),
    (1, 1, 0), (-1, -1, 0), (1, -1, 0), (-1, 1, 0),
    (1, 0, 1), (-1, 0, -1), (1, 0, -1), (-1, 0, 1),
    (0, 1, 1), (0, -1, -1), (0, 1, -1), (0, -1, 1),
)
OPP = (0, 2, 1, 4, 3, 6, 5, 8, 7, 10, 9, 12, 11, 14, 13, 16, 15, 18, 17)
INV_W = (3.0,) + (18.0,) * 6 + (36.0,) * 12

NF = 38
ZI = 10
ROWS_STORE = ZI * 16


def vel(n):
    return VEL[n % 19]


def mirror(n, dim):
    v = list(vel(n))
    v[dim] = -v[dim]
    return n // 19 * 19 + VEL.index(tuple(v))


def planes(dim):
    out = []
    for n in range(NF):
        c = vel(n)[dim]
        if c == 0:
            out.append((n, True, True))
        elif c == 1:
            out.append((n, False, True))
            out.append((n, True, False))
    return out


ZP, XP = planes(2), planes(0)
NP = len(ZP)
ZROWS = 200
XROWS = 400
SLOT_ROWS = 24


def moments(f):
    m = {}

    def pair(a):
        return f[a] + f[a + 1], f[a] - f[a + 1]

    sx, dx = pair(1)
    sy, dy = pair(3)
    sz, dz = pair(5)
    for name, a, t1, t2 in (("xy", 7, "xyy", "xxy"), ("xz", 11, "xzz", "xxz"), ("yz", 15, "yzz", "yyz")):
        sa, da = pair(a)
        sb, db = pair(a + 2)
        m["Q" + name] = sa + sb
        m["P" + name] = sa - sb
        m["T" + t1] = da + db
        m["T" + t2] = da - db
    qa = m["Qxy"] + m["Qxz"]
    m["Pxx"] = sx + qa
    m["Pyy"] = sy + (m["Qxy"] + m["Qyz"])
    m["Pzz"] = sz + (m["Qxz"] + m["Qyz"])
    m["rho"] = (f[0] + sx) + (sy + sz) + (qa + m["Qyz"])
    m["jx"] = dx + (m["Txyy"] + m["Txzz"])
    m["jy"] = dy + (m["Txxy"] + m["Tyzz"])
    m["jz"] = dz + (m["Txxz"] + m["Tyyz"])
    return m


def defects(m):
    ux, uy, uz = m["jx"], m["jy"], m["jz"]
    xx, yy, zz = ux * ux, uy * uy, uz * uz
    third = m["rho"] * (1.0 / 3.0)
    ninth = m["rho"] * (1.0 / 9.0) - (xx + yy + zz) * (1.0 / 6.0)
    d = {}
    d["Pxx"] = third + xx - m["Pxx"]
    d["Pyy"] = third + yy - m["Pyy"]
    d["Pzz"] = third + zz - m["Pzz"]
    d["Pxy"] = ux * uy - m["Pxy"]
    d["Pxz"] = ux * uz - m["Pxz"]
    d["Pyz"] = uy * uz - m["Pyz"]
    d["Qxy"] = ninth + (xx + yy) * 0.5 - m["Qxy"]
    d["Qxz"] = ninth + (xx + zz) * 0.5 - m["Qxz"]
    d["Qyz"] = ninth + (yy + zz) * 0.5 - m["Qyz"]
    return d


P_NAMES = ("Pxx", "Pyy", "Pzz", "Pxy", "Pxz", "Pyz")
Q_NAMES = ("Qxy", "Qxz", "Qyz")
M_NAMES = ("rho", "jx", "jy", "jz") + P_NAMES + Q_NAMES + ("Txyy", "Txzz", "Txxy", "Tyzz", "Txxz", "Tyyz")
T_OF = {"x": ("Txyy", "Txzz"), "y": ("Txxy", "Tyzz"), "z": ("Txxz", "Tyyz")}


def collide(m, d, s):
    h = 1.0 - s
    h16 = 1.6 * h
    t_keep = 0.8 * h - 1.0
    h04 = 0.4 * h
    j_keep = h - s
    o = {}
    for name in P_NAMES:
        o[name] = m[name] + h16 * d[name]
    for name in Q_NAMES:
        o[name] = m[name] + h * d[name]
    for axis in "xyz":
        j = m["j" + axis]
        o["j" + axis] = j_keep * j
        hj = h04 * j
        for name in T_OF[axis]:
            o[name] = t_keep * m[name] + hj
    f = [None] * 19
    qs = (o["Qxy"] + o["Qxz"]) + o["Qyz"]
    f[0] = (m["rho"] + qs) - ((o["Pxx"] + o["Pyy"]) + o["Pzz"])
    for a, p, q1, q2, axis in ((1, "Pxx", "Qxy", "Qxz", "x"), (3, "Pyy", "Qxy", "Qyz", "y"), (5, "Pzz", "Qxz", "Qyz", "z")):
        s_ = (o[p] - (o[q1] + o[q2])) * 0.5
        d_ = (o["j" + axis] - (o[T_OF[axis][0]] + o[T_OF[axis][1]])) * 0.5
        f[a] = s_ + d_
        f[a + 1] = s_ - d_
    for name, a, t1, t2 in (("xy", 7, "Txyy", "Txxy"), ("xz", 11, "Txzz", "Txxz"), ("yz", 15, "Tyzz", "Tyyz")):
        q = o["Q" + name] * 0.25
        p = o["P" + name] * 0.25
        u = o[t1] * 0.25
        w = o[t2] * 0.25
        sa, sb, da, db = q + p, q - p, u + w, u - w
        f[a] = sa + da
        f[a + 1] = sa - da
        f[a + 2] = sb + db
        f[a + 3] = sb - db
    return f


def adjoint(m, d, s, q):
    h = 1.0 - s
    h16 = 1.6 * h
    t_keep = 0.8 * h - 1.0
    h04 = 0.4 * h
    j_keep = h - s
    t = {}
    half = {}
    for axis, a in (("x", 1), ("y", 3), ("z", 5)):
        half[axis] = (q[a] + q[a + 1]) * 0.5
        t["j" + axis] = (q[a] - q[a + 1]) * 0.5
        t["P" + axis + axis] = half[axis] - q[0]
    for name, a, t1, t2 in (("xy", 7, "Txyy", "Txxy"), ("xz", 11, "Txzz", "Txxz"), ("yz", 15, "Tyzz", "Tyyz")):
        sa, da = q[a] + q[a + 1], q[a] - q[a + 1]
        sb, db = q[a + 2] + q[a + 3], q[a + 2] - q[a + 3]
        t["Q" + name] = (sa + sb) * 0.25 - half[name[0]] - t["P" + name[1] * 2]
        t["P" + name] = (sa - sb) * 0.25
        t[t1] = (da + db) * 0.25 - t["j" + name[0]]
        t[t2] = (da - db) * 0.25 - t["j" + name[1]]
    gp = t["Pxx"] * d["Pxx"]
    for name in P_NAMES[1:]:
        gp = gp + t[name] * d[name]
    gq = t["Qxy"] * d["Qxy"] + t["Qxz"] * d["Qxz"] + t["Qyz"] * d["Qyz"]
    gt = None
    gj = None
    tsum = {}
    for axis in "xyz":
        tsum[axis] = t[T_OF[axis][0]] + t[T_OF[axis][1]]
        term = t[T_OF[axis][0]] * m[T_OF[axis][0]] + t[T_OF[axis][1]] * m[T_OF[axis][1]]
        gt = term if gt is None else gt + term
        term = (2.0 * t["j" + axis] + 0.4 * tsum[axis]) * m["j" + axis]
        gj = term if gj is None else gj + term
    gs = -(1.6 * gp + gq + gj + 0.8 * gt)
    ux, uy, uz = m["jx"], m["jy"], m["jz"]
    p_keep = 1.0 - h16
    qsum = t["Qxy"] + t["Qxz"] + t["Qyz"]
    u = {}
    u["rho"] = q[0] + (h16 * (1.0 / 3.0)) * (t["Pxx"] + t["Pyy"] + t["Pzz"]) + (h * (1.0 / 9.0)) * qsum
    third = qsum * (1.0 / 3.0)
    w16 = {"x": t["Pxy"] * uy + t["Pxz"] * uz, "y": t["Pxy"] * ux + t["Pyz"] * uz, "z": t["Pxz"] * ux + t["Pyz"] * uy}
    other = {"x": "Qyz", "y": "Qxz", "z": "Qxy"}
    for axis, uu in (("x", ux), ("y", uy), ("z", uz)):
        quad = 2.0 * third - t[other[axis]]
        u["j" + axis] = (
            j_keep * t["j" + axis]
            + h04 * tsum[axis]
            + h16 * (w16[axis] + 2.0 * t["P" + axis + axis] * uu)
            + h * (quad * uu)
        )
    for name in P_NAMES:
        u[name] = p_keep * t[name]
    for name in Q_NAMES:
        u[name] = s * t[name]
    for axis in "xyz":
        for name in T_OF[axis]:
            u[name] = t_keep * t[name]
    a_ = [None] * 19
    a_[0] = u["rho"]
    for axis, a in (("x", 1), ("y", 3), ("z", 5)):
        e = u["rho"] + u["P" + axis + axis]
        a_[a] = e + u["j" + axis]
        a_[a + 1] = e - u["j" + axis]
    for name, a, t1, t2 in (("xy", 7, "Txyy", "Txxy"), ("xz", 11, "Txzz", "Txxz"), ("yz", 15, "Tyzz", "Tyyz")):
        e = u["rho"] + u["P" + name[0] * 2] + u["P" + name[1] * 2] + u["Q" + name]
        ea, eb = e + u["P" + name], e - u["P" + name]
        o1, o2 = u["j" + name[0]] + u[t1], u["j" + name[1]] + u[t2]
        oa, ob = o1 + o2, o1 - o2
        a_[a] = ea + oa
        a_[a + 1] = ea - oa
        a_[a + 2] = eb + ob
        a_[a + 3] = eb - ob
    return a_, gs


def misfit(c, arrived):
    q = []
    for i in range(19):
        v = arrived[OPP[i]]
        q.append(jnp.where(v > 0.5, (c[i] - (v - 2.0)) * INV_W[i], 0.0))
    return q


def iota(shape, dim):
    return lax.broadcasted_iota(jnp.int32, shape, dim)


def columns(slots, shape):
    row = iota(shape, 0)
    col = jnp.full(shape, -1, jnp.int32)
    for k in range(SLOTS):
        col = jnp.where(row == k, slots[k], col)
    return col


def load_all(copies):
    for c in copies:
        c.start()
    for c in copies:
        c.wait()


def unpack(f_raw, t_raw, s_raw, w_raw, f_rows, t_rows, frac, tiles):
    for t in range(tiles):
        lanes = pl.ds(t * 128, 128)
        for k in range(SLOTS):
            f_rows[t, pl.ds(k * SLOT_ROWS, 19), :] = f_raw[k, :, lanes]
            t_rows[t, pl.ds(k * SLOT_ROWS, 19), :] = t_raw[k, :, lanes].astype(jnp.float32)
        frac[pl.ds(0, SLOTS), lanes] = jnp.where(w_raw[:, lanes] == 1, 1.0, s_raw[:, lanes])


def fields_of(f_rows, t_rows, frac, valid, tile):
    f = [f_rows[tile, pl.ds(i, 8, stride=SLOT_ROWS), :] for i in range(19)]
    s = frac[:, pl.ds(pl.multiple_of(tile * 128, 128), 128)]
    m = moments(f)
    c = collide(m, defects(m), s)
    out = [jnp.where(valid, c[i], 0.0) for i in range(19)]
    for i in range(19):
        t = t_rows[tile, pl.ds(OPP[i], 8, stride=SLOT_ROWS), :]
        out.append(jnp.where(valid, t + 2.0, 0.0))
    return out, jnp.where(valid, s + 1.0, 0.0), m


def even(axis):
    return lax.rem(lax.axis_index(axis), 2) == 0


def border_kernel(slots_h, f_h, t_h, s_h, w_h, inside, across, slots, f_raw, t_raw, s_raw, w_raw, f_rows, t_rows, frac, sem):
    copies = [pltpu.make_async_copy(slots_h, slots, sem.at[0])]
    for e, lane in enumerate((0, CELLS - 512)):
        src, dst = pl.ds(lane, 512), pl.ds(e * 512, 512)
        copies += [
            pltpu.make_async_copy(f_h.at[:, :, src], f_raw.at[:, :, dst], sem.at[1 + e]),
            pltpu.make_async_copy(t_h.at[:, :, src], t_raw.at[:, :, dst], sem.at[3 + e]),
            pltpu.make_async_copy(s_h.at[:, src], s_raw.at[:, dst], sem.at[5 + e]),
            pltpu.make_async_copy(w_h.at[:, src], w_raw.at[:, dst], sem.at[7 + e]),
        ]
    load_all(copies)
    unpack(f_raw, t_raw, s_raw, w_raw, f_rows, t_rows, frac, 8)
    valid = columns(slots, (8, 128)) >= 0
    even_z = even("gz")
    for out, goes_up in ((inside, even_z), (across, jnp.logical_not(even_z))):
        for outer in (True, False):
            layer = jnp.where(goes_up, 3, 0) if outer else jnp.where(goes_up, 2, 1)
            for half in range(2):
                dst = pl.ds(half * 128, 128)
                fields, v, _ = fields_of(f_rows, t_rows, frac, valid, layer * 2 + half)
                for p, (n, src, _) in enumerate(ZP):
                    if src == outer:
                        m = mirror(n, 2)
                        val = fields[n] if m == n else jnp.where(goes_up, fields[n], fields[m])
                        out[pl.ds(p * SLOTS, SLOTS), dst] = val[0:SLOTS]
                if outer:
                    out[pl.ds(NP * SLOTS, SLOTS), dst] = v[0:SLOTS]


def fields_kernel(slots_h, f_h, t_h, s_h, w_h, store, vstore, mstore, slots, f_raw, t_raw, s_raw, w_raw, f_rows, t_rows, frac, sem):
    load_all([
        pltpu.make_async_copy(slots_h, slots, sem.at[0]),
        pltpu.make_async_copy(f_h, f_raw, sem.at[1]),
        pltpu.make_async_copy(t_h, t_raw, sem.at[2]),
        pltpu.make_async_copy(s_h, s_raw, sem.at[3]),
        pltpu.make_async_copy(w_h, w_raw, sem.at[4]),
    ])
    unpack(f_raw, t_raw, s_raw, w_raw, f_rows, t_rows, frac, 16)
    valid = columns(slots, (8, 128)) >= 0

    def body(z, carry):
        for half in range(2):
            fields, v, m = fields_of(f_rows, t_rows, frac, valid, z * 2 + half)
            base = pl.multiple_of((z + 1) * 16 + half * 8, 8)
            for n in range(NF):
                store[n, pl.ds(base + vel(n)[2] * 16, 8), :] = fields[n]
            vstore[pl.ds(base, 8), :] = v
            for i, name in enumerate(M_NAMES):
                mstore[i, pl.ds(pl.multiple_of(z * 16 + half * 8, 8), 8), :] = m[name]
        return carry

    lax.fori_loop(0, DZ, body, 0)


def side_kernel(slots_h, store_in, vstore_in, r_inside, r_across, store, vstore, inside, across, slots, sem):
    del store_in, vstore_in
    load_all([pltpu.make_async_copy(slots_h, slots, sem.at[0])])
    group = iota((8, 128), 1) // EDGE
    even_z = even("gz")
    for r, below in ((r_inside, jnp.logical_not(even_z)), (r_across, even_z)):
        ghost, first = jnp.where(below, 0, ZI - 1), jnp.where(below, 1, ZI - 2)
        for half in range(2):
            src = pl.ds(half * 128, 128)
            for p, (n, _, is_ghost) in enumerate(ZP):
                m = mirror(n, 2)
                field = n if m == n else jnp.where(below, n, m)
                zi = ghost if is_ghost else first
                store[field, pl.ds(zi * 16 + half * 8, SLOTS), :] = r[pl.ds(p * SLOTS, SLOTS), src]
            vstore[pl.ds(ghost * 16 + half * 8, SLOTS), :] = r[pl.ds(NP * SLOTS, SLOTS), src]
    masks = [group == slots[k] for k in range(SLOTS)]
    even_x = even("blk")
    for out, right in ((inside, even_x), (across, jnp.logical_not(even_x))):
        half = jnp.where(right, 1, 0)
        for p, (n, outer, _) in enumerate(XP + [(None, True, None)]):
            if outer:
                xl = jnp.where(right, 7, 0)
            else:
                xl = jnp.where(right, 6, 1)
            if n is not None:
                m = mirror(n, 0)
                field = n if m == n else jnp.where(right, n, m)
            for part, count in ((0, 8), (1, 2)):
                acc = jnp.zeros((count, 128), jnp.float32)
                for k in range(SLOTS):
                    rows = pl.ds(part * 128 + half * 8 + k, count, stride=16)
                    v = vstore[rows, :] if n is None else store[field, rows, :]
                    shift = lax.rem((slots[k] - xl + 16) * EDGE, 128)
                    acc = jnp.where(masks[k][0:count], pltpu.roll(v, shift, 1), acc)
                out[pl.ds(p * ZI + part * 8, count), :] = acc


def shifter(slots):
    lane = iota((8, 128), 1)
    y = lax.rem(lane, EDGE)
    row = iota((8, 128), 0)
    col = columns(slots, (8, 128))
    prev = pltpu.roll(col, 1, 0)
    nxt = pltpu.roll(col, 7, 0)
    edge = {1: y == 0, -1: y == EDGE - 1}
    conn = {
        1: edge[1] & (row >= 1) & (col >= 0) & (prev == col - 1),
        -1: edge[-1] & (row < SLOTS - 1) & (nxt >= 0) & (nxt == col + 1),
    }
    low, high = lane < EDGE, lane >= 128 - EDGE

    def yshift(t, cy):
        if cy == 0:
            return t
        a = pltpu.roll(t, cy % 128, 1)
        b = pltpu.roll(pltpu.roll(t, (-15 * cy) % 128, 1), cy % 8, 0)
        return jnp.where(conn[cy], b, jnp.where(edge[cy], 0.0, a))

    def xyshift(t0, t1, v, ghost):
        t0, t1 = yshift(t0, v[1]), yshift(t1, v[1])
        if v[0] == 1:
            r0, r1 = pltpu.roll(t0, EDGE, 1), pltpu.roll(t1, EDGE, 1)
            return jnp.where(low, ghost, r0), jnp.where(low, r0, r1)
        if v[0] == -1:
            r0, r1 = pltpu.roll(t0, 128 - EDGE, 1), pltpu.roll(t1, 128 - EDGE, 1)
            return jnp.where(high, r1, r0), jnp.where(high, ghost, r1)
        return t0, t1

    return xyshift, low, high, col


def shift_kernel(slots_h, store, moved, slots, sem):
    load_all([pltpu.make_async_copy(slots_h, slots, sem.at[0])])
    xyshift, _, _, _ = shifter(slots)

    def body(zi, carry):
        r0, r1 = pl.multiple_of(zi * 16, 8), pl.multiple_of(zi * 16 + 8, 8)
        for n in range(NF):
            t0, t1 = xyshift(store[n, pl.ds(r0, 8), :], store[n, pl.ds(r1, 8), :], vel(n), 0.0)
            moved[n, pl.ds(r0, 8), :] = t0
            moved[n, pl.ds(r1, 8), :] = t1
        return carry

    lax.fori_loop(0, ZI, body, 0)


def final_kernel(slots_h, moved, vstore, mstore, inside, across, r_inside, r_across, grad, out,
                 slots, gx, ghost_a, adj, back, out_rows, sem):
    load_all([pltpu.make_async_copy(slots_h, slots, sem.at[0])])
    xyshift, low, high, col = shifter(slots)
    lane16 = iota((16, 128), 1)
    first, last = lane16 == 0, lane16 == 127

    def yshift_dense(t, cy):
        if cy == 0:
            return t
        a = pltpu.roll(t, cy % 128, 1)
        return jnp.where(first if cy == 1 else last, 0.0, a)

    def to_packed(t, dst, n, xl):
        for k in range(SLOTS):
            shift = lax.rem((xl - slots[k] + 16) * EDGE, 128)
            r = pltpu.roll(t, shift, 1)
            dst[n, pl.ds(k, 8, stride=8), :] = r[0:8]
            dst[n, pl.ds(64 + k, 8, stride=8), :] = r[8:16]

    even_x = even("blk")
    for c_in, xl in ((1, 0), (-1, 7)):
        from_inside = jnp.logical_not(even_x) if c_in == 1 else even_x
        ghost = [None] * NF
        for p, (n, _, is_ghost) in enumerate(XP + [(None, None, True)]):
            rows = pl.ds(p * ZI, 16)
            t = jnp.where(from_inside, r_inside[rows, :], r_across[rows, :])
            if n is None:
                v = t
                continue
            m = n if c_in == 1 else mirror(n, 0)
            if is_ghost:
                ghost[m] = t
            else:
                to_packed(yshift_dense(t, vel(m)[1]), gx, m, xl)
                own = jnp.where(from_inside, inside[rows, :], across[rows, :])
                ghost[mirror(m, 0)] = own
        ghost = [yshift_dense(ghost[n], vel(n)[1]) for n in range(NF)]
        m = moments(ghost[:19])
        d = defects(m)
        s = v - 1.0
        a, _ = adjoint(m, d, s, misfit(collide(m, d, s), ghost[19:]))
        for n in range(19):
            if VEL[n][0] == c_in:
                t = jnp.where(v > 0.5, a[OPP[n]], 0.0)
                to_packed(yshift_dense(t, VEL[n][1]), ghost_a, n, xl)

    def advance(zi, carry):
        for half in range(2):
            r = pl.multiple_of(zi * 16 + half * 8, 8)
            f = []
            for n in range(NF):
                t = moved[n, pl.ds(r, 8), :]
                if vel(n)[0] == 1 - 2 * half:
                    g = gx[n, pl.ds(pl.multiple_of(zi * 8, 8), 8), :]
                    t = jnp.where(high if half else low, g, t)
                f.append(t)
            v = vstore[pl.ds(r, 8), :]
            s = v - 1.0
            m = moments(f[:19])
            d = defects(m)
            a, gs = adjoint(m, d, s, misfit(collide(m, d, s), f[19:]))
            listed = (v > 0.5) & (col >= 0)
            for n in range(19):
                adj[n, pl.ds(r, 8), :] = jnp.where(listed, a[OPP[n]], 0.0)
            adj[19, pl.ds(r, 8), :] = gs
        return carry

    lax.fori_loop(0, ZI, advance, 0)

    def retreat(z, carry):
        zi = z + 1
        for n in range(19):
            src = zi - VEL[n][2]
            t0 = adj[n, pl.ds(pl.multiple_of(src * 16, 8), 8), :]
            t1 = adj[n, pl.ds(pl.multiple_of(src * 16 + 8, 8), 8), :]
            g = ghost_a[n, pl.ds(pl.multiple_of(src * 8, 8), 8), :] if VEL[n][0] else None
            t0, t1 = xyshift(t0, t1, VEL[n], g)
            back[n, 0] = t0
            back[n, 1] = t1
        for half in range(2):
            lanes = pl.ds(pl.multiple_of(z * 256 + half * 128, 128), 128)
            r = pl.ds(pl.multiple_of(z * 16 + half * 8, 8), 8)
            r1 = pl.ds(pl.multiple_of(zi * 16 + half * 8, 8), 8)
            m = {name: mstore[i, r, :] for i, name in enumerate(M_NAMES)}
            v = vstore[r1, :]
            listed = (v > 0.5) & (col >= 0)
            s = v - 1.0
            q = [back[OPP[i], half] for i in range(19)]
            a, gs = adjoint(m, defects(m), s, q)
            for i in range(19):
                out_rows[z * 2 + half, pl.ds(i, 8, stride=SLOT_ROWS), :] = jnp.where(listed, a[i], 0.0)
            g2 = jnp.where(listed & (v < 1.75), gs + adj[19, r1, :], 0.0)
            grad[:, lanes] = g2[0:SLOTS]
        return carry

    lax.fori_loop(0, DZ, retreat, 0)
    for k in range(SLOTS):
        for t in range(16):
            out[k, :, pl.ds(t * 128, 128)] = out_rows[t, pl.ds(k * SLOT_ROWS, 19), :]


HBM = pl.BlockSpec(memory_space=pltpu.HBM)
VMEM = pl.BlockSpec(memory_space=pltpu.VMEM)


def exchange(inside, across, axis):
    count = lax.axis_size(axis)
    first = [(i, i ^ 1) for i in range(count)]
    second = []
    for i in range(1, count - 1, 2):
        second += [(i, i + 1), (i + 1, i)]
    return lax.ppermute(inside, axis, first), lax.ppermute(across, axis, second)


def per_device(populations, target, solid_frac, wall_mask, slot_column):
    f32 = jnp.float32
    populations = jnp.transpose(populations, (1, 0, 2))
    target = jnp.transpose(target, (1, 0, 2))
    populations, target, solid_frac, wall_mask, slot_column = (
        pltpu.with_memory_space_constraint(x, pltpu.HBM) for x in (populations, target, solid_frac, wall_mask, slot_column)
    )

    def params(mib):
        return pltpu.CompilerParams(vmem_limit_bytes=mib << 20)

    def inputs(cells):
        return [
            pltpu.SMEM((SLOTS,), jnp.int32),
            pltpu.VMEM((SLOTS, 19, cells), f32),
            pltpu.VMEM((SLOTS, 19, cells), jnp.bfloat16),
            pltpu.VMEM((SLOTS, cells), f32),
            pltpu.VMEM((SLOTS, cells), jnp.int32),
            pltpu.VMEM((cells // 128, 8 * SLOT_ROWS, 128), f32),
            pltpu.VMEM((cells // 128, 8 * SLOT_ROWS, 128), f32),
            pltpu.VMEM((8, cells), f32),
            pltpu.SemaphoreType.DMA((9,)),
        ]

    slots_in = [pltpu.SMEM((SLOTS,), jnp.int32)]
    zbuf = jax.ShapeDtypeStruct((ZROWS, 256), f32)
    inside, across = pl.pallas_call(
        border_kernel,
        in_specs=[HBM] * 5,
        out_specs=[VMEM] * 2,
        out_shape=[zbuf, zbuf],
        scratch_shapes=inputs(1024),
        compiler_params=params(8),
    )(slot_column, populations, target, solid_frac, wall_mask)
    r_inside, r_across = exchange(inside, across, "gz")
    store_t = jax.ShapeDtypeStruct((NF, ROWS_STORE, 128), f32)
    vstore_t = jax.ShapeDtypeStruct((ROWS_STORE, 128), f32)
    store, vstore, mstore = pl.pallas_call(
        fields_kernel,
        in_specs=[HBM] * 5,
        out_specs=[VMEM] * 3,
        out_shape=[store_t, vstore_t, jax.ShapeDtypeStruct((19, DZ * 16, 128), f32)],
        scratch_shapes=inputs(CELLS),
        compiler_params=params(12),
    )(slot_column, populations, target, solid_frac, wall_mask)
    xbuf = jax.ShapeDtypeStruct((XROWS, 128), f32)
    store, vstore, inside, across = pl.pallas_call(
        side_kernel,
        in_specs=[HBM] + [VMEM] * 4,
        out_specs=[VMEM] * 4,
        out_shape=[store_t, vstore_t, xbuf, xbuf],
        input_output_aliases={1: 0, 2: 1},
        scratch_shapes=slots_in + [pltpu.SemaphoreType.DMA((1,))],
        compiler_params=params(12),
    )(slot_column, store, vstore, r_inside, r_across)
    r_inside, r_across = exchange(inside, across, "blk")
    moved = pl.pallas_call(
        shift_kernel,
        in_specs=[HBM, VMEM],
        out_specs=VMEM,
        out_shape=store_t,
        scratch_shapes=slots_in + [pltpu.SemaphoreType.DMA((1,))],
        compiler_params=params(12),
    )(slot_column, store)
    grad, adjoint_out = pl.pallas_call(
        final_kernel,
        in_specs=[HBM] + [VMEM] * 7,
        out_specs=[VMEM, VMEM],
        out_shape=[
            jax.ShapeDtypeStruct((SLOTS, CELLS), f32),
            jax.ShapeDtypeStruct((SLOTS, 19, CELLS), f32),
        ],
        scratch_shapes=slots_in + [
            pltpu.VMEM((NF, 128, 128), f32),
            pltpu.VMEM((19, 128, 128), f32),
            pltpu.VMEM((20, ZI * 16, 128), f32),
            pltpu.VMEM((19, 2, 8, 128), f32),
            pltpu.VMEM((CELLS // 128, 8 * SLOT_ROWS, 128), f32),
            pltpu.SemaphoreType.DMA((1,)),
        ],
        compiler_params=params(20),
    )(slot_column, moved, vstore, mstore, inside, across, r_inside, r_across)
    return grad, jnp.transpose(adjoint_out, (1, 0, 2))


def solution(mesh):
    return jax.shard_map(
        per_device,
        mesh=mesh,
        in_specs=(
            P(None, "blk", "gz"),
            P(None, "blk", "gz"),
            P("blk", "gz"),
            P("blk", "gz"),
            P("blk"),
        ),
        out_specs=(P("blk", "gz"), P(None, "blk", "gz")),
        check_vma=False,
    )
```

```python
import jax
import jax.numpy as jnp
from jax import lax
from jax.experimental import pallas as pl
from jax.experimental.pallas import tpu as pltpu
from jax.sharding import PartitionSpec as P

EDGE = 16
GY = 8
SLOTS = 5
DZ = 8
CELLS = DZ * EDGE * EDGE

VEL = (
    (0, 0, 0),
    (1, 0, 0), (-1, 0, 0), (0, 1, 0), (0, -1, 0), (0, 0, 1), (0, 0, -1),
    (1, 1, 0), (-1, -1, 0), (1, -1, 0), (-1, 1, 0),
    (1, 0, 1), (-1, 0, -1), (1, 0, -1), (-1, 0, 1),
    (0, 1, 1), (0, -1, -1), (0, 1, -1), (0, -1, 1),
)
OPP = (0, 2, 1, 4, 3, 6, 5, 8, 7, 10, 9, 12, 11, 14, 13, 16, 15, 18, 17)
INV_W = (3.0,) + (18.0,) * 6 + (36.0,) * 12

NF = 38
ZI = 10
ROWS_STORE = ZI * 16


def vel(n):
    return VEL[n % 19]


def mirror(n, dim):
    v = list(vel(n))
    v[dim] = -v[dim]
    return n // 19 * 19 + VEL.index(tuple(v))


def planes(dim):
    out = []
    for n in range(NF):
        c = vel(n)[dim]
        if c == 0:
            out.append((n, True, True))
        elif c == 1:
            out.append((n, False, True))
            out.append((n, True, False))
    return out


ZP, XP = planes(2), planes(0)
NP = len(ZP)
ZROWS = 200
XROWS = 400
SLOT_ROWS = 24


def moments(f):
    m = {}

    def pair(a):
        return f[a] + f[a + 1], f[a] - f[a + 1]

    sx, dx = pair(1)
    sy, dy = pair(3)
    sz, dz = pair(5)
    for name, a, t1, t2 in (("xy", 7, "xyy", "xxy"), ("xz", 11, "xzz", "xxz"), ("yz", 15, "yzz", "yyz")):
        sa, da = pair(a)
        sb, db = pair(a + 2)
        m["Q" + name] = sa + sb
        m["P" + name] = sa - sb
        m["T" + t1] = da + db
        m["T" + t2] = da - db
    qa = m["Qxy"] + m["Qxz"]
    m["Pxx"] = sx + qa
    m["Pyy"] = sy + (m["Qxy"] + m["Qyz"])
    m["Pzz"] = sz + (m["Qxz"] + m["Qyz"])
    m["rho"] = (f[0] + sx) + (sy + sz) + (qa + m["Qyz"])
    m["jx"] = dx + (m["Txyy"] + m["Txzz"])
    m["jy"] = dy + (m["Txxy"] + m["Tyzz"])
    m["jz"] = dz + (m["Txxz"] + m["Tyyz"])
    return m


def defects(m):
    ux, uy, uz = m["jx"], m["jy"], m["jz"]
    xx, yy, zz = ux * ux, uy * uy, uz * uz
    third = m["rho"] * (1.0 / 3.0)
    ninth = m["rho"] * (1.0 / 9.0) - (xx + yy + zz) * (1.0 / 6.0)
    d = {}
    d["Pxx"] = third + xx - m["Pxx"]
    d["Pyy"] = third + yy - m["Pyy"]
    d["Pzz"] = third + zz - m["Pzz"]
    d["Pxy"] = ux * uy - m["Pxy"]
    d["Pxz"] = ux * uz - m["Pxz"]
    d["Pyz"] = uy * uz - m["Pyz"]
    d["Qxy"] = ninth + (xx + yy) * 0.5 - m["Qxy"]
    d["Qxz"] = ninth + (xx + zz) * 0.5 - m["Qxz"]
    d["Qyz"] = ninth + (yy + zz) * 0.5 - m["Qyz"]
    return d


P_NAMES = ("Pxx", "Pyy", "Pzz", "Pxy", "Pxz", "Pyz")
Q_NAMES = ("Qxy", "Qxz", "Qyz")
M_NAMES = ("rho", "jx", "jy", "jz") + P_NAMES + Q_NAMES + ("Txyy", "Txzz", "Txxy", "Tyzz", "Txxz", "Tyyz")
T_OF = {"x": ("Txyy", "Txzz"), "y": ("Txxy", "Tyzz"), "z": ("Txxz", "Tyyz")}


def collide(m, d, s):
    h = 1.0 - s
    h16 = 1.6 * h
    t_keep = 0.8 * h - 1.0
    h04 = 0.4 * h
    j_keep = h - s
    o = {}
    for name in P_NAMES:
        o[name] = m[name] + h16 * d[name]
    for name in Q_NAMES:
        o[name] = m[name] + h * d[name]
    for axis in "xyz":
        j = m["j" + axis]
        o["j" + axis] = j_keep * j
        hj = h04 * j
        for name in T_OF[axis]:
            o[name] = t_keep * m[name] + hj
    f = [None] * 19
    qs = (o["Qxy"] + o["Qxz"]) + o["Qyz"]
    f[0] = (m["rho"] + qs) - ((o["Pxx"] + o["Pyy"]) + o["Pzz"])
    for a, p, q1, q2, axis in ((1, "Pxx", "Qxy", "Qxz", "x"), (3, "Pyy", "Qxy", "Qyz", "y"), (5, "Pzz", "Qxz", "Qyz", "z")):
        s_ = (o[p] - (o[q1] + o[q2])) * 0.5
        d_ = (o["j" + axis] - (o[T_OF[axis][0]] + o[T_OF[axis][1]])) * 0.5
        f[a] = s_ + d_
        f[a + 1] = s_ - d_
    for name, a, t1, t2 in (("xy", 7, "Txyy", "Txxy"), ("xz", 11, "Txzz", "Txxz"), ("yz", 15, "Tyzz", "Tyyz")):
        q = o["Q" + name] * 0.25
        p = o["P" + name] * 0.25
        u = o[t1] * 0.25
        w = o[t2] * 0.25
        sa, sb, da, db = q + p, q - p, u + w, u - w
        f[a] = sa + da
        f[a + 1] = sa - da
        f[a + 2] = sb + db
        f[a + 3] = sb - db
    return f


def adjoint(m, d, s, q):
    h = 1.0 - s
    h16 = 1.6 * h
    t_keep = 0.8 * h - 1.0
    h04 = 0.4 * h
    j_keep = h - s
    t = {}
    half = {}
    for axis, a in (("x", 1), ("y", 3), ("z", 5)):
        half[axis] = (q[a] + q[a + 1]) * 0.5
        t["j" + axis] = (q[a] - q[a + 1]) * 0.5
        t["P" + axis + axis] = half[axis] - q[0]
    for name, a, t1, t2 in (("xy", 7, "Txyy", "Txxy"), ("xz", 11, "Txzz", "Txxz"), ("yz", 15, "Tyzz", "Tyyz")):
        sa, da = q[a] + q[a + 1], q[a] - q[a + 1]
        sb, db = q[a + 2] + q[a + 3], q[a + 2] - q[a + 3]
        t["Q" + name] = (sa + sb) * 0.25 - half[name[0]] - t["P" + name[1] * 2]
        t["P" + name] = (sa - sb) * 0.25
        t[t1] = (da + db) * 0.25 - t["j" + name[0]]
        t[t2] = (da - db) * 0.25 - t["j" + name[1]]
    gp = t["Pxx"] * d["Pxx"]
    for name in P_NAMES[1:]:
        gp = gp + t[name] * d[name]
    gq = t["Qxy"] * d["Qxy"] + t["Qxz"] * d["Qxz"] + t["Qyz"] * d["Qyz"]
    gt = None
    gj = None
    tsum = {}
    for axis in "xyz":
        tsum[axis] = t[T_OF[axis][0]] + t[T_OF[axis][1]]
        term = t[T_OF[axis][0]] * m[T_OF[axis][0]] + t[T_OF[axis][1]] * m[T_OF[axis][1]]
        gt = term if gt is None else gt + term
        term = (2.0 * t["j" + axis] + 0.4 * tsum[axis]) * m["j" + axis]
        gj = term if gj is None else gj + term
    gs = -(1.6 * gp + gq + gj + 0.8 * gt)
    ux, uy, uz = m["jx"], m["jy"], m["jz"]
    p_keep = 1.0 - h16
    qsum = t["Qxy"] + t["Qxz"] + t["Qyz"]
    u = {}
    u["rho"] = q[0] + (h16 * (1.0 / 3.0)) * (t["Pxx"] + t["Pyy"] + t["Pzz"]) + (h * (1.0 / 9.0)) * qsum
    third = qsum * (1.0 / 3.0)
    w16 = {"x": t["Pxy"] * uy + t["Pxz"] * uz, "y": t["Pxy"] * ux + t["Pyz"] * uz, "z": t["Pxz"] * ux + t["Pyz"] * uy}
    other = {"x": "Qyz", "y": "Qxz", "z": "Qxy"}
    for axis, uu in (("x", ux), ("y", uy), ("z", uz)):
        quad = 2.0 * third - t[other[axis]]
        u["j" + axis] = (
            j_keep * t["j" + axis]
            + h04 * tsum[axis]
            + h16 * (w16[axis] + 2.0 * t["P" + axis + axis] * uu)
            + h * (quad * uu)
        )
    for name in P_NAMES:
        u[name] = p_keep * t[name]
    for name in Q_NAMES:
        u[name] = s * t[name]
    for axis in "xyz":
        for name in T_OF[axis]:
            u[name] = t_keep * t[name]
    a_ = [None] * 19
    a_[0] = u["rho"]
    for axis, a in (("x", 1), ("y", 3), ("z", 5)):
        e = u["rho"] + u["P" + axis + axis]
        a_[a] = e + u["j" + axis]
        a_[a + 1] = e - u["j" + axis]
    for name, a, t1, t2 in (("xy", 7, "Txyy", "Txxy"), ("xz", 11, "Txzz", "Txxz"), ("yz", 15, "Tyzz", "Tyyz")):
        e = u["rho"] + u["P" + name[0] * 2] + u["P" + name[1] * 2] + u["Q" + name]
        ea, eb = e + u["P" + name], e - u["P" + name]
        o1, o2 = u["j" + name[0]] + u[t1], u["j" + name[1]] + u[t2]
        oa, ob = o1 + o2, o1 - o2
        a_[a] = ea + oa
        a_[a + 1] = ea - oa
        a_[a + 2] = eb + ob
        a_[a + 3] = eb - ob
    return a_, gs


def misfit(c, arrived):
    q = []
    for i in range(19):
        v = arrived[OPP[i]]
        q.append(jnp.where(v > 0.5, (c[i] - (v - 2.0)) * INV_W[i], 0.0))
    return q


def iota(shape, dim):
    return lax.broadcasted_iota(jnp.int32, shape, dim)


def columns(slots, shape):
    row = iota(shape, 0)
    col = jnp.full(shape, -1, jnp.int32)
    for k in range(SLOTS):
        col = jnp.where(row == k, slots[k], col)
    return col


def load_all(copies):
    for c in copies:
        c.start()
    for c in copies:
        c.wait()


def unpack(f_raw, t_raw, s_raw, w_raw, f_rows, t_rows, frac, tiles):
    for t in range(tiles):
        lanes = pl.ds(t * 128, 128)
        for k in range(SLOTS):
            f_rows[t, pl.ds(k * SLOT_ROWS, 19), :] = f_raw[k, :, lanes]
            t_rows[t, pl.ds(k * SLOT_ROWS, 19), :] = t_raw[k, :, lanes].astype(jnp.float32)
        frac[pl.ds(0, SLOTS), lanes] = jnp.where(w_raw[:, lanes] == 1, 1.0, s_raw[:, lanes])


def fields_of(f_rows, t_rows, frac, valid, tile):
    f = [f_rows[tile, pl.ds(i, 8, stride=SLOT_ROWS), :] for i in range(19)]
    s = frac[:, pl.ds(pl.multiple_of(tile * 128, 128), 128)]
    m = moments(f)
    c = collide(m, defects(m), s)
    out = [jnp.where(valid, c[i], 0.0) for i in range(19)]
    for i in range(19):
        t = t_rows[tile, pl.ds(OPP[i], 8, stride=SLOT_ROWS), :]
        out.append(jnp.where(valid, t + 2.0, 0.0))
    return out, jnp.where(valid, s + 1.0, 0.0), m


def even(axis):
    return lax.rem(lax.axis_index(axis), 2) == 0


def border_kernel(slots_h, f_h, t_h, s_h, w_h, inside, across, slots, f_raw, t_raw, s_raw, w_raw, f_rows, t_rows, frac, sem):
    copies = [pltpu.make_async_copy(slots_h, slots, sem.at[0])]
    for e, lane in enumerate((0, CELLS - 512)):
        src, dst = pl.ds(lane, 512), pl.ds(e * 512, 512)
        copies += [
            pltpu.make_async_copy(f_h.at[:, :, src], f_raw.at[:, :, dst], sem.at[1 + e]),
            pltpu.make_async_copy(t_h.at[:, :, src], t_raw.at[:, :, dst], sem.at[3 + e]),
            pltpu.make_async_copy(s_h.at[:, src], s_raw.at[:, dst], sem.at[5 + e]),
            pltpu.make_async_copy(w_h.at[:, src], w_raw.at[:, dst], sem.at[7 + e]),
        ]
    load_all(copies)
    unpack(f_raw, t_raw, s_raw, w_raw, f_rows, t_rows, frac, 8)
    valid = columns(slots, (8, 128)) >= 0
    even_z = even("gz")
    for out, goes_up in ((inside, even_z), (across, jnp.logical_not(even_z))):
        for outer in (True, False):
            layer = jnp.where(goes_up, 3, 0) if outer else jnp.where(goes_up, 2, 1)
            for half in range(2):
                dst = pl.ds(half * 128, 128)
                fields, v, _ = fields_of(f_rows, t_rows, frac, valid, layer * 2 + half)
                for p, (n, src, _) in enumerate(ZP):
                    if src == outer:
                        m = mirror(n, 2)
                        val = fields[n] if m == n else jnp.where(goes_up, fields[n], fields[m])
                        out[pl.ds(p * SLOTS, SLOTS), dst] = val[0:SLOTS]
                if outer:
                    out[pl.ds(NP * SLOTS, SLOTS), dst] = v[0:SLOTS]


def fields_kernel(slots_h, f_h, t_h, s_h, w_h, store, vstore, mstore, moved, slots, f_raw, t_raw, s_raw, w_raw, f_rows, t_rows, frac, sem):
    load_all([
        pltpu.make_async_copy(slots_h, slots, sem.at[0]),
        pltpu.make_async_copy(f_h, f_raw, sem.at[1]),
        pltpu.make_async_copy(t_h, t_raw, sem.at[2]),
        pltpu.make_async_copy(s_h, s_raw, sem.at[3]),
        pltpu.make_async_copy(w_h, w_raw, sem.at[4]),
    ])
    unpack(f_raw, t_raw, s_raw, w_raw, f_rows, t_rows, frac, 16)
    valid = columns(slots, (8, 128)) >= 0

    def body(z, carry):
        for half in range(2):
            fields, v, m = fields_of(f_rows, t_rows, frac, valid, z * 2 + half)
            base = pl.multiple_of((z + 1) * 16 + half * 8, 8)
            for n in range(NF):
                store[n, pl.ds(base + vel(n)[2] * 16, 8), :] = fields[n]
            vstore[pl.ds(base, 8), :] = v
            for i, name in enumerate(M_NAMES):
                mstore[i, pl.ds(pl.multiple_of(z * 16 + half * 8, 8), 8), :] = m[name]
        return carry

    lax.fori_loop(0, DZ, body, 0)
    shift_layers(slots, store, moved, 2, ZI - 2)


def side_kernel(slots_h, store_in, vstore_in, r_inside, r_across, store, vstore, inside, across, slots, sem):
    del store_in, vstore_in
    fetch = pltpu.make_async_copy(slots_h, slots, sem.at[0])
    fetch.start()
    group = iota((8, 128), 1) // EDGE
    even_z = even("gz")
    for r, below in ((r_inside, jnp.logical_not(even_z)), (r_across, even_z)):
        ghost, first = jnp.where(below, 0, ZI - 1), jnp.where(below, 1, ZI - 2)
        for half in range(2):
            src = pl.ds(half * 128, 128)
            for p, (n, _, is_ghost) in enumerate(ZP):
                m = mirror(n, 2)
                field = n if m == n else jnp.where(below, n, m)
                zi = ghost if is_ghost else first
                store[field, pl.ds(zi * 16 + half * 8, SLOTS), :] = r[pl.ds(p * SLOTS, SLOTS), src]
            vstore[pl.ds(ghost * 16 + half * 8, SLOTS), :] = r[pl.ds(NP * SLOTS, SLOTS), src]
    fetch.wait()
    masks = [group == slots[k] for k in range(SLOTS)]
    even_x = even("blk")
    for out, right in ((inside, even_x), (across, jnp.logical_not(even_x))):
        half = jnp.where(right, 1, 0)
        for p, (n, outer, _) in enumerate(XP + [(None, True, None)]):
            if outer:
                xl = jnp.where(right, 7, 0)
            else:
                xl = jnp.where(right, 6, 1)
            if n is not None:
                m = mirror(n, 0)
                field = n if m == n else jnp.where(right, n, m)
            for part, count in ((0, 8), (1, 2)):
                acc = jnp.zeros((count, 128), jnp.float32)
                for k in range(SLOTS):
                    rows = pl.ds(part * 128 + half * 8 + k, count, stride=16)
                    v = vstore[rows, :] if n is None else store[field, rows, :]
                    shift = lax.rem((slots[k] - xl + 16) * EDGE, 128)
                    acc = jnp.where(masks[k][0:count], pltpu.roll(v, shift, 1), acc)
                out[pl.ds(p * ZI + part * 8, count), :] = acc


def shifter(slots):
    lane = iota((8, 128), 1)
    y = lax.rem(lane, EDGE)
    row = iota((8, 128), 0)
    col = columns(slots, (8, 128))
    prev = pltpu.roll(col, 1, 0)
    nxt = pltpu.roll(col, 7, 0)
    edge = {1: y == 0, -1: y == EDGE - 1}
    conn = {
        1: edge[1] & (row >= 1) & (col >= 0) & (prev == col - 1),
        -1: edge[-1] & (row < SLOTS - 1) & (nxt >= 0) & (nxt == col + 1),
    }
    low, high = lane < EDGE, lane >= 128 - EDGE

    def yshift(t, cy):
        if cy == 0:
            return t
        a = pltpu.roll(t, cy % 128, 1)
        b = pltpu.roll(pltpu.roll(t, (-15 * cy) % 128, 1), cy % 8, 0)
        return jnp.where(conn[cy], b, jnp.where(edge[cy], 0.0, a))

    def xyshift(t0, t1, v, ghost):
        t0, t1 = yshift(t0, v[1]), yshift(t1, v[1])
        if v[0] == 1:
            r0, r1 = pltpu.roll(t0, EDGE, 1), pltpu.roll(t1, EDGE, 1)
            return jnp.where(low, ghost, r0), jnp.where(low, r0, r1)
        if v[0] == -1:
            r0, r1 = pltpu.roll(t0, 128 - EDGE, 1), pltpu.roll(t1, 128 - EDGE, 1)
            return jnp.where(high, r1, r0), jnp.where(high, ghost, r1)
        return t0, t1

    return xyshift, low, high, col


def shift_layers(slots, store, moved, first, last):
    xyshift = shifter(slots)[0]

    def body(zi, carry):
        r0, r1 = pl.multiple_of(zi * 16, 8), pl.multiple_of(zi * 16 + 8, 8)
        for n in range(NF):
            t0, t1 = xyshift(store[n, pl.ds(r0, 8), :], store[n, pl.ds(r1, 8), :], vel(n), 0.0)
            moved[n, pl.ds(r0, 8), :] = t0
            moved[n, pl.ds(r1, 8), :] = t1
        return carry

    lax.fori_loop(first, last, body, 0)


def shift_kernel(slots_h, store, moved_in, moved, slots, sem):
    del moved_in
    load_all([pltpu.make_async_copy(slots_h, slots, sem.at[0])])
    shift_layers(slots, store, moved, 0, 2)
    shift_layers(slots, store, moved, ZI - 2, ZI)


def final_kernel(slots_h, moved, vstore, mstore, inside, across, r_inside, r_across, grad_h, out_h,
                 slots, gx, ghost_a, adj, back, out_rows, grad, out, sem):
    fetch = pltpu.make_async_copy(slots_h, slots, sem.at[0])
    fetch.start()
    lane16 = iota((16, 128), 1)
    first, last = lane16 == 0, lane16 == 127

    def yshift_dense(t, cy):
        if cy == 0:
            return t
        a = pltpu.roll(t, cy % 128, 1)
        return jnp.where(first if cy == 1 else last, 0.0, a)

    def to_packed(t, dst, n, xl):
        for k in range(SLOTS):
            shift = lax.rem((xl - slots[k] + 16) * EDGE, 128)
            r = pltpu.roll(t, shift, 1)
            dst[n, pl.ds(k, 8, stride=8), :] = r[0:8]
            dst[n, pl.ds(64 + k, 8, stride=8), :] = r[8:16]

    even_x = even("blk")
    for c_in, xl in ((1, 0), (-1, 7)):
        from_inside = jnp.logical_not(even_x) if c_in == 1 else even_x
        ghost = [None] * NF
        packs = []
        for p, (n, _, is_ghost) in enumerate(XP + [(None, None, True)]):
            rows = pl.ds(p * ZI, 16)
            t = jnp.where(from_inside, r_inside[rows, :], r_across[rows, :])
            if n is None:
                v = t
                continue
            m = n if c_in == 1 else mirror(n, 0)
            if is_ghost:
                ghost[m] = t
            else:
                packs.append((yshift_dense(t, vel(m)[1]), gx, m))
                own = jnp.where(from_inside, inside[rows, :], across[rows, :])
                ghost[mirror(m, 0)] = own
        ghost = [yshift_dense(ghost[n], vel(n)[1]) for n in range(NF)]
        m = moments(ghost[:19])
        d = defects(m)
        s = v - 1.0
        a, _ = adjoint(m, d, s, misfit(collide(m, d, s), ghost[19:]))
        for n in range(19):
            if VEL[n][0] == c_in:
                t = jnp.where(v > 0.5, a[OPP[n]], 0.0)
                packs.append((yshift_dense(t, VEL[n][1]), ghost_a, n))
        if c_in == 1:
            fetch.wait()
        for t, dst, n in packs:
            to_packed(t, dst, n, xl)

    xyshift, low, high, col = shifter(slots)

    def advance(zi, carry):
        for half in range(2):
            r = pl.multiple_of(zi * 16 + half * 8, 8)
            f = []
            for n in range(NF):
                t = moved[n, pl.ds(r, 8), :]
                if vel(n)[0] == 1 - 2 * half:
                    g = gx[n, pl.ds(pl.multiple_of(zi * 8, 8), 8), :]
                    t = jnp.where(high if half else low, g, t)
                f.append(t)
            v = vstore[pl.ds(r, 8), :]
            s = v - 1.0
            m = moments(f[:19])
            d = defects(m)
            a, gs = adjoint(m, d, s, misfit(collide(m, d, s), f[19:]))
            listed = (v > 0.5) & (col >= 0)
            for n in range(19):
                adj[n, pl.ds(r, 8), :] = jnp.where(listed, a[OPP[n]], 0.0)
            adj[19, pl.ds(r, 8), :] = gs
        return carry

    lax.fori_loop(0, ZI, advance, 0)

    def writes(z):
        lanes = pl.ds(pl.multiple_of(z * 256, 128), 256)
        return (
            pltpu.make_async_copy(out.at[:, :, lanes], out_h.at[:, :, lanes], sem.at[1 + z]),
            pltpu.make_async_copy(grad.at[:, lanes], grad_h.at[:, lanes], sem.at[1 + DZ + z]),
        )

    def retreat(z, carry):
        zi = z + 1
        for n in range(19):
            src = zi - VEL[n][2]
            t0 = adj[n, pl.ds(pl.multiple_of(src * 16, 8), 8), :]
            t1 = adj[n, pl.ds(pl.multiple_of(src * 16 + 8, 8), 8), :]
            g = ghost_a[n, pl.ds(pl.multiple_of(src * 8, 8), 8), :] if VEL[n][0] else None
            t0, t1 = xyshift(t0, t1, VEL[n], g)
            back[n, 0] = t0
            back[n, 1] = t1
        for half in range(2):
            lanes = pl.ds(pl.multiple_of(z * 256 + half * 128, 128), 128)
            r = pl.ds(pl.multiple_of(z * 16 + half * 8, 8), 8)
            r1 = pl.ds(pl.multiple_of(zi * 16 + half * 8, 8), 8)
            m = {name: mstore[i, r, :] for i, name in enumerate(M_NAMES)}
            v = vstore[r1, :]
            listed = (v > 0.5) & (col >= 0)
            s = v - 1.0
            q = [back[OPP[i], half] for i in range(19)]
            a, gs = adjoint(m, defects(m), s, q)
            for i in range(19):
                out_rows[z * 2 + half, pl.ds(i, 8, stride=SLOT_ROWS), :] = jnp.where(listed, a[i], 0.0)
            g2 = jnp.where(listed & (v < 1.75), gs + adj[19, r1, :], 0.0)
            grad[:, lanes] = g2[0:SLOTS]
            for k in range(SLOTS):
                out[k, :, lanes] = out_rows[z * 2 + half, pl.ds(k * SLOT_ROWS, 19), :]
        for c in writes(z):
            c.start()
        return carry

    lax.fori_loop(0, DZ, retreat, 0, unroll=2)

    def finish(z, carry):
        for c in writes(z):
            c.wait()
        return carry

    lax.fori_loop(0, DZ, finish, 0)


HBM = pl.BlockSpec(memory_space=pltpu.HBM)
VMEM = pl.BlockSpec(memory_space=pltpu.VMEM)


def exchange(inside, across, axis):
    count = lax.axis_size(axis)
    first = [(i, i ^ 1) for i in range(count)]
    second = []
    for i in range(1, count - 1, 2):
        second += [(i, i + 1), (i + 1, i)]
    return lax.ppermute(inside, axis, first), lax.ppermute(across, axis, second)


def per_device(populations, target, solid_frac, wall_mask, slot_column):
    f32 = jnp.float32
    populations = jnp.transpose(populations, (1, 0, 2))
    target = jnp.transpose(target, (1, 0, 2))
    populations, target, solid_frac, wall_mask, slot_column = (
        pltpu.with_memory_space_constraint(x, pltpu.HBM) for x in (populations, target, solid_frac, wall_mask, slot_column)
    )

    def params(mib):
        return pltpu.CompilerParams(vmem_limit_bytes=mib << 20)

    def inputs(cells):
        return [
            pltpu.SMEM((SLOTS,), jnp.int32),
            pltpu.VMEM((SLOTS, 19, cells), f32),
            pltpu.VMEM((SLOTS, 19, cells), jnp.bfloat16),
            pltpu.VMEM((SLOTS, cells), f32),
            pltpu.VMEM((SLOTS, cells), jnp.int32),
            pltpu.VMEM((cells // 128, 8 * SLOT_ROWS, 128), f32),
            pltpu.VMEM((cells // 128, 8 * SLOT_ROWS, 128), f32),
            pltpu.VMEM((8, cells), f32),
            pltpu.SemaphoreType.DMA((9,)),
        ]

    slots_in = [pltpu.SMEM((SLOTS,), jnp.int32)]
    zbuf = jax.ShapeDtypeStruct((ZROWS, 256), f32)
    inside, across = pl.pallas_call(
        border_kernel,
        in_specs=[HBM] * 5,
        out_specs=[VMEM] * 2,
        out_shape=[zbuf, zbuf],
        scratch_shapes=inputs(1024),
        compiler_params=params(8),
    )(slot_column, populations, target, solid_frac, wall_mask)
    r_inside, r_across = exchange(inside, across, "gz")
    store_t = jax.ShapeDtypeStruct((NF, ROWS_STORE, 128), f32)
    vstore_t = jax.ShapeDtypeStruct((ROWS_STORE, 128), f32)
    store, vstore, mstore, moved = pl.pallas_call(
        fields_kernel,
        in_specs=[HBM] * 5,
        out_specs=[VMEM] * 4,
        out_shape=[store_t, vstore_t, jax.ShapeDtypeStruct((19, DZ * 16, 128), f32), store_t],
        scratch_shapes=inputs(CELLS),
        compiler_params=params(12),
    )(slot_column, populations, target, solid_frac, wall_mask)
    xbuf = jax.ShapeDtypeStruct((XROWS, 128), f32)
    store, vstore, inside, across = pl.pallas_call(
        side_kernel,
        in_specs=[HBM] + [VMEM] * 4,
        out_specs=[VMEM] * 4,
        out_shape=[store_t, vstore_t, xbuf, xbuf],
        input_output_aliases={1: 0, 2: 1},
        scratch_shapes=slots_in + [pltpu.SemaphoreType.DMA((1,))],
        compiler_params=params(12),
    )(slot_column, store, vstore, r_inside, r_across)
    r_inside, r_across = exchange(inside, across, "blk")
    moved = pl.pallas_call(
        shift_kernel,
        in_specs=[HBM, VMEM, VMEM],
        out_specs=VMEM,
        out_shape=store_t,
        input_output_aliases={2: 0},
        scratch_shapes=slots_in + [pltpu.SemaphoreType.DMA((1,))],
        compiler_params=params(12),
    )(slot_column, store, moved)
    grad, adjoint_out = pl.pallas_call(
        final_kernel,
        in_specs=[HBM] + [VMEM] * 7,
        out_specs=[HBM, HBM],
        out_shape=[
            jax.ShapeDtypeStruct((SLOTS, CELLS), f32),
            jax.ShapeDtypeStruct((SLOTS, 19, CELLS), f32),
        ],
        scratch_shapes=slots_in + [
            pltpu.VMEM((NF, 128, 128), f32),
            pltpu.VMEM((19, 128, 128), f32),
            pltpu.VMEM((20, ZI * 16, 128), f32),
            pltpu.VMEM((19, 2, 8, 128), f32),
            pltpu.VMEM((CELLS // 128, 8 * SLOT_ROWS, 128), f32),
            pltpu.VMEM((SLOTS, CELLS), f32),
            pltpu.VMEM((SLOTS, 19, CELLS), f32),
            pltpu.SemaphoreType.DMA((1 + 2 * DZ,)),
        ],
        compiler_params=params(20),
    )(slot_column, moved, vstore, mstore, inside, across, r_inside, r_across)
    return grad, jnp.transpose(adjoint_out, (1, 0, 2))


def solution(mesh):
    return jax.shard_map(
        per_device,
        mesh=mesh,
        in_specs=(
            P(None, "blk", "gz"),
            P(None, "blk", "gz"),
            P("blk", "gz"),
            P("blk", "gz"),
            P("blk"),
        ),
        out_specs=(P("blk", "gz"), P(None, "blk", "gz")),
        check_vma=False,
    )
```

```python
import jax
import jax.numpy as jnp
from jax import lax
from jax.experimental import pallas as pl
from jax.experimental.pallas import tpu as pltpu
from jax.sharding import PartitionSpec as P

EDGE = 16
GY = 8
SLOTS = 5
DZ = 8
CELLS = DZ * EDGE * EDGE

VEL = (
    (0, 0, 0),
    (1, 0, 0), (-1, 0, 0), (0, 1, 0), (0, -1, 0), (0, 0, 1), (0, 0, -1),
    (1, 1, 0), (-1, -1, 0), (1, -1, 0), (-1, 1, 0),
    (1, 0, 1), (-1, 0, -1), (1, 0, -1), (-1, 0, 1),
    (0, 1, 1), (0, -1, -1), (0, 1, -1), (0, -1, 1),
)
OPP = (0, 2, 1, 4, 3, 6, 5, 8, 7, 10, 9, 12, 11, 14, 13, 16, 15, 18, 17)
T_SCALE = (3.0,) + (9.0,) * 18

NF = 38
ZI = 10
ROWS_STORE = ZI * 16
HALF = 56
ROWS_COMPACT = 2 * HALF
ROWS_OWN = 2 * DZ * 5
EDGE_LAYERS = 4


def place(zd):
    return {-1: 0, 0: 1, DZ - 1: 2, DZ: 3}.get(zd, zd + 3)


def place_of(zd):
    return jnp.where(zd < 1, zd + 1, jnp.where(zd > DZ - 2, zd - DZ + 3, zd + 3))


def vel(n):
    return VEL[n % 19]


def mirror(n, dim):
    v = list(vel(n))
    v[dim] = -v[dim]
    return n // 19 * 19 + VEL.index(tuple(v))


def planes(dim):
    out = []
    for n in range(NF):
        c = vel(n)[dim]
        if c == 0:
            out.append((n, True, True))
        elif c == 1:
            out.append((n, False, True))
            out.append((n, True, False))
    return out


ZP, XP = planes(2), planes(0)
NP = len(ZP)
ZROWS = 200
XROWS = 400
SLOT_ROWS = 24


def moments(f):
    m = {}

    def pair(a):
        return f[a] + f[a + 1], f[a] - f[a + 1]

    sx, dx = pair(1)
    sy, dy = pair(3)
    sz, dz = pair(5)
    for name, a, t1, t2 in (("xy", 7, "xyy", "xxy"), ("xz", 11, "xzz", "xxz"), ("yz", 15, "yzz", "yyz")):
        sa, da = pair(a)
        sb, db = pair(a + 2)
        m["Q" + name] = sa + sb
        m["P" + name] = sa - sb
        m["T" + t1] = da + db
        m["T" + t2] = da - db
    qa = m["Qxy"] + m["Qxz"]
    m["Pxx"] = sx + qa
    m["Pyy"] = sy + (m["Qxy"] + m["Qyz"])
    m["Pzz"] = sz + (m["Qxz"] + m["Qyz"])
    m["rho"] = (f[0] + sx) + (sy + sz) + (qa + m["Qyz"])
    m["jx"] = dx + (m["Txyy"] + m["Txzz"])
    m["jy"] = dy + (m["Txxy"] + m["Tyzz"])
    m["jz"] = dz + (m["Txxz"] + m["Tyyz"])
    return m


def defects(m):
    ux, uy, uz = m["jx"], m["jy"], m["jz"]
    xx, yy, zz = ux * ux, uy * uy, uz * uz
    third = m["rho"] * (1.0 / 3.0)
    ninth = m["rho"] * (1.0 / 9.0) - (xx + yy + zz) * (1.0 / 6.0)
    d = {}
    d["Pxx"] = third + xx - m["Pxx"]
    d["Pyy"] = third + yy - m["Pyy"]
    d["Pzz"] = third + zz - m["Pzz"]
    d["Pxy"] = ux * uy - m["Pxy"]
    d["Pxz"] = ux * uz - m["Pxz"]
    d["Pyz"] = uy * uz - m["Pyz"]
    d["Qxy"] = ninth + (xx + yy) * 0.5 - m["Qxy"]
    d["Qxz"] = ninth + (xx + zz) * 0.5 - m["Qxz"]
    d["Qyz"] = ninth + (yy + zz) * 0.5 - m["Qyz"]
    return d


P_NAMES = ("Pxx", "Pyy", "Pzz", "Pxy", "Pxz", "Pyz")
Q_NAMES = ("Qxy", "Qxz", "Qyz")
M_NAMES = ("rho", "jx", "jy", "jz") + P_NAMES + Q_NAMES + ("Txyy", "Txzz", "Txxy", "Tyzz", "Txxz", "Tyyz")
T_OF = {"x": ("Txyy", "Txzz"), "y": ("Txxy", "Tyzz"), "z": ("Txxz", "Tyyz")}


def collide(m, d, s, scaled=False):
    two, four, shift = (4.5, 2.25, 18.0) if scaled else (0.5, 0.25, None)
    h = 1.0 - s
    h16 = 1.6 * h
    t_keep = 0.8 * h - 1.0
    h04 = 0.4 * h
    j_keep = h - s
    o = {}
    for name in P_NAMES:
        o[name] = m[name] + h16 * d[name]
    for name in Q_NAMES:
        o[name] = m[name] + h * d[name]
    for axis in "xyz":
        j = m["j" + axis]
        o["j" + axis] = j_keep * j
        hj = h04 * j
        for name in T_OF[axis]:
            o[name] = t_keep * m[name] + hj
    f = [None] * 19
    qs = (o["Qxy"] + o["Qxz"]) + o["Qyz"]
    f[0] = (m["rho"] + qs) - ((o["Pxx"] + o["Pyy"]) + o["Pzz"])
    if scaled:
        f[0] = 3.0 * f[0] + 6.0
    for a, p, q1, q2, axis in ((1, "Pxx", "Qxy", "Qxz", "x"), (3, "Pyy", "Qxy", "Qyz", "y"), (5, "Pzz", "Qxz", "Qyz", "z")):
        s_ = (o[p] - (o[q1] + o[q2])) * two
        if scaled:
            s_ = s_ + shift
        d_ = (o["j" + axis] - (o[T_OF[axis][0]] + o[T_OF[axis][1]])) * two
        f[a] = s_ + d_
        f[a + 1] = s_ - d_
    for name, a, t1, t2 in (("xy", 7, "Txyy", "Txxy"), ("xz", 11, "Txzz", "Txxz"), ("yz", 15, "Tyzz", "Tyyz")):
        q = o["Q" + name] * four
        if scaled:
            q = q + shift
        p = o["P" + name] * four
        u = o[t1] * four
        w = o[t2] * four
        sa, sb, da, db = q + p, q - p, u + w, u - w
        f[a] = sa + da
        f[a + 1] = sa - da
        f[a + 2] = sb + db
        f[a + 3] = sb - db
    return f


def adjoint(m, d, s, q, scaled=False):
    by_two = (lambda x: x) if scaled else (lambda x: x * 0.5)
    by_four = (lambda x: x) if scaled else (lambda x: x * 0.25)
    h = 1.0 - s
    h16 = 1.6 * h
    t_keep = 0.8 * h - 1.0
    h04 = 0.4 * h
    j_keep = h - s
    t = {}
    half = {}
    for axis, a in (("x", 1), ("y", 3), ("z", 5)):
        half[axis] = by_two(q[a] + q[a + 1])
        t["j" + axis] = by_two(q[a] - q[a + 1])
        t["P" + axis + axis] = half[axis] - q[0]
    for name, a, t1, t2 in (("xy", 7, "Txyy", "Txxy"), ("xz", 11, "Txzz", "Txxz"), ("yz", 15, "Tyzz", "Tyyz")):
        sa, da = q[a] + q[a + 1], q[a] - q[a + 1]
        sb, db = q[a + 2] + q[a + 3], q[a + 2] - q[a + 3]
        t["Q" + name] = by_four(sa + sb) - half[name[0]] - t["P" + name[1] * 2]
        t["P" + name] = by_four(sa - sb)
        t[t1] = by_four(da + db) - t["j" + name[0]]
        t[t2] = by_four(da - db) - t["j" + name[1]]
    gp = t["Pxx"] * d["Pxx"]
    for name in P_NAMES[1:]:
        gp = gp + t[name] * d[name]
    gq = t["Qxy"] * d["Qxy"] + t["Qxz"] * d["Qxz"] + t["Qyz"] * d["Qyz"]
    gt = None
    gj = None
    tsum = {}
    for axis in "xyz":
        tsum[axis] = t[T_OF[axis][0]] + t[T_OF[axis][1]]
        term = t[T_OF[axis][0]] * m[T_OF[axis][0]] + t[T_OF[axis][1]] * m[T_OF[axis][1]]
        gt = term if gt is None else gt + term
        term = (2.0 * t["j" + axis] + 0.4 * tsum[axis]) * m["j" + axis]
        gj = term if gj is None else gj + term
    gs = -(1.6 * gp + gq + gj + 0.8 * gt)
    ux, uy, uz = m["jx"], m["jy"], m["jz"]
    p_keep = 1.0 - h16
    qsum = t["Qxy"] + t["Qxz"] + t["Qyz"]
    u = {}
    u["rho"] = q[0] + (h16 * (1.0 / 3.0)) * (t["Pxx"] + t["Pyy"] + t["Pzz"]) + (h * (1.0 / 9.0)) * qsum
    third = qsum * (1.0 / 3.0)
    w16 = {"x": t["Pxy"] * uy + t["Pxz"] * uz, "y": t["Pxy"] * ux + t["Pyz"] * uz, "z": t["Pxz"] * ux + t["Pyz"] * uy}
    other = {"x": "Qyz", "y": "Qxz", "z": "Qxy"}
    for axis, uu in (("x", ux), ("y", uy), ("z", uz)):
        quad = 2.0 * third - t[other[axis]]
        u["j" + axis] = (
            j_keep * t["j" + axis]
            + h04 * tsum[axis]
            + h16 * (w16[axis] + 2.0 * t["P" + axis + axis] * uu)
            + h * (quad * uu)
        )
    for name in P_NAMES:
        u[name] = p_keep * t[name]
    for name in Q_NAMES:
        u[name] = s * t[name]
    for axis in "xyz":
        for name in T_OF[axis]:
            u[name] = t_keep * t[name]
    a_ = [None] * 19
    a_[0] = u["rho"]
    for axis, a in (("x", 1), ("y", 3), ("z", 5)):
        e = u["rho"] + u["P" + axis + axis]
        a_[a] = e + u["j" + axis]
        a_[a + 1] = e - u["j" + axis]
    for name, a, t1, t2 in (("xy", 7, "Txyy", "Txxy"), ("xz", 11, "Txzz", "Txxz"), ("yz", 15, "Tyzz", "Tyyz")):
        e = u["rho"] + u["P" + name[0] * 2] + u["P" + name[1] * 2] + u["Q" + name]
        ea, eb = e + u["P" + name], e - u["P" + name]
        o1, o2 = u["j" + name[0]] + u[t1], u["j" + name[1]] + u[t2]
        oa, ob = o1 + o2, o1 - o2
        a_[a] = ea + oa
        a_[a + 1] = ea - oa
        a_[a + 2] = eb + ob
        a_[a + 3] = eb - ob
    return a_, gs


def misfit(c, arrived):
    return [jnp.where(arrived[OPP[i]] > 1.0, c[i] - arrived[OPP[i]], 0.0) for i in range(19)]


def iota(shape, dim):
    return lax.broadcasted_iota(jnp.int32, shape, dim)


def columns(slots, shape):
    row = iota(shape, 0)
    col = jnp.full(shape, -1, jnp.int32)
    for k in range(SLOTS):
        col = jnp.where(row == k, slots[k], col)
    return col


def load_all(copies):
    for c in copies:
        c.start()
    for c in copies:
        c.wait()


def unpack(f_raw, t_raw, s_raw, w_raw, f_rows, t_rows, frac, tiles):
    for t in range(tiles):
        lanes = pl.ds(t * 128, 128)
        for k in range(SLOTS):
            f_rows[t, pl.ds(k * SLOT_ROWS, 19), :] = f_raw[k, :, lanes]
            t_rows[t, pl.ds(k * SLOT_ROWS, 19), :] = t_raw[k, :, lanes].astype(jnp.float32)
        frac[pl.ds(0, SLOTS), lanes] = jnp.where(w_raw[:, lanes] == 1, 1.0, s_raw[:, lanes])


def fields_of(f_rows, t_rows, frac, valid, tile):
    f = [f_rows[tile, pl.ds(i, 8, stride=SLOT_ROWS), :] for i in range(19)]
    s = frac[:, pl.ds(pl.multiple_of(tile * 128, 128), 128)]
    m = moments(f)
    c = collide(m, defects(m), s)
    out = [jnp.where(valid, c[i], 0.0) for i in range(19)]
    for i in range(19):
        t = t_rows[tile, pl.ds(OPP[i], 8, stride=SLOT_ROWS), :]
        out.append(jnp.where(valid, T_SCALE[i] * t + 2.0 * T_SCALE[i], 0.0))
    return out, jnp.where(valid, s + 1.0, 0.0), m


def even(axis):
    return lax.rem(lax.axis_index(axis), 2) == 0


def border_kernel(slots_h, f_h, t_h, s_h, w_h, inside, across, slots, f_raw, t_raw, s_raw, w_raw, f_rows, t_rows, frac, sem):
    copies = [pltpu.make_async_copy(slots_h, slots, sem.at[0])]
    for e, lane in enumerate((0, CELLS - 512)):
        src, dst = pl.ds(lane, 512), pl.ds(e * 512, 512)
        copies += [
            pltpu.make_async_copy(f_h.at[:, :, src], f_raw.at[:, :, dst], sem.at[1 + e]),
            pltpu.make_async_copy(t_h.at[:, :, src], t_raw.at[:, :, dst], sem.at[3 + e]),
            pltpu.make_async_copy(s_h.at[:, src], s_raw.at[:, dst], sem.at[5 + e]),
            pltpu.make_async_copy(w_h.at[:, src], w_raw.at[:, dst], sem.at[7 + e]),
        ]
    load_all(copies)
    unpack(f_raw, t_raw, s_raw, w_raw, f_rows, t_rows, frac, 8)
    valid = columns(slots, (8, 128)) >= 0
    even_z = even("gz")
    for out, goes_up in ((inside, even_z), (across, jnp.logical_not(even_z))):
        for outer in (True, False):
            layer = jnp.where(goes_up, 3, 0) if outer else jnp.where(goes_up, 2, 1)
            for half in range(2):
                dst = pl.ds(half * 128, 128)
                fields, v, _ = fields_of(f_rows, t_rows, frac, valid, layer * 2 + half)
                for p, (n, src, _) in enumerate(ZP):
                    if src == outer:
                        m = mirror(n, 2)
                        val = fields[n] if m == n else jnp.where(goes_up, fields[n], fields[m])
                        out[pl.ds(p * SLOTS, SLOTS), dst] = val[0:SLOTS]
                if outer:
                    out[pl.ds(NP * SLOTS, SLOTS), dst] = v[0:SLOTS]


def fields_kernel(slots_h, f_h, t_h, s_h, w_h, store, vstore, mstore, moved, inside, across, slots, f_raw, t_raw, s_raw, w_raw, f_rows, t_rows, frac, sem):
    load_all([
        pltpu.make_async_copy(slots_h, slots, sem.at[0]),
        pltpu.make_async_copy(f_h, f_raw, sem.at[1]),
        pltpu.make_async_copy(t_h, t_raw, sem.at[2]),
        pltpu.make_async_copy(s_h, s_raw, sem.at[3]),
        pltpu.make_async_copy(w_h, w_raw, sem.at[4]),
    ])
    unpack(f_raw, t_raw, s_raw, w_raw, f_rows, t_rows, frac, 16)
    valid = columns(slots, (8, 128)) >= 0

    def body(z, carry):
        rows = {c: pl.multiple_of(place_of(z + c) * 16, 16) for c in (-1, 0, 1)}
        for half in range(2):
            fields, v, m = fields_of(f_rows, t_rows, frac, valid, z * 2 + half)
            for n in range(NF):
                store[n, pl.ds(rows[vel(n)[2]] + half * 8, 8), :] = fields[n]
            vstore[pl.ds(rows[0] + half * 8, 8), :] = v
            own = pl.ds(half * DZ * 5 + z * 5, SLOTS)
            for i, name in enumerate(M_NAMES):
                mstore[i, own, :] = m[name][0:SLOTS]
            mstore[19, own, :] = v[0:SLOTS]
        return carry

    lax.fori_loop(0, DZ, body, 0)
    side_planes(slots, store, vstore, inside, across, EDGE_LAYERS, ZI)
    shift_layers(slots, store, moved, EDGE_LAYERS, ZI)


def side_planes(slots, store, vstore, inside, across, first, last):
    count = last - first
    group = iota((count, 128), 1) // EDGE
    masks = [group == slots[k] for k in range(SLOTS)]
    even_x = even("blk")
    for out, right in ((inside, even_x), (across, jnp.logical_not(even_x))):
        if out is None:
            continue
        half = jnp.where(right, 1, 0)
        outer_x, inner_x = jnp.where(right, 7, 0), jnp.where(right, 6, 1)
        shifts = {
            outer: [lax.rem((slots[k] - (outer_x if outer else inner_x) + 16) * EDGE, 128) for k in range(SLOTS)]
            for outer in (True, False)
        }
        for p, (n, outer, _) in enumerate(XP + [(None, True, None)]):
            if n is not None:
                m = mirror(n, 0)
                field = n if m == n else jnp.where(right, n, m)
            acc = jnp.zeros((count, 128), jnp.float32)
            for k in range(SLOTS):
                rows = pl.ds(first * 16 + half * 8 + k, count, stride=16)
                v = vstore[rows, :] if n is None else store[field, rows, :]
                acc = jnp.where(masks[k], pltpu.roll(v, shifts[outer][k], 1), acc)
            out[pl.ds(p * ZI + first, count), :] = acc


def side_kernel(slots_h, store_in, vstore_in, inside_in, across_in, r_inside, r_across,
                store, vstore, inside, across, slots, sem):
    del store_in, vstore_in, inside_in, across_in
    fetch = pltpu.make_async_copy(slots_h, slots, sem.at[0])
    fetch.start()
    even_z, alone = even("gz"), at_end("gz")
    for r, below in ((r_inside, jnp.logical_not(even_z)), (r_across, even_z)):
        ghost = jnp.where(below, place(-1), place(DZ)) * 16
        first = jnp.where(below, place(0), place(DZ - 1)) * 16
        for half in range(2):
            src = pl.ds(half * 128, 128)
            for p, (n, _, is_ghost) in enumerate(ZP):
                m = mirror(n, 2)
                field = n if m == n else jnp.where(below, n, m)
                row = ghost if is_ghost else first
                t = r[pl.ds(p * SLOTS, SLOTS), src]
                if r is r_across and not is_ghost:
                    t = jnp.where(alone, 0.0, t)
                store[field, pl.ds(row + half * 8, SLOTS), :] = t
            t = r[pl.ds(NP * SLOTS, SLOTS), src]
            if r is r_across:
                t = jnp.where(alone, 0.0, t)
            vstore[pl.ds(ghost + half * 8, SLOTS), :] = t
    fetch.wait()
    side_planes(slots, store, vstore, inside, across, 0, EDGE_LAYERS)


def shifter(slots):
    lane = iota((8, 128), 1)
    y = lax.rem(lane, EDGE)
    row = iota((8, 128), 0)
    col = columns(slots, (8, 128))
    prev = pltpu.roll(col, 1, 0)
    nxt = pltpu.roll(col, 7, 0)
    edge = {1: y == 0, -1: y == EDGE - 1}
    conn = {
        1: edge[1] & (row >= 1) & (col >= 0) & (prev == col - 1),
        -1: edge[-1] & (row < SLOTS - 1) & (nxt >= 0) & (nxt == col + 1),
    }
    low, high = lane < EDGE, lane >= 128 - EDGE

    def yshift(t, cy):
        if cy == 0:
            return t
        a = pltpu.roll(t, cy % 128, 1)
        b = pltpu.roll(pltpu.roll(t, (-15 * cy) % 128, 1), cy % 8, 0)
        return jnp.where(conn[cy], b, jnp.where(edge[cy], 0.0, a))

    def xyshift(t0, t1, v, ghost):
        t0, t1 = yshift(t0, v[1]), yshift(t1, v[1])
        if v[0] == 1:
            r0, r1 = pltpu.roll(t0, EDGE, 1), pltpu.roll(t1, EDGE, 1)
            return jnp.where(low, ghost, r0), jnp.where(low, r0, r1)
        if v[0] == -1:
            r0, r1 = pltpu.roll(t0, 128 - EDGE, 1), pltpu.roll(t1, 128 - EDGE, 1)
            return jnp.where(high, r1, r0), jnp.where(high, ghost, r1)
        return t0, t1

    return xyshift, low, high


def shift_layers(slots, store, moved, first, last):
    xyshift = shifter(slots)[0]

    def body(at, carry):
        r0, r1 = pl.multiple_of(at * 16, 8), pl.multiple_of(at * 16 + 8, 8)
        for n in range(NF):
            t0, t1 = xyshift(store[n, pl.ds(r0, 8), :], store[n, pl.ds(r1, 8), :], vel(n), 0.0)
            moved[n, pl.ds(at * 5, SLOTS), :] = t0[0:SLOTS]
            moved[n, pl.ds(HALF + at * 5, SLOTS), :] = t1[0:SLOTS]
        return carry

    lax.fori_loop(first, last, body, 0)


def shift_kernel(slots_h, store, vstore, moved_in, moved, vmoved, slots, sem):
    del moved_in
    fetch = pltpu.make_async_copy(slots_h, slots, sem.at[0])
    fetch.start()
    for at in range(ZI):
        for half in range(2):
            vmoved[pl.ds(half * HALF + at * 5, SLOTS), :] = vstore[pl.ds(at * 16 + half * 8, SLOTS), :]
    fetch.wait()
    shift_layers(slots, store, moved, 0, EDGE_LAYERS)


def final_kernel(slots_h, moved, vmoved, mstore, inside, across, r_inside, r_across, grad_h, out_h,
                 slots, gx, ghost_a, adj, back, a0, g0, grad, out, sem):
    fetch = pltpu.make_async_copy(slots_h, slots, sem.at[0])
    fetch.start()
    lane16 = iota((16, 128), 1)
    first, last = lane16 == 0, lane16 == 127

    def yshift_dense(t, cy):
        if cy == 0:
            return t
        a = pltpu.roll(t, cy % 128, 1)
        return jnp.where(first if cy == 1 else last, 0.0, a)

    def to_packed(t, dst, n, xl):
        for k in range(SLOTS):
            shift = lax.rem((xl - slots[k] + 16) * EDGE, 128)
            r = pltpu.roll(t, shift, 1)
            dst[n, pl.ds(k, 8, stride=5), :] = r[0:8]
            dst[n, pl.ds(40 + k, ZI - 8, stride=5), :] = r[8:ZI]

    even_x, alone = even("blk"), at_end("blk")
    for c_in, xl in ((1, 0), (-1, 7)):
        from_inside = jnp.logical_not(even_x) if c_in == 1 else even_x
        ghost = [None] * NF
        packs = []
        for p, (n, _, is_ghost) in enumerate(XP + [(None, None, True)]):
            rows = pl.ds(p * ZI, 16)
            t = jnp.where(from_inside, r_inside[rows, :], r_across[rows, :])
            if n is None or not is_ghost:
                t = jnp.where(alone & jnp.logical_not(from_inside), 0.0, t)
            if n is None:
                v = t
                continue
            m = n if c_in == 1 else mirror(n, 0)
            if is_ghost:
                ghost[m] = t
            else:
                packs.append((yshift_dense(t, vel(m)[1]), gx, m))
                own = jnp.where(from_inside, inside[rows, :], across[rows, :])
                ghost[mirror(m, 0)] = own
        ghost = [yshift_dense(ghost[n], vel(n)[1]) for n in range(NF)]
        m = moments(ghost[:19])
        d = defects(m)
        s = v - 1.0
        a, _ = adjoint(m, d, s, misfit(collide(m, d, s, True), ghost[19:]), True)
        for n in range(19):
            if VEL[n][0] == c_in:
                t = jnp.where(v > 0.5, a[OPP[n]], 0.0)
                packs.append((yshift_dense(t, VEL[n][1]), ghost_a, n))
        if c_in == 1:
            fetch.wait()
        for t, dst, n in packs:
            to_packed(t, dst, n, xl)

    xyshift, low, high = shifter(slots)

    def advance(i, carry):
        for half in range(2):
            r = pl.ds(pl.multiple_of(half * HALF + i * 8, 8), 8)
            f = []
            for n in range(NF):
                t = moved[n, r, :]
                if vel(n)[0] == 1 - 2 * half:
                    g = gx[n, pl.ds(pl.multiple_of(i * 8, 8), 8), :]
                    t = jnp.where(high if half else low, g, t)
                f.append(t)
            v = vmoved[r, :]
            s = v - 1.0
            m = moments(f[:19])
            d = defects(m)
            a, gs = adjoint(m, d, s, misfit(collide(m, d, s, True), f[19:]), True)
            listed = v > 0.5
            for n in range(19):
                adj[n, r, :] = jnp.where(listed, a[OPP[n]], 0.0)
            adj[19, r, :] = gs
        return carry

    lax.fori_loop(0, HALF // 8, advance, 0, unroll=7)

    def writes(z):
        lanes = pl.ds(pl.multiple_of(z * 256, 256), 256)
        return (
            pltpu.make_async_copy(out.at[:, :, lanes], out_h.at[:, :, lanes], sem.at[1 + z]),
            pltpu.make_async_copy(grad.at[:, lanes], grad_h.at[:, lanes], sem.at[1 + DZ + z]),
        )

    def pull(z, carry):
        rows = {c: place_of(z + c) * 5 for c in (-1, 0, 1)}
        for n in range(19):
            src = rows[-VEL[n][2]]
            t0 = adj[n, pl.ds(src, 8), :]
            t1 = adj[n, pl.ds(HALF + src, 8), :]
            g = ghost_a[n, pl.ds(src, 8), :] if VEL[n][0] else None
            t0, t1 = xyshift(t0, t1, VEL[n], g)
            back[n, pl.ds(z * 5, SLOTS), :] = t0[0:SLOTS]
            back[n, pl.ds(DZ * 5 + z * 5, SLOTS), :] = t1[0:SLOTS]
        for half in range(2):
            back[19, pl.ds(half * DZ * 5 + z * 5, SLOTS), :] = adj[19, pl.ds(half * HALF + rows[0], SLOTS), :]
        return carry

    def retreat(i, carry):
        for half in range(2):
            r = pl.ds(pl.multiple_of(half * DZ * 5 + i * 8, 8), 8)
            m = {name: mstore[j, r, :] for j, name in enumerate(M_NAMES)}
            v = mstore[19, r, :]
            listed = v > 0.5
            s = v - 1.0
            a, gs = adjoint(m, defects(m), s, [back[OPP[j], r, :] for j in range(19)])
            for j in range(19):
                a0[pl.ds(pl.multiple_of(j * ROWS_OWN + half * DZ * 5 + i * 8, 8), 8), :] = jnp.where(listed, a[j], 0.0)
            g0[r, :] = jnp.where(listed & (v < 1.75), gs + back[19, r, :], 0.0)
        return carry

    def send(z, carry):
        for half in range(2):
            lanes = pl.ds(pl.multiple_of(z * 256 + half * 128, 128), 128)
            base = half * DZ * 5 + z * 5
            for k in range(SLOTS):
                out[k, :, lanes] = a0[pl.ds(base + k, 19, stride=ROWS_OWN), :]
            grad[:, lanes] = g0[pl.ds(base, SLOTS), :]
        for c in writes(z):
            c.start()
        return carry

    lax.fori_loop(0, DZ, pull, 0, unroll=2)
    lax.fori_loop(0, DZ * 5 // 8, retreat, 0)
    lax.fori_loop(0, DZ, send, 0)

    def finish(z, carry):
        for c in writes(z):
            c.wait()
        return carry

    lax.fori_loop(0, DZ, finish, 0)


HBM = pl.BlockSpec(memory_space=pltpu.HBM)
VMEM = pl.BlockSpec(memory_space=pltpu.VMEM)


def exchange(inside, across, axis):
    rows, depth = lax.axis_size("blk"), lax.axis_size("gz")
    along_gz = axis == "gz"
    count = depth if along_gz else rows
    index = (lambda at, other: other * depth + at) if along_gz else (lambda at, other: at * depth + other)
    second = []
    for other in range(rows if along_gz else depth):
        for at in range(1, count - 1, 2):
            second += [(index(at, other), index(at + 1, other)), (index(at + 1, other), index(at, other))]
        second += [(index(at, other), index(at, other ^ 1)) for at in (0, count - 1)]
    first = [(i, i ^ 1) for i in range(count)]
    if inside is not None:
        inside = lax.ppermute(inside, axis, first)
    if across is not None:
        across = lax.ppermute(across, ("blk", "gz"), second)
    return inside, across


def at_end(axis):
    at = lax.axis_index(axis)
    return (at == 0) | (at == lax.axis_size(axis) - 1)


def per_device(populations, target, solid_frac, wall_mask, slot_column):
    f32 = jnp.float32
    populations = jnp.transpose(populations, (1, 0, 2))
    target = jnp.transpose(target, (1, 0, 2))
    populations, target, solid_frac, wall_mask, slot_column = (
        pltpu.with_memory_space_constraint(x, pltpu.HBM) for x in (populations, target, solid_frac, wall_mask, slot_column)
    )

    def params(mib):
        return pltpu.CompilerParams(vmem_limit_bytes=mib << 20)

    def inputs(cells):
        return [
            pltpu.SMEM((SLOTS,), jnp.int32),
            pltpu.VMEM((SLOTS, 19, cells), f32),
            pltpu.VMEM((SLOTS, 19, cells), jnp.bfloat16),
            pltpu.VMEM((SLOTS, cells), f32),
            pltpu.VMEM((SLOTS, cells), jnp.int32),
            pltpu.VMEM((cells // 128, 8 * SLOT_ROWS, 128), f32),
            pltpu.VMEM((cells // 128, 8 * SLOT_ROWS, 128), f32),
            pltpu.VMEM((8, cells), f32),
            pltpu.SemaphoreType.DMA((9,)),
        ]

    slots_in = [pltpu.SMEM((SLOTS,), jnp.int32)]
    zbuf = jax.ShapeDtypeStruct((ZROWS, 256), f32)
    inside, across = pl.pallas_call(
        border_kernel,
        in_specs=[HBM] * 5,
        out_specs=[VMEM] * 2,
        out_shape=[zbuf, zbuf],
        scratch_shapes=inputs(1024),
        compiler_params=params(8),
    )(slot_column, populations, target, solid_frac, wall_mask)
    r_inside, r_across = exchange(inside, across, "gz")
    store_t = jax.ShapeDtypeStruct((NF, ROWS_STORE, 128), f32)
    vstore_t = jax.ShapeDtypeStruct((ROWS_STORE, 128), f32)
    xbuf = jax.ShapeDtypeStruct((XROWS, 128), f32)
    moved_t = jax.ShapeDtypeStruct((NF, ROWS_COMPACT, 128), f32)
    store, vstore, mstore, moved, inside, across = pl.pallas_call(
        fields_kernel,
        in_specs=[HBM] * 5,
        out_specs=[VMEM] * 6,
        out_shape=[store_t, vstore_t, jax.ShapeDtypeStruct((20, ROWS_OWN, 128), f32), moved_t, xbuf, xbuf],
        scratch_shapes=inputs(CELLS),
        compiler_params=params(12),
    )(slot_column, populations, target, solid_frac, wall_mask)
    store, vstore, inside, across = pl.pallas_call(
        side_kernel,
        in_specs=[HBM] + [VMEM] * 6,
        out_specs=[VMEM] * 4,
        out_shape=[store_t, vstore_t, xbuf, xbuf],
        input_output_aliases={1: 0, 2: 1, 3: 2, 4: 3},
        scratch_shapes=slots_in + [pltpu.SemaphoreType.DMA((1,))],
        compiler_params=params(12),
    )(slot_column, store, vstore, inside, across, r_inside, r_across)
    r_inside, r_across = exchange(inside, across, "blk")
    moved, vmoved = pl.pallas_call(
        shift_kernel,
        in_specs=[HBM, VMEM, VMEM, VMEM],
        out_specs=[VMEM, VMEM],
        out_shape=[moved_t, jax.ShapeDtypeStruct((ROWS_COMPACT, 128), f32)],
        input_output_aliases={3: 0},
        scratch_shapes=slots_in + [pltpu.SemaphoreType.DMA((1,))],
        compiler_params=params(12),
    )(slot_column, store, vstore, moved)
    grad, adjoint_out = pl.pallas_call(
        final_kernel,
        in_specs=[HBM] + [VMEM] * 7,
        out_specs=[HBM, HBM],
        out_shape=[
            jax.ShapeDtypeStruct((SLOTS, CELLS), f32),
            jax.ShapeDtypeStruct((SLOTS, 19, CELLS), f32),
        ],
        scratch_shapes=slots_in + [
            pltpu.VMEM((NF, HALF, 128), f32),
            pltpu.VMEM((19, HALF, 128), f32),
            pltpu.VMEM((20, ROWS_COMPACT, 128), f32),
            pltpu.VMEM((20, ROWS_OWN, 128), f32),
            pltpu.VMEM((19 * ROWS_OWN, 128), f32),
            pltpu.VMEM((ROWS_OWN, 128), f32),
            pltpu.VMEM((SLOTS, CELLS), f32),
            pltpu.VMEM((SLOTS, 19, CELLS), f32),
            pltpu.SemaphoreType.DMA((1 + 2 * DZ,)),
        ],
        compiler_params=params(20),
    )(slot_column, moved, vmoved, mstore, inside, across, r_inside, r_across)
    return grad, jnp.transpose(adjoint_out, (1, 0, 2))


def solution(mesh):
    return jax.shard_map(
        per_device,
        mesh=mesh,
        in_specs=(
            P(None, "blk", "gz"),
            P(None, "blk", "gz"),
            P("blk", "gz"),
            P("blk", "gz"),
            P("blk"),
        ),
        out_specs=(P("blk", "gz"), P(None, "blk", "gz")),
        check_vma=False,
    )
```

```python
import jax
import jax.numpy as jnp
from jax import lax
from jax.experimental import pallas as pl
from jax.experimental.pallas import tpu as pltpu
from jax.sharding import PartitionSpec as P

EDGE = 16
GY = 8
SLOTS = 5
DZ = 8
CELLS = DZ * EDGE * EDGE

VEL = (
    (0, 0, 0),
    (1, 0, 0), (-1, 0, 0), (0, 1, 0), (0, -1, 0), (0, 0, 1), (0, 0, -1),
    (1, 1, 0), (-1, -1, 0), (1, -1, 0), (-1, 1, 0),
    (1, 0, 1), (-1, 0, -1), (1, 0, -1), (-1, 0, 1),
    (0, 1, 1), (0, -1, -1), (0, 1, -1), (0, -1, 1),
)
OPP = (0, 2, 1, 4, 3, 6, 5, 8, 7, 10, 9, 12, 11, 14, 13, 16, 15, 18, 17)
T_SCALE = (3.0,) + (9.0,) * 18

NF = 38
ZI = 10
ROWS_STORE = ZI * 16
HALF = 56
ROWS_COMPACT = 2 * HALF
ROWS_OWN = 2 * DZ * 5
EDGE_LAYERS = 4


def place(zd):
    return {-1: 0, 0: 1, DZ - 1: 2, DZ: 3}.get(zd, zd + 3)


def place_of(zd):
    return jnp.where(zd < 1, zd + 1, jnp.where(zd > DZ - 2, zd - DZ + 3, zd + 3))


def vel(n):
    return VEL[n % 19]


def mirror(n, dim):
    v = list(vel(n))
    v[dim] = -v[dim]
    return n // 19 * 19 + VEL.index(tuple(v))


def planes(dim):
    out = []
    for n in range(NF):
        c = vel(n)[dim]
        if c == 0:
            out.append((n, True, True))
        elif c == 1:
            out.append((n, False, True))
            out.append((n, True, False))
    return out


ZP, XP = planes(2), planes(0)
NP = len(ZP)
ZROWS = 200
XROWS = 400
SLOT_ROWS = 24


def moments(f):
    m = {}

    def pair(a):
        return f[a] + f[a + 1], f[a] - f[a + 1]

    sx, dx = pair(1)
    sy, dy = pair(3)
    sz, dz = pair(5)
    for name, a, t1, t2 in (("xy", 7, "xyy", "xxy"), ("xz", 11, "xzz", "xxz"), ("yz", 15, "yzz", "yyz")):
        sa, da = pair(a)
        sb, db = pair(a + 2)
        m["Q" + name] = sa + sb
        m["P" + name] = sa - sb
        m["T" + t1] = da + db
        m["T" + t2] = da - db
    qa = m["Qxy"] + m["Qxz"]
    m["Pxx"] = sx + qa
    m["Pyy"] = sy + (m["Qxy"] + m["Qyz"])
    m["Pzz"] = sz + (m["Qxz"] + m["Qyz"])
    m["rho"] = (f[0] + sx) + (sy + sz) + (qa + m["Qyz"])
    m["jx"] = dx + (m["Txyy"] + m["Txzz"])
    m["jy"] = dy + (m["Txxy"] + m["Tyzz"])
    m["jz"] = dz + (m["Txxz"] + m["Tyyz"])
    return m


def defects(m):
    ux, uy, uz = m["jx"], m["jy"], m["jz"]
    xx, yy, zz = ux * ux, uy * uy, uz * uz
    third = m["rho"] * (1.0 / 3.0)
    ninth = m["rho"] * (1.0 / 9.0) - (xx + yy + zz) * (1.0 / 6.0)
    d = {}
    d["Pxx"] = third + xx - m["Pxx"]
    d["Pyy"] = third + yy - m["Pyy"]
    d["Pzz"] = third + zz - m["Pzz"]
    d["Pxy"] = ux * uy - m["Pxy"]
    d["Pxz"] = ux * uz - m["Pxz"]
    d["Pyz"] = uy * uz - m["Pyz"]
    d["Qxy"] = ninth + (xx + yy) * 0.5 - m["Qxy"]
    d["Qxz"] = ninth + (xx + zz) * 0.5 - m["Qxz"]
    d["Qyz"] = ninth + (yy + zz) * 0.5 - m["Qyz"]
    return d


P_NAMES = ("Pxx", "Pyy", "Pzz", "Pxy", "Pxz", "Pyz")
Q_NAMES = ("Qxy", "Qxz", "Qyz")
M_NAMES = ("rho", "jx", "jy", "jz") + P_NAMES + Q_NAMES + ("Txyy", "Txzz", "Txxy", "Tyzz", "Txxz", "Tyyz")
T_OF = {"x": ("Txyy", "Txzz"), "y": ("Txxy", "Tyzz"), "z": ("Txxz", "Tyyz")}


def collide(m, d, s, scaled=False):
    two, four, shift = (4.5, 2.25, 18.0) if scaled else (0.5, 0.25, None)
    h = 1.0 - s
    h16 = 1.6 * h
    t_keep = 0.8 * h - 1.0
    h04 = 0.4 * h
    j_keep = h - s
    o = {}
    for name in P_NAMES:
        o[name] = m[name] + h16 * d[name]
    for name in Q_NAMES:
        o[name] = m[name] + h * d[name]
    for axis in "xyz":
        j = m["j" + axis]
        o["j" + axis] = j_keep * j
        hj = h04 * j
        for name in T_OF[axis]:
            o[name] = t_keep * m[name] + hj
    f = [None] * 19
    qs = (o["Qxy"] + o["Qxz"]) + o["Qyz"]
    f[0] = (m["rho"] + qs) - ((o["Pxx"] + o["Pyy"]) + o["Pzz"])
    if scaled:
        f[0] = 3.0 * f[0] + 6.0
    for a, p, q1, q2, axis in ((1, "Pxx", "Qxy", "Qxz", "x"), (3, "Pyy", "Qxy", "Qyz", "y"), (5, "Pzz", "Qxz", "Qyz", "z")):
        s_ = (o[p] - (o[q1] + o[q2])) * two
        if scaled:
            s_ = s_ + shift
        d_ = (o["j" + axis] - (o[T_OF[axis][0]] + o[T_OF[axis][1]])) * two
        f[a] = s_ + d_
        f[a + 1] = s_ - d_
    for name, a, t1, t2 in (("xy", 7, "Txyy", "Txxy"), ("xz", 11, "Txzz", "Txxz"), ("yz", 15, "Tyzz", "Tyyz")):
        q = o["Q" + name] * four
        if scaled:
            q = q + shift
        p = o["P" + name] * four
        u = o[t1] * four
        w = o[t2] * four
        sa, sb, da, db = q + p, q - p, u + w, u - w
        f[a] = sa + da
        f[a + 1] = sa - da
        f[a + 2] = sb + db
        f[a + 3] = sb - db
    return f


def adjoint(m, d, s, q, scaled=False):
    by_two = (lambda x: x) if scaled else (lambda x: x * 0.5)
    by_four = (lambda x: x) if scaled else (lambda x: x * 0.25)
    h = 1.0 - s
    h16 = 1.6 * h
    t_keep = 0.8 * h - 1.0
    h04 = 0.4 * h
    j_keep = h - s
    t = {}
    half = {}
    for axis, a in (("x", 1), ("y", 3), ("z", 5)):
        half[axis] = by_two(q[a] + q[a + 1])
        t["j" + axis] = by_two(q[a] - q[a + 1])
        t["P" + axis + axis] = half[axis] - q[0]
    for name, a, t1, t2 in (("xy", 7, "Txyy", "Txxy"), ("xz", 11, "Txzz", "Txxz"), ("yz", 15, "Tyzz", "Tyyz")):
        sa, da = q[a] + q[a + 1], q[a] - q[a + 1]
        sb, db = q[a + 2] + q[a + 3], q[a + 2] - q[a + 3]
        t["Q" + name] = by_four(sa + sb) - half[name[0]] - t["P" + name[1] * 2]
        t["P" + name] = by_four(sa - sb)
        t[t1] = by_four(da + db) - t["j" + name[0]]
        t[t2] = by_four(da - db) - t["j" + name[1]]
    gp = t["Pxx"] * d["Pxx"]
    for name in P_NAMES[1:]:
        gp = gp + t[name] * d[name]
    gq = t["Qxy"] * d["Qxy"] + t["Qxz"] * d["Qxz"] + t["Qyz"] * d["Qyz"]
    gt = None
    gj = None
    tsum = {}
    for axis in "xyz":
        tsum[axis] = t[T_OF[axis][0]] + t[T_OF[axis][1]]
        term = t[T_OF[axis][0]] * m[T_OF[axis][0]] + t[T_OF[axis][1]] * m[T_OF[axis][1]]
        gt = term if gt is None else gt + term
        term = (2.0 * t["j" + axis] + 0.4 * tsum[axis]) * m["j" + axis]
        gj = term if gj is None else gj + term
    gs = -(1.6 * gp + gq + gj + 0.8 * gt)
    ux, uy, uz = m["jx"], m["jy"], m["jz"]
    p_keep = 1.0 - h16
    qsum = t["Qxy"] + t["Qxz"] + t["Qyz"]
    u = {}
    u["rho"] = q[0] + (h16 * (1.0 / 3.0)) * (t["Pxx"] + t["Pyy"] + t["Pzz"]) + (h * (1.0 / 9.0)) * qsum
    third = qsum * (1.0 / 3.0)
    w16 = {"x": t["Pxy"] * uy + t["Pxz"] * uz, "y": t["Pxy"] * ux + t["Pyz"] * uz, "z": t["Pxz"] * ux + t["Pyz"] * uy}
    other = {"x": "Qyz", "y": "Qxz", "z": "Qxy"}
    for axis, uu in (("x", ux), ("y", uy), ("z", uz)):
        quad = 2.0 * third - t[other[axis]]
        u["j" + axis] = (
            j_keep * t["j" + axis]
            + h04 * tsum[axis]
            + h16 * (w16[axis] + 2.0 * t["P" + axis + axis] * uu)
            + h * (quad * uu)
        )
    for name in P_NAMES:
        u[name] = p_keep * t[name]
    for name in Q_NAMES:
        u[name] = s * t[name]
    for axis in "xyz":
        for name in T_OF[axis]:
            u[name] = t_keep * t[name]
    a_ = [None] * 19
    a_[0] = u["rho"]
    for axis, a in (("x", 1), ("y", 3), ("z", 5)):
        e = u["rho"] + u["P" + axis + axis]
        a_[a] = e + u["j" + axis]
        a_[a + 1] = e - u["j" + axis]
    for name, a, t1, t2 in (("xy", 7, "Txyy", "Txxy"), ("xz", 11, "Txzz", "Txxz"), ("yz", 15, "Tyzz", "Tyyz")):
        e = u["rho"] + u["P" + name[0] * 2] + u["P" + name[1] * 2] + u["Q" + name]
        ea, eb = e + u["P" + name], e - u["P" + name]
        o1, o2 = u["j" + name[0]] + u[t1], u["j" + name[1]] + u[t2]
        oa, ob = o1 + o2, o1 - o2
        a_[a] = ea + oa
        a_[a + 1] = ea - oa
        a_[a + 2] = eb + ob
        a_[a + 3] = eb - ob
    return a_, gs


def misfit(c, arrived):
    return [jnp.where(arrived[OPP[i]] > 1.0, c[i] - arrived[OPP[i]], 0.0) for i in range(19)]


def iota(shape, dim):
    return lax.broadcasted_iota(jnp.int32, shape, dim)


def columns(slots, shape):
    row = iota(shape, 0)
    col = jnp.full(shape, -1, jnp.int32)
    for k in range(SLOTS):
        col = jnp.where(row == k, slots[k], col)
    return col


def load_all(copies):
    for c in copies:
        c.start()
    for c in copies:
        c.wait()


def unpack(f_raw, t_raw, s_raw, w_raw, f_rows, t_rows, frac, tiles):
    for t in range(tiles):
        lanes = pl.ds(t * 128, 128)
        for k in range(SLOTS):
            f_rows[t, pl.ds(k * SLOT_ROWS, 19), :] = f_raw[k, :, lanes]
            t_rows[t, pl.ds(k * SLOT_ROWS, 19), :] = t_raw[k, :, lanes].astype(jnp.float32)
        frac[pl.ds(0, SLOTS), lanes] = jnp.where(w_raw[:, lanes] == 1, 1.0, s_raw[:, lanes])


def fields_of(f_rows, t_rows, frac, valid, tile):
    f = [f_rows[tile, pl.ds(i, 8, stride=SLOT_ROWS), :] for i in range(19)]
    s = frac[:, pl.ds(pl.multiple_of(tile * 128, 128), 128)]
    m = moments(f)
    c = collide(m, defects(m), s)
    out = [jnp.where(valid, c[i], 0.0) for i in range(19)]
    for i in range(19):
        t = t_rows[tile, pl.ds(OPP[i], 8, stride=SLOT_ROWS), :]
        out.append(jnp.where(valid, T_SCALE[i] * t + 2.0 * T_SCALE[i], 0.0))
    return out, jnp.where(valid, s + 1.0, 0.0), m


def even(axis):
    return lax.rem(lax.axis_index(axis), 2) == 0


def border_kernel(slots_h, f_h, t_h, s_h, w_h, inside, across, slots, f_raw, t_raw, s_raw, w_raw, f_rows, t_rows, frac, sem):
    copies = [pltpu.make_async_copy(slots_h, slots, sem.at[0])]
    for e, lane in enumerate((0, CELLS - 512)):
        src, dst = pl.ds(lane, 512), pl.ds(e * 512, 512)
        copies += [
            pltpu.make_async_copy(f_h.at[:, :, src], f_raw.at[:, :, dst], sem.at[1 + e]),
            pltpu.make_async_copy(t_h.at[:, :, src], t_raw.at[:, :, dst], sem.at[3 + e]),
            pltpu.make_async_copy(s_h.at[:, src], s_raw.at[:, dst], sem.at[5 + e]),
            pltpu.make_async_copy(w_h.at[:, src], w_raw.at[:, dst], sem.at[7 + e]),
        ]
    load_all(copies)
    unpack(f_raw, t_raw, s_raw, w_raw, f_rows, t_rows, frac, 8)
    valid = columns(slots, (8, 128)) >= 0
    even_z = even("gz")
    for out, goes_up in ((inside, even_z), (across, jnp.logical_not(even_z))):
        for outer in (True, False):
            layer = jnp.where(goes_up, 3, 0) if outer else jnp.where(goes_up, 2, 1)
            for half in range(2):
                dst = pl.ds(half * 128, 128)
                fields, v, _ = fields_of(f_rows, t_rows, frac, valid, layer * 2 + half)
                for p, (n, src, _) in enumerate(ZP):
                    if src == outer:
                        m = mirror(n, 2)
                        val = fields[n] if m == n else jnp.where(goes_up, fields[n], fields[m])
                        out[pl.ds(p * SLOTS, SLOTS), dst] = val[0:SLOTS]
                if outer:
                    out[pl.ds(NP * SLOTS, SLOTS), dst] = v[0:SLOTS]


def fields_kernel(slots_h, f_h, t_h, s_h, w_h, store, vstore, mstore, moved, inside, across, slots, f_raw, t_raw, s_raw, w_raw, f_rows, t_rows, frac, sem):
    load_all([
        pltpu.make_async_copy(slots_h, slots, sem.at[0]),
        pltpu.make_async_copy(f_h, f_raw, sem.at[1]),
        pltpu.make_async_copy(t_h, t_raw, sem.at[2]),
        pltpu.make_async_copy(s_h, s_raw, sem.at[3]),
        pltpu.make_async_copy(w_h, w_raw, sem.at[4]),
    ])
    unpack(f_raw, t_raw, s_raw, w_raw, f_rows, t_rows, frac, 16)
    valid = columns(slots, (8, 128)) >= 0

    def body(z, carry):
        rows = {c: pl.multiple_of(place_of(z + c) * 16, 16) for c in (-1, 0, 1)}
        for half in range(2):
            fields, v, m = fields_of(f_rows, t_rows, frac, valid, z * 2 + half)
            for n in range(NF):
                store[n, pl.ds(rows[vel(n)[2]] + half * 8, 8), :] = fields[n]
            vstore[pl.ds(rows[0] + half * 8, 8), :] = v
            own = pl.ds(half * DZ * 5 + z * 5, SLOTS)
            for i, name in enumerate(M_NAMES):
                mstore[i, own, :] = m[name][0:SLOTS]
            mstore[19, own, :] = v[0:SLOTS]
        return carry

    lax.fori_loop(0, DZ, body, 0)
    side_planes(slots, store, vstore, inside, across, EDGE_LAYERS, ZI)
    shift_layers(slots, store, moved, EDGE_LAYERS, ZI)


def side_planes(slots, store, vstore, inside, across, first, last):
    count = last - first
    group = iota((count, 128), 1) // EDGE
    masks = [group == slots[k] for k in range(SLOTS)]
    even_x = even("blk")
    for out, right in ((inside, even_x), (across, jnp.logical_not(even_x))):
        if out is None:
            continue
        half = jnp.where(right, 1, 0)
        outer_x, inner_x = jnp.where(right, 7, 0), jnp.where(right, 6, 1)
        shifts = {
            outer: [lax.rem((slots[k] - (outer_x if outer else inner_x) + 16) * EDGE, 128) for k in range(SLOTS)]
            for outer in (True, False)
        }
        for p, (n, outer, _) in enumerate(XP + [(None, True, None)]):
            if n is not None:
                m = mirror(n, 0)
                field = n if m == n else jnp.where(right, n, m)
            acc = jnp.zeros((count, 128), jnp.float32)
            for k in range(SLOTS):
                rows = pl.ds(first * 16 + half * 8 + k, count, stride=16)
                v = vstore[rows, :] if n is None else store[field, rows, :]
                acc = jnp.where(masks[k], pltpu.roll(v, shifts[outer][k], 1), acc)
            out[pl.ds(p * ZI + first, count), :] = acc


def side_kernel(slots_h, store_in, vstore_in, across_in, r_inside, r_across, store, vstore, across, slots, sem):
    del store_in, vstore_in, across_in
    fetch = pltpu.make_async_copy(slots_h, slots, sem.at[0])
    fetch.start()
    even_z, alone = even("gz"), at_end("gz")
    for r, below in ((r_inside, jnp.logical_not(even_z)), (r_across, even_z)):
        ghost = jnp.where(below, place(-1), place(DZ)) * 16
        first = jnp.where(below, place(0), place(DZ - 1)) * 16
        for half in range(2):
            src = pl.ds(half * 128, 128)
            for p, (n, _, is_ghost) in enumerate(ZP):
                m = mirror(n, 2)
                field = n if m == n else jnp.where(below, n, m)
                row = ghost if is_ghost else first
                t = r[pl.ds(p * SLOTS, SLOTS), src]
                if r is r_across and not is_ghost:
                    t = jnp.where(alone, 0.0, t)
                store[field, pl.ds(row + half * 8, SLOTS), :] = t
            t = r[pl.ds(NP * SLOTS, SLOTS), src]
            if r is r_across:
                t = jnp.where(alone, 0.0, t)
            vstore[pl.ds(ghost + half * 8, SLOTS), :] = t
    fetch.wait()
    side_planes(slots, store, vstore, None, across, 0, EDGE_LAYERS)


def shifter(slots):
    lane = iota((8, 128), 1)
    y = lax.rem(lane, EDGE)
    row = iota((8, 128), 0)
    col = columns(slots, (8, 128))
    prev = pltpu.roll(col, 1, 0)
    nxt = pltpu.roll(col, 7, 0)
    edge = {1: y == 0, -1: y == EDGE - 1}
    conn = {
        1: edge[1] & (row >= 1) & (col >= 0) & (prev == col - 1),
        -1: edge[-1] & (row < SLOTS - 1) & (nxt >= 0) & (nxt == col + 1),
    }
    low, high = lane < EDGE, lane >= 128 - EDGE

    def yshift(t, cy):
        if cy == 0:
            return t
        a = pltpu.roll(t, cy % 128, 1)
        b = pltpu.roll(pltpu.roll(t, (-15 * cy) % 128, 1), cy % 8, 0)
        return jnp.where(conn[cy], b, jnp.where(edge[cy], 0.0, a))

    def xyshift(t0, t1, v, ghost):
        t0, t1 = yshift(t0, v[1]), yshift(t1, v[1])
        if v[0] == 1:
            r0, r1 = pltpu.roll(t0, EDGE, 1), pltpu.roll(t1, EDGE, 1)
            return jnp.where(low, ghost, r0), jnp.where(low, r0, r1)
        if v[0] == -1:
            r0, r1 = pltpu.roll(t0, 128 - EDGE, 1), pltpu.roll(t1, 128 - EDGE, 1)
            return jnp.where(high, r1, r0), jnp.where(high, ghost, r1)
        return t0, t1

    return xyshift, low, high


def shift_layers(slots, store, moved, first, last):
    xyshift = shifter(slots)[0]

    def body(at, carry):
        r0, r1 = pl.multiple_of(at * 16, 8), pl.multiple_of(at * 16 + 8, 8)
        for n in range(NF):
            t0, t1 = xyshift(store[n, pl.ds(r0, 8), :], store[n, pl.ds(r1, 8), :], vel(n), 0.0)
            moved[n, pl.ds(at * 5, SLOTS), :] = t0[0:SLOTS]
            moved[n, pl.ds(HALF + at * 5, SLOTS), :] = t1[0:SLOTS]
        return carry

    lax.fori_loop(first, last, body, 0)


def shift_kernel(slots_h, store, vstore, moved_in, inside_in, moved, vmoved, inside, slots, sem):
    del moved_in, inside_in
    fetch = pltpu.make_async_copy(slots_h, slots, sem.at[0])
    fetch.start()
    for at in range(ZI):
        for half in range(2):
            vmoved[pl.ds(half * HALF + at * 5, SLOTS), :] = vstore[pl.ds(at * 16 + half * 8, SLOTS), :]
    fetch.wait()
    side_planes(slots, store, vstore, inside, None, 0, EDGE_LAYERS)
    shift_layers(slots, store, moved, 0, EDGE_LAYERS)


def final_kernel(slots_h, moved, vmoved, mstore, inside, across, r_inside, r_across, grad_h, out_h,
                 slots, gx, ghost_a, adj, back, a0, g0, grad, out, sem):
    fetch = pltpu.make_async_copy(slots_h, slots, sem.at[0])
    fetch.start()
    lane16 = iota((16, 128), 1)
    first, last = lane16 == 0, lane16 == 127

    def yshift_dense(t, cy):
        if cy == 0:
            return t
        a = pltpu.roll(t, cy % 128, 1)
        return jnp.where(first if cy == 1 else last, 0.0, a)

    def to_packed(t, dst, n, xl):
        for k in range(SLOTS):
            shift = lax.rem((xl - slots[k] + 16) * EDGE, 128)
            r = pltpu.roll(t, shift, 1)
            dst[n, pl.ds(k, 8, stride=5), :] = r[0:8]
            dst[n, pl.ds(40 + k, ZI - 8, stride=5), :] = r[8:ZI]

    even_x, alone = even("blk"), at_end("blk")
    for c_in, xl in ((1, 0), (-1, 7)):
        from_inside = jnp.logical_not(even_x) if c_in == 1 else even_x
        ghost = [None] * NF
        packs = []
        for p, (n, _, is_ghost) in enumerate(XP + [(None, None, True)]):
            rows = pl.ds(p * ZI, 16)
            t = jnp.where(from_inside, r_inside[rows, :], r_across[rows, :])
            if n is None or not is_ghost:
                t = jnp.where(alone & jnp.logical_not(from_inside), 0.0, t)
            if n is None:
                v = t
                continue
            m = n if c_in == 1 else mirror(n, 0)
            if is_ghost:
                ghost[m] = t
            else:
                packs.append((yshift_dense(t, vel(m)[1]), gx, m))
                own = jnp.where(from_inside, inside[rows, :], across[rows, :])
                ghost[mirror(m, 0)] = own
        ghost = [yshift_dense(ghost[n], vel(n)[1]) for n in range(NF)]
        m = moments(ghost[:19])
        d = defects(m)
        s = v - 1.0
        a, _ = adjoint(m, d, s, misfit(collide(m, d, s, True), ghost[19:]), True)
        for n in range(19):
            if VEL[n][0] == c_in:
                t = jnp.where(v > 0.5, a[OPP[n]], 0.0)
                packs.append((yshift_dense(t, VEL[n][1]), ghost_a, n))
        if c_in == 1:
            fetch.wait()
        for t, dst, n in packs:
            to_packed(t, dst, n, xl)

    xyshift, low, high = shifter(slots)

    def advance(i, carry):
        for half in range(2):
            r = pl.ds(pl.multiple_of(half * HALF + i * 8, 8), 8)
            f = []
            for n in range(NF):
                t = moved[n, r, :]
                if vel(n)[0] == 1 - 2 * half:
                    g = gx[n, pl.ds(pl.multiple_of(i * 8, 8), 8), :]
                    t = jnp.where(high if half else low, g, t)
                f.append(t)
            v = vmoved[r, :]
            s = v - 1.0
            m = moments(f[:19])
            d = defects(m)
            a, gs = adjoint(m, d, s, misfit(collide(m, d, s, True), f[19:]), True)
            listed = v > 0.5
            for n in range(19):
                adj[n, r, :] = jnp.where(listed, a[OPP[n]], 0.0)
            adj[19, r, :] = gs
        return carry

    lax.fori_loop(0, HALF // 8, advance, 0, unroll=7)

    def writes(z):
        lanes = pl.ds(pl.multiple_of(z * 256, 256), 256)
        return (
            pltpu.make_async_copy(out.at[:, :, lanes], out_h.at[:, :, lanes], sem.at[1 + z]),
            pltpu.make_async_copy(grad.at[:, lanes], grad_h.at[:, lanes], sem.at[1 + DZ + z]),
        )

    def pull(z, carry):
        rows = {c: place_of(z + c) * 5 for c in (-1, 0, 1)}
        for n in range(19):
            src = rows[-VEL[n][2]]
            t0 = adj[n, pl.ds(src, 8), :]
            t1 = adj[n, pl.ds(HALF + src, 8), :]
            g = ghost_a[n, pl.ds(src, 8), :] if VEL[n][0] else None
            t0, t1 = xyshift(t0, t1, VEL[n], g)
            back[n, pl.ds(z * 5, SLOTS), :] = t0[0:SLOTS]
            back[n, pl.ds(DZ * 5 + z * 5, SLOTS), :] = t1[0:SLOTS]
        for half in range(2):
            back[19, pl.ds(half * DZ * 5 + z * 5, SLOTS), :] = adj[19, pl.ds(half * HALF + rows[0], SLOTS), :]
        return carry

    def retreat(i, carry):
        for half in range(2):
            r = pl.ds(pl.multiple_of(half * DZ * 5 + i * 8, 8), 8)
            m = {name: mstore[j, r, :] for j, name in enumerate(M_NAMES)}
            v = mstore[19, r, :]
            listed = v > 0.5
            s = v - 1.0
            a, gs = adjoint(m, defects(m), s, [back[OPP[j], r, :] for j in range(19)])
            for j in range(19):
                a0[pl.ds(pl.multiple_of(j * ROWS_OWN + half * DZ * 5 + i * 8, 8), 8), :] = jnp.where(listed, a[j], 0.0)
            g0[r, :] = jnp.where(listed & (v < 1.75), gs + back[19, r, :], 0.0)
        return carry

    def send(z, carry):
        for half in range(2):
            lanes = pl.ds(pl.multiple_of(z * 256 + half * 128, 128), 128)
            base = half * DZ * 5 + z * 5
            for k in range(SLOTS):
                out[k, :, lanes] = a0[pl.ds(base + k, 19, stride=ROWS_OWN), :]
            grad[:, lanes] = g0[pl.ds(base, SLOTS), :]
        for c in writes(z):
            c.start()
        return carry

    lax.fori_loop(0, DZ, pull, 0, unroll=2)
    lax.fori_loop(0, DZ * 5 // 8, retreat, 0)
    lax.fori_loop(0, DZ, send, 0)

    def finish(z, carry):
        for c in writes(z):
            c.wait()
        return carry

    lax.fori_loop(0, DZ, finish, 0)


HBM = pl.BlockSpec(memory_space=pltpu.HBM)
VMEM = pl.BlockSpec(memory_space=pltpu.VMEM)


def exchange(inside, across, axis):
    rows, depth = lax.axis_size("blk"), lax.axis_size("gz")
    along_gz = axis == "gz"
    count = depth if along_gz else rows
    index = (lambda at, other: other * depth + at) if along_gz else (lambda at, other: at * depth + other)
    second = []
    for other in range(rows if along_gz else depth):
        for at in range(1, count - 1, 2):
            second += [(index(at, other), index(at + 1, other)), (index(at + 1, other), index(at, other))]
        second += [(index(at, other), index(at, other ^ 1)) for at in (0, count - 1)]
    first = [(i, i ^ 1) for i in range(count)]
    if inside is not None:
        inside = lax.ppermute(inside, axis, first)
    if across is not None:
        across = lax.ppermute(across, ("blk", "gz"), second)
    return inside, across


def at_end(axis):
    at = lax.axis_index(axis)
    return (at == 0) | (at == lax.axis_size(axis) - 1)


def per_device(populations, target, solid_frac, wall_mask, slot_column):
    f32 = jnp.float32
    populations = jnp.transpose(populations, (1, 0, 2))
    target = jnp.transpose(target, (1, 0, 2))
    populations, target, solid_frac, wall_mask, slot_column = (
        pltpu.with_memory_space_constraint(x, pltpu.HBM) for x in (populations, target, solid_frac, wall_mask, slot_column)
    )

    def params(mib):
        return pltpu.CompilerParams(vmem_limit_bytes=mib << 20)

    def inputs(cells):
        return [
            pltpu.SMEM((SLOTS,), jnp.int32),
            pltpu.VMEM((SLOTS, 19, cells), f32),
            pltpu.VMEM((SLOTS, 19, cells), jnp.bfloat16),
            pltpu.VMEM((SLOTS, cells), f32),
            pltpu.VMEM((SLOTS, cells), jnp.int32),
            pltpu.VMEM((cells // 128, 8 * SLOT_ROWS, 128), f32),
            pltpu.VMEM((cells // 128, 8 * SLOT_ROWS, 128), f32),
            pltpu.VMEM((8, cells), f32),
            pltpu.SemaphoreType.DMA((9,)),
        ]

    slots_in = [pltpu.SMEM((SLOTS,), jnp.int32)]
    zbuf = jax.ShapeDtypeStruct((ZROWS, 256), f32)
    inside, across = pl.pallas_call(
        border_kernel,
        in_specs=[HBM] * 5,
        out_specs=[VMEM] * 2,
        out_shape=[zbuf, zbuf],
        scratch_shapes=inputs(1024),
        compiler_params=params(8),
    )(slot_column, populations, target, solid_frac, wall_mask)
    r_inside, r_across = exchange(inside, across, "gz")
    store_t = jax.ShapeDtypeStruct((NF, ROWS_STORE, 128), f32)
    vstore_t = jax.ShapeDtypeStruct((ROWS_STORE, 128), f32)
    xbuf = jax.ShapeDtypeStruct((XROWS, 128), f32)
    xbuf2 = jax.ShapeDtypeStruct((XROWS + 8, 128), f32)
    moved_t = jax.ShapeDtypeStruct((NF, ROWS_COMPACT, 128), f32)
    store, vstore, mstore, moved, inside, across = pl.pallas_call(
        fields_kernel,
        in_specs=[HBM] * 5,
        out_specs=[VMEM] * 6,
        out_shape=[store_t, vstore_t, jax.ShapeDtypeStruct((20, ROWS_OWN, 128), f32), moved_t, xbuf, xbuf2],
        scratch_shapes=inputs(CELLS),
        compiler_params=params(12),
    )(slot_column, populations, target, solid_frac, wall_mask)
    store, vstore, across = pl.pallas_call(
        side_kernel,
        in_specs=[HBM] + [VMEM] * 5,
        out_specs=[VMEM] * 3,
        out_shape=[store_t, vstore_t, xbuf2],
        input_output_aliases={1: 0, 2: 1, 3: 2},
        scratch_shapes=slots_in + [pltpu.SemaphoreType.DMA((1,))],
        compiler_params=params(12),
    )(slot_column, store, vstore, across, r_inside, r_across)
    _, r_across = exchange(None, across, "blk")
    moved, vmoved, inside = pl.pallas_call(
        shift_kernel,
        in_specs=[HBM] + [VMEM] * 4,
        out_specs=[VMEM] * 3,
        out_shape=[moved_t, jax.ShapeDtypeStruct((ROWS_COMPACT, 128), f32), xbuf],
        input_output_aliases={3: 0, 4: 2},
        scratch_shapes=slots_in + [pltpu.SemaphoreType.DMA((1,))],
        compiler_params=params(12),
    )(slot_column, store, vstore, moved, inside)
    r_inside, _ = exchange(inside, None, "blk")
    grad, adjoint_out = pl.pallas_call(
        final_kernel,
        in_specs=[HBM] + [VMEM] * 7,
        out_specs=[HBM, HBM],
        out_shape=[
            jax.ShapeDtypeStruct((SLOTS, CELLS), f32),
            jax.ShapeDtypeStruct((SLOTS, 19, CELLS), f32),
        ],
        scratch_shapes=slots_in + [
            pltpu.VMEM((NF, HALF, 128), f32),
            pltpu.VMEM((19, HALF, 128), f32),
            pltpu.VMEM((20, ROWS_COMPACT, 128), f32),
            pltpu.VMEM((20, ROWS_OWN, 128), f32),
            pltpu.VMEM((19 * ROWS_OWN, 128), f32),
            pltpu.VMEM((ROWS_OWN, 128), f32),
            pltpu.VMEM((SLOTS, CELLS), f32),
            pltpu.VMEM((SLOTS, 19, CELLS), f32),
            pltpu.SemaphoreType.DMA((1 + 2 * DZ,)),
        ],
        compiler_params=params(20),
    )(slot_column, moved, vmoved, mstore, inside, across, r_inside, r_across)
    return grad, jnp.transpose(adjoint_out, (1, 0, 2))


def solution(mesh):
    return jax.shard_map(
        per_device,
        mesh=mesh,
        in_specs=(
            P(None, "blk", "gz"),
            P(None, "blk", "gz"),
            P("blk", "gz"),
            P("blk", "gz"),
            P("blk"),
        ),
        out_specs=(P("blk", "gz"), P(None, "blk", "gz")),
        check_vma=False,
    )
```

```python
import jax
import jax.numpy as jnp
from jax import lax
from jax.experimental import pallas as pl
from jax.experimental.pallas import tpu as pltpu
from jax.sharding import PartitionSpec as P

EDGE = 16
GY = 8
SLOTS = 5
DZ = 8
CELLS = DZ * EDGE * EDGE

VEL = (
    (0, 0, 0),
    (1, 0, 0), (-1, 0, 0), (0, 1, 0), (0, -1, 0), (0, 0, 1), (0, 0, -1),
    (1, 1, 0), (-1, -1, 0), (1, -1, 0), (-1, 1, 0),
    (1, 0, 1), (-1, 0, -1), (1, 0, -1), (-1, 0, 1),
    (0, 1, 1), (0, -1, -1), (0, 1, -1), (0, -1, 1),
)
OPP = (0, 2, 1, 4, 3, 6, 5, 8, 7, 10, 9, 12, 11, 14, 13, 16, 15, 18, 17)
T_SCALE = (3.0,) + (9.0,) * 18

NF = 38
ZI = 10
ROWS_STORE = ZI * 16
HALF = 56
ROWS_COMPACT = 2 * HALF
ROWS_OWN = 2 * DZ * 5
EDGE_LAYERS = 4


def place(zd):
    return {-1: 0, 0: 1, DZ - 1: 2, DZ: 3}.get(zd, zd + 3)


def place_of(zd):
    return jnp.where(zd < 1, zd + 1, jnp.where(zd > DZ - 2, zd - DZ + 3, zd + 3))


def vel(n):
    return VEL[n % 19]


def mirror(n, dim):
    v = list(vel(n))
    v[dim] = -v[dim]
    return n // 19 * 19 + VEL.index(tuple(v))


def planes(dim):
    out = []
    for n in range(NF):
        c = vel(n)[dim]
        if c == 0:
            out.append((n, True, True))
        elif c == 1:
            out.append((n, False, True))
            out.append((n, True, False))
    return out


ZP, XP = planes(2), planes(0)
NP = len(ZP)
ZROWS = 200
XROWS = 400
SLOT_ROWS = 24


def moments(f):
    m = {}

    def pair(a):
        return f[a] + f[a + 1], f[a] - f[a + 1]

    sx, dx = pair(1)
    sy, dy = pair(3)
    sz, dz = pair(5)
    for name, a, t1, t2 in (("xy", 7, "xyy", "xxy"), ("xz", 11, "xzz", "xxz"), ("yz", 15, "yzz", "yyz")):
        sa, da = pair(a)
        sb, db = pair(a + 2)
        m["Q" + name] = sa + sb
        m["P" + name] = sa - sb
        m["T" + t1] = da + db
        m["T" + t2] = da - db
    qa = m["Qxy"] + m["Qxz"]
    m["Pxx"] = sx + qa
    m["Pyy"] = sy + (m["Qxy"] + m["Qyz"])
    m["Pzz"] = sz + (m["Qxz"] + m["Qyz"])
    m["rho"] = (f[0] + sx) + (sy + sz) + (qa + m["Qyz"])
    m["jx"] = dx + (m["Txyy"] + m["Txzz"])
    m["jy"] = dy + (m["Txxy"] + m["Tyzz"])
    m["jz"] = dz + (m["Txxz"] + m["Tyyz"])
    return m


def defects(m):
    ux, uy, uz = m["jx"], m["jy"], m["jz"]
    xx, yy, zz = ux * ux, uy * uy, uz * uz
    third = m["rho"] * (1.0 / 3.0)
    ninth = m["rho"] * (1.0 / 9.0) - (xx + yy + zz) * (1.0 / 6.0)
    d = {}
    d["Pxx"] = third + xx - m["Pxx"]
    d["Pyy"] = third + yy - m["Pyy"]
    d["Pzz"] = third + zz - m["Pzz"]
    d["Pxy"] = ux * uy - m["Pxy"]
    d["Pxz"] = ux * uz - m["Pxz"]
    d["Pyz"] = uy * uz - m["Pyz"]
    d["Qxy"] = ninth + (xx + yy) * 0.5 - m["Qxy"]
    d["Qxz"] = ninth + (xx + zz) * 0.5 - m["Qxz"]
    d["Qyz"] = ninth + (yy + zz) * 0.5 - m["Qyz"]
    return d


P_NAMES = ("Pxx", "Pyy", "Pzz", "Pxy", "Pxz", "Pyz")
Q_NAMES = ("Qxy", "Qxz", "Qyz")
M_NAMES = ("rho", "jx", "jy", "jz") + P_NAMES + Q_NAMES + ("Txyy", "Txzz", "Txxy", "Tyzz", "Txxz", "Tyyz")
T_OF = {"x": ("Txyy", "Txzz"), "y": ("Txxy", "Tyzz"), "z": ("Txxz", "Tyyz")}


def collide(m, d, s, scaled=False):
    two, four, shift = (4.5, 2.25, 18.0) if scaled else (0.5, 0.25, None)
    h = 1.0 - s
    h16 = 1.6 * h
    t_keep = 0.8 * h - 1.0
    h04 = 0.4 * h
    j_keep = h - s
    o = {}
    for name in P_NAMES:
        o[name] = m[name] + h16 * d[name]
    for name in Q_NAMES:
        o[name] = m[name] + h * d[name]
    for axis in "xyz":
        j = m["j" + axis]
        o["j" + axis] = j_keep * j
        hj = h04 * j
        for name in T_OF[axis]:
            o[name] = t_keep * m[name] + hj
    f = [None] * 19
    qs = (o["Qxy"] + o["Qxz"]) + o["Qyz"]
    f[0] = (m["rho"] + qs) - ((o["Pxx"] + o["Pyy"]) + o["Pzz"])
    if scaled:
        f[0] = 3.0 * f[0] + 6.0
    for a, p, q1, q2, axis in ((1, "Pxx", "Qxy", "Qxz", "x"), (3, "Pyy", "Qxy", "Qyz", "y"), (5, "Pzz", "Qxz", "Qyz", "z")):
        s_ = (o[p] - (o[q1] + o[q2])) * two
        if scaled:
            s_ = s_ + shift
        d_ = (o["j" + axis] - (o[T_OF[axis][0]] + o[T_OF[axis][1]])) * two
        f[a] = s_ + d_
        f[a + 1] = s_ - d_
    for name, a, t1, t2 in (("xy", 7, "Txyy", "Txxy"), ("xz", 11, "Txzz", "Txxz"), ("yz", 15, "Tyzz", "Tyyz")):
        q = o["Q" + name] * four
        if scaled:
            q = q + shift
        p = o["P" + name] * four
        u = o[t1] * four
        w = o[t2] * four
        sa, sb, da, db = q + p, q - p, u + w, u - w
        f[a] = sa + da
        f[a + 1] = sa - da
        f[a + 2] = sb + db
        f[a + 3] = sb - db
    return f


def adjoint(m, d, s, q, scaled=False):
    by_two = (lambda x: x) if scaled else (lambda x: x * 0.5)
    by_four = (lambda x: x) if scaled else (lambda x: x * 0.25)
    h = 1.0 - s
    h16 = 1.6 * h
    t_keep = 0.8 * h - 1.0
    h04 = 0.4 * h
    j_keep = h - s
    t = {}
    half = {}
    for axis, a in (("x", 1), ("y", 3), ("z", 5)):
        half[axis] = by_two(q[a] + q[a + 1])
        t["j" + axis] = by_two(q[a] - q[a + 1])
        t["P" + axis + axis] = half[axis] - q[0]
    for name, a, t1, t2 in (("xy", 7, "Txyy", "Txxy"), ("xz", 11, "Txzz", "Txxz"), ("yz", 15, "Tyzz", "Tyyz")):
        sa, da = q[a] + q[a + 1], q[a] - q[a + 1]
        sb, db = q[a + 2] + q[a + 3], q[a + 2] - q[a + 3]
        t["Q" + name] = by_four(sa + sb) - half[name[0]] - t["P" + name[1] * 2]
        t["P" + name] = by_four(sa - sb)
        t[t1] = by_four(da + db) - t["j" + name[0]]
        t[t2] = by_four(da - db) - t["j" + name[1]]
    gp = t["Pxx"] * d["Pxx"]
    for name in P_NAMES[1:]:
        gp = gp + t[name] * d[name]
    gq = t["Qxy"] * d["Qxy"] + t["Qxz"] * d["Qxz"] + t["Qyz"] * d["Qyz"]
    gt = None
    gj = None
    tsum = {}
    for axis in "xyz":
        tsum[axis] = t[T_OF[axis][0]] + t[T_OF[axis][1]]
        term = t[T_OF[axis][0]] * m[T_OF[axis][0]] + t[T_OF[axis][1]] * m[T_OF[axis][1]]
        gt = term if gt is None else gt + term
        term = (2.0 * t["j" + axis] + 0.4 * tsum[axis]) * m["j" + axis]
        gj = term if gj is None else gj + term
    gs = -(1.6 * gp + gq + gj + 0.8 * gt)
    ux, uy, uz = m["jx"], m["jy"], m["jz"]
    p_keep = 1.0 - h16
    qsum = t["Qxy"] + t["Qxz"] + t["Qyz"]
    u = {}
    u["rho"] = q[0] + (h16 * (1.0 / 3.0)) * (t["Pxx"] + t["Pyy"] + t["Pzz"]) + (h * (1.0 / 9.0)) * qsum
    third = qsum * (1.0 / 3.0)
    w16 = {"x": t["Pxy"] * uy + t["Pxz"] * uz, "y": t["Pxy"] * ux + t["Pyz"] * uz, "z": t["Pxz"] * ux + t["Pyz"] * uy}
    other = {"x": "Qyz", "y": "Qxz", "z": "Qxy"}
    for axis, uu in (("x", ux), ("y", uy), ("z", uz)):
        quad = 2.0 * third - t[other[axis]]
        u["j" + axis] = (
            j_keep * t["j" + axis]
            + h04 * tsum[axis]
            + h16 * (w16[axis] + 2.0 * t["P" + axis + axis] * uu)
            + h * (quad * uu)
        )
    for name in P_NAMES:
        u[name] = p_keep * t[name]
    for name in Q_NAMES:
        u[name] = s * t[name]
    for axis in "xyz":
        for name in T_OF[axis]:
            u[name] = t_keep * t[name]
    a_ = [None] * 19
    a_[0] = u["rho"]
    for axis, a in (("x", 1), ("y", 3), ("z", 5)):
        e = u["rho"] + u["P" + axis + axis]
        a_[a] = e + u["j" + axis]
        a_[a + 1] = e - u["j" + axis]
    for name, a, t1, t2 in (("xy", 7, "Txyy", "Txxy"), ("xz", 11, "Txzz", "Txxz"), ("yz", 15, "Tyzz", "Tyyz")):
        e = u["rho"] + u["P" + name[0] * 2] + u["P" + name[1] * 2] + u["Q" + name]
        ea, eb = e + u["P" + name], e - u["P" + name]
        o1, o2 = u["j" + name[0]] + u[t1], u["j" + name[1]] + u[t2]
        oa, ob = o1 + o2, o1 - o2
        a_[a] = ea + oa
        a_[a + 1] = ea - oa
        a_[a + 2] = eb + ob
        a_[a + 3] = eb - ob
    return a_, gs


def misfit(c, arrived):
    return [jnp.where(arrived[OPP[i]] > 1.0, c[i] - arrived[OPP[i]], 0.0) for i in range(19)]


def iota(shape, dim):
    return lax.broadcasted_iota(jnp.int32, shape, dim)


def columns(slots, shape):
    row = iota(shape, 0)
    col = jnp.full(shape, -1, jnp.int32)
    for k in range(SLOTS):
        col = jnp.where(row == k, slots[k], col)
    return col


def load_all(copies):
    for c in copies:
        c.start()
    for c in copies:
        c.wait()


def unpack(f_raw, t_raw, s_raw, w_raw, f_rows, t_rows, frac, tiles):
    for t in range(tiles):
        lanes = pl.ds(t * 128, 128)
        for k in range(SLOTS):
            f_rows[t, pl.ds(k * SLOT_ROWS, 19), :] = f_raw[k, :, lanes]
            t_rows[t, pl.ds(k * SLOT_ROWS, 19), :] = t_raw[k, :, lanes].astype(jnp.float32)
        frac[pl.ds(0, SLOTS), lanes] = jnp.where(w_raw[:, lanes] == 1, 1.0, s_raw[:, lanes])


def fields_of(f_rows, t_rows, frac, valid, tile):
    f = [f_rows[tile, pl.ds(i, 8, stride=SLOT_ROWS), :] for i in range(19)]
    s = frac[:, pl.ds(pl.multiple_of(tile * 128, 128), 128)]
    m = moments(f)
    c = collide(m, defects(m), s)
    out = [jnp.where(valid, c[i], 0.0) for i in range(19)]
    for i in range(19):
        t = t_rows[tile, pl.ds(OPP[i], 8, stride=SLOT_ROWS), :]
        out.append(jnp.where(valid, T_SCALE[i] * t + 2.0 * T_SCALE[i], 0.0))
    return out, jnp.where(valid, s + 1.0, 0.0), m


def even(axis):
    return lax.rem(lax.axis_index(axis), 2) == 0


def border_kernel(slots_h, f_h, t_h, s_h, w_h, inside, across, slots, f_raw, t_raw, s_raw, w_raw, f_rows, t_rows, frac, sem):
    copies = [pltpu.make_async_copy(slots_h, slots, sem.at[0])]
    for e, lane in enumerate((0, CELLS - 512)):
        src, dst = pl.ds(lane, 512), pl.ds(e * 512, 512)
        copies += [
            pltpu.make_async_copy(f_h.at[:, :, src], f_raw.at[:, :, dst], sem.at[1 + e]),
            pltpu.make_async_copy(t_h.at[:, :, src], t_raw.at[:, :, dst], sem.at[3 + e]),
            pltpu.make_async_copy(s_h.at[:, src], s_raw.at[:, dst], sem.at[5 + e]),
            pltpu.make_async_copy(w_h.at[:, src], w_raw.at[:, dst], sem.at[7 + e]),
        ]
    load_all(copies)
    unpack(f_raw, t_raw, s_raw, w_raw, f_rows, t_rows, frac, 8)
    valid = columns(slots, (8, 128)) >= 0
    even_z = even("gz")
    for out, goes_up in ((inside, even_z), (across, jnp.logical_not(even_z))):
        for outer in (True, False):
            layer = jnp.where(goes_up, 3, 0) if outer else jnp.where(goes_up, 2, 1)
            for half in range(2):
                dst = pl.ds(half * 128, 128)
                fields, v, _ = fields_of(f_rows, t_rows, frac, valid, layer * 2 + half)
                for p, (n, src, _) in enumerate(ZP):
                    if src == outer:
                        m = mirror(n, 2)
                        val = fields[n] if m == n else jnp.where(goes_up, fields[n], fields[m])
                        out[pl.ds(p * SLOTS, SLOTS), dst] = val[0:SLOTS]
                if outer:
                    out[pl.ds(NP * SLOTS, SLOTS), dst] = v[0:SLOTS]


def fields_kernel(slots_h, f_h, t_h, s_h, w_h, store, vstore, mstore, moved, inside, across, slots, f_raw, t_raw, s_raw, w_raw, f_rows, t_rows, frac, sem):
    load_all([
        pltpu.make_async_copy(slots_h, slots, sem.at[0]),
        pltpu.make_async_copy(f_h, f_raw, sem.at[1]),
        pltpu.make_async_copy(t_h, t_raw, sem.at[2]),
        pltpu.make_async_copy(s_h, s_raw, sem.at[3]),
        pltpu.make_async_copy(w_h, w_raw, sem.at[4]),
    ])
    unpack(f_raw, t_raw, s_raw, w_raw, f_rows, t_rows, frac, 16)
    valid = columns(slots, (8, 128)) >= 0

    def body(z, carry):
        rows = {c: pl.multiple_of(place_of(z + c) * 16, 16) for c in (-1, 0, 1)}
        for half in range(2):
            fields, v, m = fields_of(f_rows, t_rows, frac, valid, z * 2 + half)
            for n in range(NF):
                store[n, pl.ds(rows[vel(n)[2]] + half * 8, 8), :] = fields[n]
            vstore[pl.ds(rows[0] + half * 8, 8), :] = v
            own = pl.ds(half * DZ * 5 + z * 5, SLOTS)
            for i, name in enumerate(M_NAMES):
                mstore[i, own, :] = m[name][0:SLOTS]
            mstore[19, own, :] = v[0:SLOTS]
        return carry

    lax.fori_loop(0, DZ, body, 0)
    side_planes(slots, store, vstore, inside, across, EDGE_LAYERS, ZI)
    shift_layers(slots, store, moved, EDGE_LAYERS, ZI)


def side_planes(slots, store, vstore, inside, across, first, last):
    count = last - first
    group = iota((count, 128), 1) // EDGE
    masks = [group == slots[k] for k in range(SLOTS)]
    even_x = even("blk")
    for out, right in ((inside, even_x), (across, jnp.logical_not(even_x))):
        if out is None:
            continue
        half = jnp.where(right, 1, 0)
        outer_x, inner_x = jnp.where(right, 7, 0), jnp.where(right, 6, 1)
        shifts = {
            outer: [lax.rem((slots[k] - (outer_x if outer else inner_x) + 16) * EDGE, 128) for k in range(SLOTS)]
            for outer in (True, False)
        }
        for p, (n, outer, _) in enumerate(XP + [(None, True, None)]):
            if n is not None:
                m = mirror(n, 0)
                field = n if m == n else jnp.where(right, n, m)
            acc = jnp.zeros((count, 128), jnp.float32)
            for k in range(SLOTS):
                rows = pl.ds(first * 16 + half * 8 + k, count, stride=16)
                v = vstore[rows, :] if n is None else store[field, rows, :]
                acc = jnp.where(masks[k], pltpu.roll(v, shifts[outer][k], 1), acc)
            out[pl.ds(p * ZI + first, count), :] = acc


def side_kernel(slots_h, store_in, vstore_in, across_in, r_inside, r_across, store, vstore, across, slots, sem):
    del store_in, vstore_in, across_in
    fetch = pltpu.make_async_copy(slots_h, slots, sem.at[0])
    fetch.start()
    even_z, alone = even("gz"), at_end("gz")
    for r, below in ((r_inside, jnp.logical_not(even_z)), (r_across, even_z)):
        ghost = jnp.where(below, place(-1), place(DZ)) * 16
        first = jnp.where(below, place(0), place(DZ - 1)) * 16
        for half in range(2):
            src = pl.ds(half * 128, 128)
            for p, (n, _, is_ghost) in enumerate(ZP):
                m = mirror(n, 2)
                field = n if m == n else jnp.where(below, n, m)
                row = ghost if is_ghost else first
                t = r[pl.ds(p * SLOTS, SLOTS), src]
                if r is r_across and not is_ghost:
                    t = jnp.where(alone, 0.0, t)
                store[field, pl.ds(row + half * 8, SLOTS), :] = t
            t = r[pl.ds(NP * SLOTS, SLOTS), src]
            if r is r_across:
                t = jnp.where(alone, 0.0, t)
            vstore[pl.ds(ghost + half * 8, SLOTS), :] = t
    fetch.wait()
    side_planes(slots, store, vstore, None, across, 0, EDGE_LAYERS)


def shifter(slots):
    lane = iota((8, 128), 1)
    y = lax.rem(lane, EDGE)
    row = iota((8, 128), 0)
    col = columns(slots, (8, 128))
    prev = pltpu.roll(col, 1, 0)
    nxt = pltpu.roll(col, 7, 0)
    edge = {1: y == 0, -1: y == EDGE - 1}
    conn = {
        1: edge[1] & (row >= 1) & (col >= 0) & (prev == col - 1),
        -1: edge[-1] & (row < SLOTS - 1) & (nxt >= 0) & (nxt == col + 1),
    }
    low, high = lane < EDGE, lane >= 128 - EDGE

    def yshift(t, cy):
        if cy == 0:
            return t
        a = pltpu.roll(t, cy % 128, 1)
        b = pltpu.roll(pltpu.roll(t, (-15 * cy) % 128, 1), cy % 8, 0)
        return jnp.where(conn[cy], b, jnp.where(edge[cy], 0.0, a))

    def xyshift(t0, t1, v, ghost):
        t0, t1 = yshift(t0, v[1]), yshift(t1, v[1])
        if v[0] == 1:
            r0, r1 = pltpu.roll(t0, EDGE, 1), pltpu.roll(t1, EDGE, 1)
            return jnp.where(low, ghost, r0), jnp.where(low, r0, r1)
        if v[0] == -1:
            r0, r1 = pltpu.roll(t0, 128 - EDGE, 1), pltpu.roll(t1, 128 - EDGE, 1)
            return jnp.where(high, r1, r0), jnp.where(high, ghost, r1)
        return t0, t1

    return xyshift


def shift_layers(slots, store, moved, first, last):
    xyshift = shifter(slots)

    def body(at, carry):
        r0, r1 = pl.multiple_of(at * 16, 8), pl.multiple_of(at * 16 + 8, 8)
        for n in range(NF):
            t0, t1 = xyshift(store[n, pl.ds(r0, 8), :], store[n, pl.ds(r1, 8), :], vel(n), 0.0)
            moved[n, pl.ds(at * 5, SLOTS), :] = t0[0:SLOTS]
            moved[n, pl.ds(HALF + at * 5, SLOTS), :] = t1[0:SLOTS]
        return carry

    lax.fori_loop(first, last, body, 0)


def inside_kernel(slots_h, store, vstore, inside_in, inside, slots, sem):
    del inside_in
    load_all([pltpu.make_async_copy(slots_h, slots, sem.at[0])])
    side_planes(slots, store, vstore, inside, None, 0, EDGE_LAYERS)


def shift_kernel(slots_h, store, vstore, moved_in, moved, vmoved, slots, sem):
    del moved_in
    fetch = pltpu.make_async_copy(slots_h, slots, sem.at[0])
    fetch.start()
    for at in range(ZI):
        for half in range(2):
            vmoved[pl.ds(half * HALF + at * 5, SLOTS), :] = vstore[pl.ds(at * 16 + half * 8, SLOTS), :]
    fetch.wait()
    shift_layers(slots, store, moved, 0, EDGE_LAYERS)


def one_side(left, absent, slots, fetch, own, recv, moved, vmoved, gx, ghost_a, adj):
    lane16 = iota((16, 128), 1)
    first, last = lane16 == 0, lane16 == 127

    def yshift_dense(t, cy):
        if cy == 0:
            return t
        a = pltpu.roll(t, cy % 128, 1)
        return jnp.where(first if cy == 1 else last, 0.0, a)

    ghost = [None] * NF
    packs = []
    for p, (n, _, is_ghost) in enumerate(XP + [(None, None, True)]):
        rows = pl.ds(p * ZI, 16)
        t = recv[rows, :]
        if absent is not None and (n is None or not is_ghost):
            t = jnp.where(absent, 0.0, t)
        if n is None:
            v = t
        elif is_ghost:
            ghost[n] = yshift_dense(t, vel(n)[1])
        else:
            packs.append((yshift_dense(t, vel(n)[1]), gx, n))
            ghost[mirror(n, 0)] = yshift_dense(own[rows, :], vel(n)[1])
    m = moments(ghost[:19])
    d = defects(m)
    s = v - 1.0
    a, _ = adjoint(m, d, s, misfit(collide(m, d, s, True), ghost[19:]), True)
    for n in range(19):
        if VEL[n][0] == 1:
            t = jnp.where(v > 0.5, a[OPP[n]], 0.0)
            packs.append((yshift_dense(t, VEL[n][1]), ghost_a, n))
    fetch.wait()
    shifts = [lax.rem((jnp.where(left, 0, 7) - slots[k] + 16) * EDGE, 128) for k in range(SLOTS)]
    for t, dst, n in packs:
        field = jnp.where(left, n, mirror(n, 0))
        for k in range(SLOTS):
            r = pltpu.roll(t, shifts[k], 1)
            dst[field, pl.ds(k, 8, stride=5), :] = r[0:8]
            dst[field, pl.ds(40 + k, ZI - 8, stride=5), :] = r[8:ZI]

    lane = iota((8, 128), 1)
    entry = {1: (lane < EDGE) & left, -1: (lane >= 128 - EDGE) & jnp.logical_not(left)}
    base = jnp.where(left, 0, HALF)

    def advance(i, carry):
        r = pl.ds(pl.multiple_of(base + i * 8, 8), 8)
        f = []
        for n in range(NF):
            t = moved[n, r, :]
            if vel(n)[0]:
                t = jnp.where(entry[vel(n)[0]], gx[n, pl.ds(pl.multiple_of(i * 8, 8), 8), :], t)
            f.append(t)
        v = vmoved[r, :]
        s = v - 1.0
        m = moments(f[:19])
        d = defects(m)
        a, gs = adjoint(m, d, s, misfit(collide(m, d, s, True), f[19:]), True)
        listed = v > 0.5
        for n in range(19):
            adj[n, r, :] = jnp.where(listed, a[OPP[n]], 0.0)
        adj[19, r, :] = gs
        return carry

    lax.fori_loop(0, HALF // 8, advance, 0, unroll=7)


def near_kernel(slots_h, moved, vmoved, own, recv, adj, ghost_a, slots, gx, sem):
    fetch = pltpu.make_async_copy(slots_h, slots, sem.at[0])
    fetch.start()
    one_side(jnp.logical_not(even("blk")), None, slots, fetch, own, recv, moved, vmoved, gx, ghost_a, adj)


def final_kernel(slots_h, moved, vmoved, mstore, own, recv, adj_in, ghost_in, grad_h, out_h, adj, ghost_a,
                 slots, gx, back, a0, g0, grad, out, sem):
    del adj_in, ghost_in
    fetch = pltpu.make_async_copy(slots_h, slots, sem.at[0])
    fetch.start()
    one_side(even("blk"), at_end("blk"), slots, fetch, own, recv, moved, vmoved, gx, ghost_a, adj)
    xyshift = shifter(slots)

    def writes(z):
        lanes = pl.ds(pl.multiple_of(z * 256, 256), 256)
        return (
            pltpu.make_async_copy(out.at[:, :, lanes], out_h.at[:, :, lanes], sem.at[1 + z]),
            pltpu.make_async_copy(grad.at[:, lanes], grad_h.at[:, lanes], sem.at[1 + DZ + z]),
        )

    def pull(z, carry):
        rows = {c: place_of(z + c) * 5 for c in (-1, 0, 1)}
        for n in range(19):
            src = rows[-VEL[n][2]]
            t0 = adj[n, pl.ds(src, 8), :]
            t1 = adj[n, pl.ds(HALF + src, 8), :]
            g = ghost_a[n, pl.ds(src, 8), :] if VEL[n][0] else None
            t0, t1 = xyshift(t0, t1, VEL[n], g)
            back[n, pl.ds(z * 5, SLOTS), :] = t0[0:SLOTS]
            back[n, pl.ds(DZ * 5 + z * 5, SLOTS), :] = t1[0:SLOTS]
        for half in range(2):
            back[19, pl.ds(half * DZ * 5 + z * 5, SLOTS), :] = adj[19, pl.ds(half * HALF + rows[0], SLOTS), :]
        return carry

    def retreat(i, carry):
        for half in range(2):
            r = pl.ds(pl.multiple_of(half * DZ * 5 + i * 8, 8), 8)
            m = {name: mstore[j, r, :] for j, name in enumerate(M_NAMES)}
            v = mstore[19, r, :]
            listed = v > 0.5
            s = v - 1.0
            a, gs = adjoint(m, defects(m), s, [back[OPP[j], r, :] for j in range(19)])
            for j in range(19):
                a0[pl.ds(pl.multiple_of(j * ROWS_OWN + half * DZ * 5 + i * 8, 8), 8), :] = jnp.where(listed, a[j], 0.0)
            g0[r, :] = jnp.where(listed & (v < 1.75), gs + back[19, r, :], 0.0)
        return carry

    def send(z, carry):
        for half in range(2):
            lanes = pl.ds(pl.multiple_of(z * 256 + half * 128, 128), 128)
            base = half * DZ * 5 + z * 5
            for k in range(SLOTS):
                out[k, :, lanes] = a0[pl.ds(base + k, 19, stride=ROWS_OWN), :]
            grad[:, lanes] = g0[pl.ds(base, SLOTS), :]
        for c in writes(z):
            c.start()
        return carry

    lax.fori_loop(0, DZ, pull, 0, unroll=2)
    lax.fori_loop(0, DZ * 5 // 8, retreat, 0)
    lax.fori_loop(0, DZ, send, 0)

    def finish(z, carry):
        for c in writes(z):
            c.wait()
        return carry

    lax.fori_loop(0, DZ, finish, 0)


HBM = pl.BlockSpec(memory_space=pltpu.HBM)
VMEM = pl.BlockSpec(memory_space=pltpu.VMEM)


def exchange(inside, across, axis):
    rows, depth = lax.axis_size("blk"), lax.axis_size("gz")
    along_gz = axis == "gz"
    count = depth if along_gz else rows
    index = (lambda at, other: other * depth + at) if along_gz else (lambda at, other: at * depth + other)
    second = []
    for other in range(rows if along_gz else depth):
        for at in range(1, count - 1, 2):
            second += [(index(at, other), index(at + 1, other)), (index(at + 1, other), index(at, other))]
        second += [(index(at, other), index(at, other ^ 1)) for at in (0, count - 1)]
    first = [(i, i ^ 1) for i in range(count)]
    if inside is not None:
        inside = lax.ppermute(inside, axis, first)
    if across is not None:
        across = lax.ppermute(across, ("blk", "gz"), second)
    return inside, across


def at_end(axis):
    at = lax.axis_index(axis)
    return (at == 0) | (at == lax.axis_size(axis) - 1)


def per_device(populations, target, solid_frac, wall_mask, slot_column):
    f32 = jnp.float32
    populations = jnp.transpose(populations, (1, 0, 2))
    target = jnp.transpose(target, (1, 0, 2))
    populations, target, solid_frac, wall_mask, slot_column = (
        pltpu.with_memory_space_constraint(x, pltpu.HBM) for x in (populations, target, solid_frac, wall_mask, slot_column)
    )

    def params(mib):
        return pltpu.CompilerParams(vmem_limit_bytes=mib << 20)

    def inputs(cells):
        return [
            pltpu.SMEM((SLOTS,), jnp.int32),
            pltpu.VMEM((SLOTS, 19, cells), f32),
            pltpu.VMEM((SLOTS, 19, cells), jnp.bfloat16),
            pltpu.VMEM((SLOTS, cells), f32),
            pltpu.VMEM((SLOTS, cells), jnp.int32),
            pltpu.VMEM((cells // 128, 8 * SLOT_ROWS, 128), f32),
            pltpu.VMEM((cells // 128, 8 * SLOT_ROWS, 128), f32),
            pltpu.VMEM((8, cells), f32),
            pltpu.SemaphoreType.DMA((9,)),
        ]

    slots_in = [pltpu.SMEM((SLOTS,), jnp.int32)]
    zbuf = jax.ShapeDtypeStruct((ZROWS, 256), f32)
    inside, across = pl.pallas_call(
        border_kernel,
        in_specs=[HBM] * 5,
        out_specs=[VMEM] * 2,
        out_shape=[zbuf, zbuf],
        scratch_shapes=inputs(1024),
        compiler_params=params(8),
    )(slot_column, populations, target, solid_frac, wall_mask)
    r_inside, r_across = exchange(inside, across, "gz")
    store_t = jax.ShapeDtypeStruct((NF, ROWS_STORE, 128), f32)
    vstore_t = jax.ShapeDtypeStruct((ROWS_STORE, 128), f32)
    xbuf = jax.ShapeDtypeStruct((XROWS, 128), f32)
    xbuf2 = jax.ShapeDtypeStruct((XROWS + 8, 128), f32)
    moved_t = jax.ShapeDtypeStruct((NF, ROWS_COMPACT, 128), f32)
    store, vstore, mstore, moved, inside, across = pl.pallas_call(
        fields_kernel,
        in_specs=[HBM] * 5,
        out_specs=[VMEM] * 6,
        out_shape=[store_t, vstore_t, jax.ShapeDtypeStruct((20, ROWS_OWN, 128), f32), moved_t, xbuf, xbuf2],
        scratch_shapes=inputs(CELLS),
        compiler_params=params(12),
    )(slot_column, populations, target, solid_frac, wall_mask)
    store, vstore, across = pl.pallas_call(
        side_kernel,
        in_specs=[HBM] + [VMEM] * 5,
        out_specs=[VMEM] * 3,
        out_shape=[store_t, vstore_t, xbuf2],
        input_output_aliases={1: 0, 2: 1, 3: 2},
        scratch_shapes=slots_in + [pltpu.SemaphoreType.DMA((1,))],
        compiler_params=params(12),
    )(slot_column, store, vstore, across, r_inside, r_across)
    _, r_across = exchange(None, across, "blk")
    inside = pl.pallas_call(
        inside_kernel,
        in_specs=[HBM] + [VMEM] * 3,
        out_specs=VMEM,
        out_shape=xbuf,
        input_output_aliases={3: 0},
        scratch_shapes=slots_in + [pltpu.SemaphoreType.DMA((1,))],
        compiler_params=params(12),
    )(slot_column, store, vstore, inside)
    r_inside, _ = exchange(inside, None, "blk")
    moved, vmoved = pl.pallas_call(
        shift_kernel,
        in_specs=[HBM] + [VMEM] * 3,
        out_specs=[VMEM] * 2,
        out_shape=[moved_t, jax.ShapeDtypeStruct((ROWS_COMPACT, 128), f32)],
        input_output_aliases={3: 0},
        scratch_shapes=slots_in + [pltpu.SemaphoreType.DMA((1,))],
        compiler_params=params(12),
    )(slot_column, store, vstore, moved)
    gx_t = pltpu.VMEM((NF, HALF, 128), f32)
    adj_t = jax.ShapeDtypeStruct((20, ROWS_COMPACT, 128), f32)
    ghost_t = jax.ShapeDtypeStruct((19, HALF, 128), f32)
    adj, ghost_a = pl.pallas_call(
        near_kernel,
        in_specs=[HBM] + [VMEM] * 4,
        out_specs=[VMEM] * 2,
        out_shape=[adj_t, ghost_t],
        scratch_shapes=slots_in + [gx_t, pltpu.SemaphoreType.DMA((1,))],
        compiler_params=params(12),
    )(slot_column, moved, vmoved, inside, r_inside)
    grad, adjoint_out, _, _ = pl.pallas_call(
        final_kernel,
        in_specs=[HBM] + [VMEM] * 7,
        out_specs=[HBM, HBM, VMEM, VMEM],
        out_shape=[
            jax.ShapeDtypeStruct((SLOTS, CELLS), f32),
            jax.ShapeDtypeStruct((SLOTS, 19, CELLS), f32),
            adj_t,
            ghost_t,
        ],
        input_output_aliases={6: 2, 7: 3},
        scratch_shapes=slots_in + [
            gx_t,
            pltpu.VMEM((20, ROWS_OWN, 128), f32),
            pltpu.VMEM((19 * ROWS_OWN, 128), f32),
            pltpu.VMEM((ROWS_OWN, 128), f32),
            pltpu.VMEM((SLOTS, CELLS), f32),
            pltpu.VMEM((SLOTS, 19, CELLS), f32),
            pltpu.SemaphoreType.DMA((1 + 2 * DZ,)),
        ],
        compiler_params=params(20),
    )(slot_column, moved, vmoved, mstore, across, r_across, adj, ghost_a)
    return grad, jnp.transpose(adjoint_out, (1, 0, 2))


def solution(mesh):
    return jax.shard_map(
        per_device,
        mesh=mesh,
        in_specs=(
            P(None, "blk", "gz"),
            P(None, "blk", "gz"),
            P("blk", "gz"),
            P("blk", "gz"),
            P("blk"),
        ),
        out_specs=(P("blk", "gz"), P(None, "blk", "gz")),
        check_vma=False,
    )
```

```python
import jax
import jax.numpy as jnp
from jax import lax
from jax.experimental import pallas as pl
from jax.experimental.pallas import tpu as pltpu
from jax.sharding import PartitionSpec as P

EDGE = 16
GY = 8
SLOTS = 5
DZ = 8
CELLS = DZ * EDGE * EDGE

VEL = (
    (0, 0, 0),
    (1, 0, 0), (-1, 0, 0), (0, 1, 0), (0, -1, 0), (0, 0, 1), (0, 0, -1),
    (1, 1, 0), (-1, -1, 0), (1, -1, 0), (-1, 1, 0),
    (1, 0, 1), (-1, 0, -1), (1, 0, -1), (-1, 0, 1),
    (0, 1, 1), (0, -1, -1), (0, 1, -1), (0, -1, 1),
)
OPP = (0, 2, 1, 4, 3, 6, 5, 8, 7, 10, 9, 12, 11, 14, 13, 16, 15, 18, 17)
T_SCALE = (3.0,) + (9.0,) * 18

NF = 38
ZI = 10
ROWS_STORE = ZI * 16
HALF = 56
ROWS_COMPACT = 2 * HALF
ROWS_OWN = 2 * DZ * 5
EDGE_LAYERS = 4


def place(zd):
    return {-1: 0, 0: 1, DZ - 1: 2, DZ: 3}.get(zd, zd + 3)


def place_of(zd):
    return jnp.where(zd < 1, zd + 1, jnp.where(zd > DZ - 2, zd - DZ + 3, zd + 3))


def vel(n):
    return VEL[n % 19]


def mirror(n, dim):
    v = list(vel(n))
    v[dim] = -v[dim]
    return n // 19 * 19 + VEL.index(tuple(v))


def planes(dim):
    out = []
    for n in range(NF):
        c = vel(n)[dim]
        if c == 0:
            out.append((n, True, True))
        elif c == 1:
            out.append((n, False, True))
            out.append((n, True, False))
    return out


ZP, XP = planes(2), planes(0)
NP = len(ZP)
ZROWS = 200
XROWS = 400
SLOT_ROWS = 24


def moments(f):
    m = {}

    def pair(a):
        return f[a] + f[a + 1], f[a] - f[a + 1]

    sx, dx = pair(1)
    sy, dy = pair(3)
    sz, dz = pair(5)
    for name, a, t1, t2 in (("xy", 7, "xyy", "xxy"), ("xz", 11, "xzz", "xxz"), ("yz", 15, "yzz", "yyz")):
        sa, da = pair(a)
        sb, db = pair(a + 2)
        m["Q" + name] = sa + sb
        m["P" + name] = sa - sb
        m["T" + t1] = da + db
        m["T" + t2] = da - db
    qa = m["Qxy"] + m["Qxz"]
    m["Pxx"] = sx + qa
    m["Pyy"] = sy + (m["Qxy"] + m["Qyz"])
    m["Pzz"] = sz + (m["Qxz"] + m["Qyz"])
    m["rho"] = (f[0] + sx) + (sy + sz) + (qa + m["Qyz"])
    m["jx"] = dx + (m["Txyy"] + m["Txzz"])
    m["jy"] = dy + (m["Txxy"] + m["Tyzz"])
    m["jz"] = dz + (m["Txxz"] + m["Tyyz"])
    return m


def defects(m):
    ux, uy, uz = m["jx"], m["jy"], m["jz"]
    xx, yy, zz = ux * ux, uy * uy, uz * uz
    third = m["rho"] * (1.0 / 3.0)
    ninth = m["rho"] * (1.0 / 9.0) - (xx + yy + zz) * (1.0 / 6.0)
    d = {}
    d["Pxx"] = third + xx - m["Pxx"]
    d["Pyy"] = third + yy - m["Pyy"]
    d["Pzz"] = third + zz - m["Pzz"]
    d["Pxy"] = ux * uy - m["Pxy"]
    d["Pxz"] = ux * uz - m["Pxz"]
    d["Pyz"] = uy * uz - m["Pyz"]
    d["Qxy"] = ninth + (xx + yy) * 0.5 - m["Qxy"]
    d["Qxz"] = ninth + (xx + zz) * 0.5 - m["Qxz"]
    d["Qyz"] = ninth + (yy + zz) * 0.5 - m["Qyz"]
    return d


P_NAMES = ("Pxx", "Pyy", "Pzz", "Pxy", "Pxz", "Pyz")
Q_NAMES = ("Qxy", "Qxz", "Qyz")
M_NAMES = ("rho", "jx", "jy", "jz") + P_NAMES + Q_NAMES + ("Txyy", "Txzz", "Txxy", "Tyzz", "Txxz", "Tyyz")
T_OF = {"x": ("Txyy", "Txzz"), "y": ("Txxy", "Tyzz"), "z": ("Txxz", "Tyyz")}


def collide(m, d, s, scaled=False):
    two, four, shift = (4.5, 2.25, 18.0) if scaled else (0.5, 0.25, None)
    h = 1.0 - s
    h16 = 1.6 * h
    t_keep = 0.8 * h - 1.0
    h04 = 0.4 * h
    j_keep = h - s
    o = {}
    for name in P_NAMES:
        o[name] = m[name] + h16 * d[name]
    for name in Q_NAMES:
        o[name] = m[name] + h * d[name]
    for axis in "xyz":
        j = m["j" + axis]
        o["j" + axis] = j_keep * j
        hj = h04 * j
        for name in T_OF[axis]:
            o[name] = t_keep * m[name] + hj
    f = [None] * 19
    qs = (o["Qxy"] + o["Qxz"]) + o["Qyz"]
    f[0] = (m["rho"] + qs) - ((o["Pxx"] + o["Pyy"]) + o["Pzz"])
    if scaled:
        f[0] = 3.0 * f[0] + 6.0
    for a, p, q1, q2, axis in ((1, "Pxx", "Qxy", "Qxz", "x"), (3, "Pyy", "Qxy", "Qyz", "y"), (5, "Pzz", "Qxz", "Qyz", "z")):
        s_ = (o[p] - (o[q1] + o[q2])) * two
        if scaled:
            s_ = s_ + shift
        d_ = (o["j" + axis] - (o[T_OF[axis][0]] + o[T_OF[axis][1]])) * two
        f[a] = s_ + d_
        f[a + 1] = s_ - d_
    for name, a, t1, t2 in (("xy", 7, "Txyy", "Txxy"), ("xz", 11, "Txzz", "Txxz"), ("yz", 15, "Tyzz", "Tyyz")):
        q = o["Q" + name] * four
        if scaled:
            q = q + shift
        p = o["P" + name] * four
        u = o[t1] * four
        w = o[t2] * four
        sa, sb, da, db = q + p, q - p, u + w, u - w
        f[a] = sa + da
        f[a + 1] = sa - da
        f[a + 2] = sb + db
        f[a + 3] = sb - db
    return f


def adjoint(m, d, s, q, scaled=False):
    by_two = (lambda x: x) if scaled else (lambda x: x * 0.5)
    by_four = (lambda x: x) if scaled else (lambda x: x * 0.25)
    h = 1.0 - s
    h16 = 1.6 * h
    t_keep = 0.8 * h - 1.0
    h04 = 0.4 * h
    j_keep = h - s
    t = {}
    half = {}
    for axis, a in (("x", 1), ("y", 3), ("z", 5)):
        half[axis] = by_two(q[a] + q[a + 1])
        t["j" + axis] = by_two(q[a] - q[a + 1])
        t["P" + axis + axis] = half[axis] - q[0]
    for name, a, t1, t2 in (("xy", 7, "Txyy", "Txxy"), ("xz", 11, "Txzz", "Txxz"), ("yz", 15, "Tyzz", "Tyyz")):
        sa, da = q[a] + q[a + 1], q[a] - q[a + 1]
        sb, db = q[a + 2] + q[a + 3], q[a + 2] - q[a + 3]
        t["Q" + name] = by_four(sa + sb) - half[name[0]] - t["P" + name[1] * 2]
        t["P" + name] = by_four(sa - sb)
        t[t1] = by_four(da + db) - t["j" + name[0]]
        t[t2] = by_four(da - db) - t["j" + name[1]]
    gp = t["Pxx"] * d["Pxx"]
    for name in P_NAMES[1:]:
        gp = gp + t[name] * d[name]
    gq = t["Qxy"] * d["Qxy"] + t["Qxz"] * d["Qxz"] + t["Qyz"] * d["Qyz"]
    gt = None
    gj = None
    tsum = {}
    for axis in "xyz":
        tsum[axis] = t[T_OF[axis][0]] + t[T_OF[axis][1]]
        term = t[T_OF[axis][0]] * m[T_OF[axis][0]] + t[T_OF[axis][1]] * m[T_OF[axis][1]]
        gt = term if gt is None else gt + term
        term = (2.0 * t["j" + axis] + 0.4 * tsum[axis]) * m["j" + axis]
        gj = term if gj is None else gj + term
    gs = -(1.6 * gp + gq + gj + 0.8 * gt)
    ux, uy, uz = m["jx"], m["jy"], m["jz"]
    p_keep = 1.0 - h16
    qsum = t["Qxy"] + t["Qxz"] + t["Qyz"]
    u = {}
    u["rho"] = q[0] + (h16 * (1.0 / 3.0)) * (t["Pxx"] + t["Pyy"] + t["Pzz"]) + (h * (1.0 / 9.0)) * qsum
    third = qsum * (1.0 / 3.0)
    w16 = {"x": t["Pxy"] * uy + t["Pxz"] * uz, "y": t["Pxy"] * ux + t["Pyz"] * uz, "z": t["Pxz"] * ux + t["Pyz"] * uy}
    other = {"x": "Qyz", "y": "Qxz", "z": "Qxy"}
    for axis, uu in (("x", ux), ("y", uy), ("z", uz)):
        quad = 2.0 * third - t[other[axis]]
        u["j" + axis] = (
            j_keep * t["j" + axis]
            + h04 * tsum[axis]
            + h16 * (w16[axis] + 2.0 * t["P" + axis + axis] * uu)
            + h * (quad * uu)
        )
    for name in P_NAMES:
        u[name] = p_keep * t[name]
    for name in Q_NAMES:
        u[name] = s * t[name]
    for axis in "xyz":
        for name in T_OF[axis]:
            u[name] = t_keep * t[name]
    a_ = [None] * 19
    a_[0] = u["rho"]
    for axis, a in (("x", 1), ("y", 3), ("z", 5)):
        e = u["rho"] + u["P" + axis + axis]
        a_[a] = e + u["j" + axis]
        a_[a + 1] = e - u["j" + axis]
    for name, a, t1, t2 in (("xy", 7, "Txyy", "Txxy"), ("xz", 11, "Txzz", "Txxz"), ("yz", 15, "Tyzz", "Tyyz")):
        e = u["rho"] + u["P" + name[0] * 2] + u["P" + name[1] * 2] + u["Q" + name]
        ea, eb = e + u["P" + name], e - u["P" + name]
        o1, o2 = u["j" + name[0]] + u[t1], u["j" + name[1]] + u[t2]
        oa, ob = o1 + o2, o1 - o2
        a_[a] = ea + oa
        a_[a + 1] = ea - oa
        a_[a + 2] = eb + ob
        a_[a + 3] = eb - ob
    return a_, gs


def misfit(c, arrived):
    return [jnp.where(arrived[OPP[i]] > 1.0, c[i] - arrived[OPP[i]], 0.0) for i in range(19)]


def iota(shape, dim):
    return lax.broadcasted_iota(jnp.int32, shape, dim)


def columns(slots, shape):
    row = iota(shape, 0)
    col = jnp.full(shape, -1, jnp.int32)
    for k in range(SLOTS):
        col = jnp.where(row == k, slots[k], col)
    return col


def load_all(copies):
    for c in copies:
        c.start()
    for c in copies:
        c.wait()


def unpack(f_raw, t_raw, s_raw, w_raw, f_rows, t_rows, frac, tiles):
    for t in range(tiles):
        lanes = pl.ds(t * 128, 128)
        for k in range(SLOTS):
            f_rows[t, pl.ds(k * SLOT_ROWS, 19), :] = f_raw[k, :, lanes]
            t_rows[t, pl.ds(k * SLOT_ROWS, 19), :] = t_raw[k, :, lanes].astype(jnp.float32)
        frac[pl.ds(0, SLOTS), lanes] = jnp.where(w_raw[:, lanes] == 1, 1.0, s_raw[:, lanes])


def fields_of(f_rows, t_rows, frac, valid, tile):
    f = [f_rows[tile, pl.ds(i, 8, stride=SLOT_ROWS), :] for i in range(19)]
    s = frac[:, pl.ds(pl.multiple_of(tile * 128, 128), 128)]
    m = moments(f)
    c = collide(m, defects(m), s)
    out = [jnp.where(valid, c[i], 0.0) for i in range(19)]
    for i in range(19):
        t = t_rows[tile, pl.ds(OPP[i], 8, stride=SLOT_ROWS), :]
        out.append(jnp.where(valid, T_SCALE[i] * t + 2.0 * T_SCALE[i], 0.0))
    return out, jnp.where(valid, s + 1.0, 0.0), m


def even(axis):
    return lax.rem(lax.axis_index(axis), 2) == 0


def border_kernel(slots_h, f_h, t_h, s_h, w_h, inside, across, slots, f_raw, t_raw, s_raw, w_raw, f_rows, t_rows, frac, sem):
    copies = [pltpu.make_async_copy(slots_h, slots, sem.at[0])]
    for e, lane in enumerate((0, CELLS - 512)):
        src, dst = pl.ds(lane, 512), pl.ds(e * 512, 512)
        copies += [
            pltpu.make_async_copy(f_h.at[:, :, src], f_raw.at[:, :, dst], sem.at[1 + e]),
            pltpu.make_async_copy(t_h.at[:, :, src], t_raw.at[:, :, dst], sem.at[3 + e]),
            pltpu.make_async_copy(s_h.at[:, src], s_raw.at[:, dst], sem.at[5 + e]),
            pltpu.make_async_copy(w_h.at[:, src], w_raw.at[:, dst], sem.at[7 + e]),
        ]
    load_all(copies)
    unpack(f_raw, t_raw, s_raw, w_raw, f_rows, t_rows, frac, 8)
    valid = columns(slots, (8, 128)) >= 0
    even_z = even("gz")
    for out, goes_up in ((inside, even_z), (across, jnp.logical_not(even_z))):
        for outer in (True, False):
            layer = jnp.where(goes_up, 3, 0) if outer else jnp.where(goes_up, 2, 1)
            for half in range(2):
                dst = pl.ds(half * 128, 128)
                fields, v, _ = fields_of(f_rows, t_rows, frac, valid, layer * 2 + half)
                for p, (n, src, _) in enumerate(ZP):
                    if src == outer:
                        m = mirror(n, 2)
                        val = fields[n] if m == n else jnp.where(goes_up, fields[n], fields[m])
                        out[pl.ds(p * SLOTS, SLOTS), dst] = val[0:SLOTS]
                if outer:
                    out[pl.ds(NP * SLOTS, SLOTS), dst] = v[0:SLOTS]


def fields_kernel(slots_h, f_h, t_h, s_h, w_h, store, vstore, mstore, moved, inside, across, slots, f_raw, t_raw, s_raw, w_raw, f_rows, t_rows, frac, sem):
    load_all([
        pltpu.make_async_copy(slots_h, slots, sem.at[0]),
        pltpu.make_async_copy(f_h, f_raw, sem.at[1]),
        pltpu.make_async_copy(t_h, t_raw, sem.at[2]),
        pltpu.make_async_copy(s_h, s_raw, sem.at[3]),
        pltpu.make_async_copy(w_h, w_raw, sem.at[4]),
    ])
    unpack(f_raw, t_raw, s_raw, w_raw, f_rows, t_rows, frac, 16)
    valid = columns(slots, (8, 128)) >= 0

    def body(z, carry):
        rows = {c: pl.multiple_of(place_of(z + c) * 16, 16) for c in (-1, 0, 1)}
        for half in range(2):
            fields, v, m = fields_of(f_rows, t_rows, frac, valid, z * 2 + half)
            for n in range(NF):
                store[n, pl.ds(rows[vel(n)[2]] + half * 8, 8), :] = fields[n]
            vstore[pl.ds(rows[0] + half * 8, 8), :] = v
            own = pl.ds(half * DZ * 5 + z * 5, SLOTS)
            for i, name in enumerate(M_NAMES):
                mstore[i, own, :] = m[name][0:SLOTS]
            mstore[19, own, :] = v[0:SLOTS]
        return carry

    lax.fori_loop(0, DZ, body, 0, unroll=2)
    side_planes(slots, store, vstore, inside, across, EDGE_LAYERS, ZI)
    shift_layers(slots, store, moved, EDGE_LAYERS, ZI)


def side_planes(slots, store, vstore, inside, across, first, last):
    count = last - first
    group = iota((count, 128), 1) // EDGE
    masks = [group == slots[k] for k in range(SLOTS)]
    even_x = even("blk")
    for out, right in ((inside, even_x), (across, jnp.logical_not(even_x))):
        if out is None:
            continue
        half = jnp.where(right, 1, 0)
        outer_x, inner_x = jnp.where(right, 7, 0), jnp.where(right, 6, 1)
        shifts = {
            outer: [lax.rem((slots[k] - (outer_x if outer else inner_x) + 16) * EDGE, 128) for k in range(SLOTS)]
            for outer in (True, False)
        }
        for p, (n, outer, _) in enumerate(XP + [(None, True, None)]):
            if n is not None:
                m = mirror(n, 0)
                field = n if m == n else jnp.where(right, n, m)
            acc = jnp.zeros((count, 128), jnp.float32)
            for k in range(SLOTS):
                rows = pl.ds(first * 16 + half * 8 + k, count, stride=16)
                v = vstore[rows, :] if n is None else store[field, rows, :]
                acc = jnp.where(masks[k], pltpu.roll(v, shifts[outer][k], 1), acc)
            out[pl.ds(p * ZI + first, count), :] = acc


def side_kernel(slots_h, store_in, vstore_in, across_in, r_inside, r_across, store, vstore, across, slots, sem):
    del store_in, vstore_in, across_in
    fetch = pltpu.make_async_copy(slots_h, slots, sem.at[0])
    fetch.start()
    even_z, alone = even("gz"), at_end("gz")
    for r, below in ((r_inside, jnp.logical_not(even_z)), (r_across, even_z)):
        ghost = jnp.where(below, place(-1), place(DZ)) * 16
        first = jnp.where(below, place(0), place(DZ - 1)) * 16
        for half in range(2):
            src = pl.ds(half * 128, 128)
            for p, (n, _, is_ghost) in enumerate(ZP):
                m = mirror(n, 2)
                field = n if m == n else jnp.where(below, n, m)
                row = ghost if is_ghost else first
                t = r[pl.ds(p * SLOTS, SLOTS), src]
                if r is r_across and not is_ghost:
                    t = jnp.where(alone, 0.0, t)
                store[field, pl.ds(row + half * 8, SLOTS), :] = t
            t = r[pl.ds(NP * SLOTS, SLOTS), src]
            if r is r_across:
                t = jnp.where(alone, 0.0, t)
            vstore[pl.ds(ghost + half * 8, SLOTS), :] = t
    fetch.wait()
    side_planes(slots, store, vstore, None, across, 0, EDGE_LAYERS)


def shifter(slots):
    lane = iota((8, 128), 1)
    y = lax.rem(lane, EDGE)
    row = iota((8, 128), 0)
    col = columns(slots, (8, 128))
    prev = pltpu.roll(col, 1, 0)
    nxt = pltpu.roll(col, 7, 0)
    edge = {1: y == 0, -1: y == EDGE - 1}
    conn = {
        1: edge[1] & (row >= 1) & (col >= 0) & (prev == col - 1),
        -1: edge[-1] & (row < SLOTS - 1) & (nxt >= 0) & (nxt == col + 1),
    }
    low, high = lane < EDGE, lane >= 128 - EDGE

    def yshift(t, cy):
        if cy == 0:
            return t
        a = pltpu.roll(t, cy % 128, 1)
        b = pltpu.roll(pltpu.roll(t, (-15 * cy) % 128, 1), cy % 8, 0)
        return jnp.where(conn[cy], b, jnp.where(edge[cy], 0.0, a))

    def xyshift(t0, t1, v, ghost):
        t0, t1 = yshift(t0, v[1]), yshift(t1, v[1])
        if v[0] == 1:
            r0, r1 = pltpu.roll(t0, EDGE, 1), pltpu.roll(t1, EDGE, 1)
            return jnp.where(low, ghost, r0), jnp.where(low, r0, r1)
        if v[0] == -1:
            r0, r1 = pltpu.roll(t0, 128 - EDGE, 1), pltpu.roll(t1, 128 - EDGE, 1)
            return jnp.where(high, r1, r0), jnp.where(high, ghost, r1)
        return t0, t1

    return xyshift


def shift_layers(slots, store, moved, first, last):
    xyshift = shifter(slots)

    def body(at, carry):
        r0, r1 = pl.multiple_of(at * 16, 8), pl.multiple_of(at * 16 + 8, 8)
        for n in range(NF):
            t0, t1 = xyshift(store[n, pl.ds(r0, 8), :], store[n, pl.ds(r1, 8), :], vel(n), 0.0)
            moved[n, pl.ds(at * 5, SLOTS), :] = t0[0:SLOTS]
            moved[n, pl.ds(HALF + at * 5, SLOTS), :] = t1[0:SLOTS]
        return carry

    lax.fori_loop(first, last, body, 0)


def inside_kernel(slots_h, store, vstore, inside_in, inside, slots, sem):
    del inside_in
    load_all([pltpu.make_async_copy(slots_h, slots, sem.at[0])])
    side_planes(slots, store, vstore, inside, None, 0, EDGE_LAYERS)


def shift_kernel(slots_h, store, vstore, moved_in, moved, vmoved, slots, sem):
    del moved_in
    fetch = pltpu.make_async_copy(slots_h, slots, sem.at[0])
    fetch.start()
    for at in range(ZI):
        for half in range(2):
            vmoved[pl.ds(half * HALF + at * 5, SLOTS), :] = vstore[pl.ds(at * 16 + half * 8, SLOTS), :]
    fetch.wait()
    shift_layers(slots, store, moved, 0, EDGE_LAYERS)


def one_side(left, absent, slots, fetch, own, recv, moved, vmoved, gx, ghost_a, adj):
    lane16 = iota((16, 128), 1)
    first, last = lane16 == 0, lane16 == 127

    def yshift_dense(t, cy):
        if cy == 0:
            return t
        a = pltpu.roll(t, cy % 128, 1)
        return jnp.where(first if cy == 1 else last, 0.0, a)

    ghost = [None] * NF
    packs = []
    for p, (n, _, is_ghost) in enumerate(XP + [(None, None, True)]):
        rows = pl.ds(p * ZI, 16)
        t = recv[rows, :]
        if absent is not None and (n is None or not is_ghost):
            t = jnp.where(absent, 0.0, t)
        if n is None:
            v = t
        elif is_ghost:
            ghost[n] = yshift_dense(t, vel(n)[1])
        else:
            packs.append((yshift_dense(t, vel(n)[1]), gx, n))
            ghost[mirror(n, 0)] = yshift_dense(own[rows, :], vel(n)[1])
    m = moments(ghost[:19])
    d = defects(m)
    s = v - 1.0
    a, _ = adjoint(m, d, s, misfit(collide(m, d, s, True), ghost[19:]), True)
    for n in range(19):
        if VEL[n][0] == 1:
            t = jnp.where(v > 0.5, a[OPP[n]], 0.0)
            packs.append((yshift_dense(t, VEL[n][1]), ghost_a, n))
    fetch.wait()
    shifts = [lax.rem((jnp.where(left, 0, 7) - slots[k] + 16) * EDGE, 128) for k in range(SLOTS)]
    for t, dst, n in packs:
        field = jnp.where(left, n, mirror(n, 0))
        for k in range(SLOTS):
            r = pltpu.roll(t, shifts[k], 1)
            dst[field, pl.ds(k, 8, stride=5), :] = r[0:8]
            dst[field, pl.ds(40 + k, ZI - 8, stride=5), :] = r[8:ZI]

    lane = iota((8, 128), 1)
    entry = {1: (lane < EDGE) & left, -1: (lane >= 128 - EDGE) & jnp.logical_not(left)}
    base = jnp.where(left, 0, HALF)

    def advance(i, carry):
        r = pl.ds(pl.multiple_of(base + i * 8, 8), 8)
        f = []
        for n in range(NF):
            t = moved[n, r, :]
            if vel(n)[0]:
                t = jnp.where(entry[vel(n)[0]], gx[n, pl.ds(pl.multiple_of(i * 8, 8), 8), :], t)
            f.append(t)
        v = vmoved[r, :]
        s = v - 1.0
        m = moments(f[:19])
        d = defects(m)
        a, gs = adjoint(m, d, s, misfit(collide(m, d, s, True), f[19:]), True)
        listed = v > 0.5
        for n in range(19):
            adj[n, r, :] = jnp.where(listed, a[OPP[n]], 0.0)
        adj[19, r, :] = gs
        return carry

    lax.fori_loop(0, HALF // 8, advance, 0, unroll=7)


def near_kernel(slots_h, moved, vmoved, own, recv, adj, ghost_a, slots, gx, sem):
    fetch = pltpu.make_async_copy(slots_h, slots, sem.at[0])
    fetch.start()
    one_side(jnp.logical_not(even("blk")), None, slots, fetch, own, recv, moved, vmoved, gx, ghost_a, adj)


def final_kernel(slots_h, moved, vmoved, mstore, own, recv, adj_in, ghost_in, grad_h, out_h, adj, ghost_a,
                 slots, gx, back, a0, g0, grad, out, sem):
    del adj_in, ghost_in
    fetch = pltpu.make_async_copy(slots_h, slots, sem.at[0])
    fetch.start()
    one_side(even("blk"), at_end("blk"), slots, fetch, own, recv, moved, vmoved, gx, ghost_a, adj)
    xyshift = shifter(slots)

    def writes(z):
        lanes = pl.ds(pl.multiple_of(z * 256, 256), 256)
        return (
            pltpu.make_async_copy(out.at[:, :, lanes], out_h.at[:, :, lanes], sem.at[1 + z]),
            pltpu.make_async_copy(grad.at[:, lanes], grad_h.at[:, lanes], sem.at[1 + DZ + z]),
        )

    def pull(z, carry):
        rows = {c: place_of(z + c) * 5 for c in (-1, 0, 1)}
        for n in range(19):
            src = rows[-VEL[n][2]]
            t0 = adj[n, pl.ds(src, 8), :]
            t1 = adj[n, pl.ds(HALF + src, 8), :]
            g = ghost_a[n, pl.ds(src, 8), :] if VEL[n][0] else None
            t0, t1 = xyshift(t0, t1, VEL[n], g)
            back[n, pl.ds(z * 5, SLOTS), :] = t0[0:SLOTS]
            back[n, pl.ds(DZ * 5 + z * 5, SLOTS), :] = t1[0:SLOTS]
        for half in range(2):
            back[19, pl.ds(half * DZ * 5 + z * 5, SLOTS), :] = adj[19, pl.ds(half * HALF + rows[0], SLOTS), :]
        return carry

    def retreat(i, carry):
        for half in range(2):
            r = pl.ds(pl.multiple_of(half * DZ * 5 + i * 8, 8), 8)
            m = {name: mstore[j, r, :] for j, name in enumerate(M_NAMES)}
            v = mstore[19, r, :]
            listed = v > 0.5
            s = v - 1.0
            a, gs = adjoint(m, defects(m), s, [back[OPP[j], r, :] for j in range(19)])
            for j in range(19):
                a0[pl.ds(pl.multiple_of(j * ROWS_OWN + half * DZ * 5 + i * 8, 8), 8), :] = jnp.where(listed, a[j], 0.0)
            g0[r, :] = jnp.where(listed & (v < 1.75), gs + back[19, r, :], 0.0)
        return carry

    def send(z, carry):
        for half in range(2):
            lanes = pl.ds(pl.multiple_of(z * 256 + half * 128, 128), 128)
            base = half * DZ * 5 + z * 5
            for k in range(SLOTS):
                out[k, :, lanes] = a0[pl.ds(base + k, 19, stride=ROWS_OWN), :]
            grad[:, lanes] = g0[pl.ds(base, SLOTS), :]
        for c in writes(z):
            c.start()
        return carry

    lax.fori_loop(0, DZ, pull, 0, unroll=2)
    lax.fori_loop(0, 3, retreat, 0)
    lax.fori_loop(0, 4, send, 0)
    lax.fori_loop(3, DZ * 5 // 8, retreat, 0)
    lax.fori_loop(4, DZ, send, 0)

    def finish(z, carry):
        for c in writes(z):
            c.wait()
        return carry

    lax.fori_loop(0, DZ, finish, 0)


HBM = pl.BlockSpec(memory_space=pltpu.HBM)
VMEM = pl.BlockSpec(memory_space=pltpu.VMEM)


def exchange(inside, across, axis):
    rows, depth = lax.axis_size("blk"), lax.axis_size("gz")
    along_gz = axis == "gz"
    count = depth if along_gz else rows
    index = (lambda at, other: other * depth + at) if along_gz else (lambda at, other: at * depth + other)
    second = []
    for other in range(rows if along_gz else depth):
        for at in range(1, count - 1, 2):
            second += [(index(at, other), index(at + 1, other)), (index(at + 1, other), index(at, other))]
        second += [(index(at, other), index(at, other ^ 1)) for at in (0, count - 1)]
    first = [(i, i ^ 1) for i in range(count)]
    if inside is not None:
        inside = lax.ppermute(inside, axis, first)
    if across is not None:
        across = lax.ppermute(across, ("blk", "gz"), second)
    return inside, across


def at_end(axis):
    at = lax.axis_index(axis)
    return (at == 0) | (at == lax.axis_size(axis) - 1)


def per_device(populations, target, solid_frac, wall_mask, slot_column):
    f32 = jnp.float32
    populations = jnp.transpose(populations, (1, 0, 2))
    target = jnp.transpose(target, (1, 0, 2))
    populations, target, solid_frac, wall_mask, slot_column = (
        pltpu.with_memory_space_constraint(x, pltpu.HBM) for x in (populations, target, solid_frac, wall_mask, slot_column)
    )

    def params(mib):
        return pltpu.CompilerParams(vmem_limit_bytes=mib << 20)

    def inputs(cells):
        return [
            pltpu.SMEM((SLOTS,), jnp.int32),
            pltpu.VMEM((SLOTS, 19, cells), f32),
            pltpu.VMEM((SLOTS, 19, cells), jnp.bfloat16),
            pltpu.VMEM((SLOTS, cells), f32),
            pltpu.VMEM((SLOTS, cells), jnp.int32),
            pltpu.VMEM((cells // 128, 8 * SLOT_ROWS, 128), f32),
            pltpu.VMEM((cells // 128, 8 * SLOT_ROWS, 128), f32),
            pltpu.VMEM((8, cells), f32),
            pltpu.SemaphoreType.DMA((9,)),
        ]

    slots_in = [pltpu.SMEM((SLOTS,), jnp.int32)]
    zbuf = jax.ShapeDtypeStruct((ZROWS, 256), f32)
    inside, across = pl.pallas_call(
        border_kernel,
        in_specs=[HBM] * 5,
        out_specs=[VMEM] * 2,
        out_shape=[zbuf, zbuf],
        scratch_shapes=inputs(1024),
        compiler_params=params(8),
    )(slot_column, populations, target, solid_frac, wall_mask)
    r_inside, r_across = exchange(inside, across, "gz")
    store_t = jax.ShapeDtypeStruct((NF, ROWS_STORE, 128), f32)
    vstore_t = jax.ShapeDtypeStruct((ROWS_STORE, 128), f32)
    xbuf = jax.ShapeDtypeStruct((XROWS, 128), f32)
    xbuf2 = jax.ShapeDtypeStruct((XROWS + 8, 128), f32)
    moved_t = jax.ShapeDtypeStruct((NF, ROWS_COMPACT, 128), f32)
    store, vstore, mstore, moved, inside, across = pl.pallas_call(
        fields_kernel,
        in_specs=[HBM] * 5,
        out_specs=[VMEM] * 6,
        out_shape=[store_t, vstore_t, jax.ShapeDtypeStruct((20, ROWS_OWN, 128), f32), moved_t, xbuf, xbuf2],
        scratch_shapes=inputs(CELLS),
        compiler_params=params(12),
    )(slot_column, populations, target, solid_frac, wall_mask)
    store, vstore, across = pl.pallas_call(
        side_kernel,
        in_specs=[HBM] + [VMEM] * 5,
        out_specs=[VMEM] * 3,
        out_shape=[store_t, vstore_t, xbuf2],
        input_output_aliases={1: 0, 2: 1, 3: 2},
        scratch_shapes=slots_in + [pltpu.SemaphoreType.DMA((1,))],
        compiler_params=params(12),
    )(slot_column, store, vstore, across, r_inside, r_across)
    _, r_across = exchange(None, across, "blk")
    inside = pl.pallas_call(
        inside_kernel,
        in_specs=[HBM] + [VMEM] * 3,
        out_specs=VMEM,
        out_shape=xbuf,
        input_output_aliases={3: 0},
        scratch_shapes=slots_in + [pltpu.SemaphoreType.DMA((1,))],
        compiler_params=params(12),
    )(slot_column, store, vstore, inside)
    r_inside, _ = exchange(inside, None, "blk")
    moved, vmoved = pl.pallas_call(
        shift_kernel,
        in_specs=[HBM] + [VMEM] * 3,
        out_specs=[VMEM] * 2,
        out_shape=[moved_t, jax.ShapeDtypeStruct((ROWS_COMPACT, 128), f32)],
        input_output_aliases={3: 0},
        scratch_shapes=slots_in + [pltpu.SemaphoreType.DMA((1,))],
        compiler_params=params(12),
    )(slot_column, store, vstore, moved)
    gx_t = pltpu.VMEM((NF, HALF, 128), f32)
    adj_t = jax.ShapeDtypeStruct((20, ROWS_COMPACT, 128), f32)
    ghost_t = jax.ShapeDtypeStruct((19, HALF, 128), f32)
    adj, ghost_a = pl.pallas_call(
        near_kernel,
        in_specs=[HBM] + [VMEM] * 4,
        out_specs=[VMEM] * 2,
        out_shape=[adj_t, ghost_t],
        scratch_shapes=slots_in + [gx_t, pltpu.SemaphoreType.DMA((1,))],
        compiler_params=params(12),
    )(slot_column, moved, vmoved, inside, r_inside)
    grad, adjoint_out, _, _ = pl.pallas_call(
        final_kernel,
        in_specs=[HBM] + [VMEM] * 7,
        out_specs=[HBM, HBM, VMEM, VMEM],
        out_shape=[
            jax.ShapeDtypeStruct((SLOTS, CELLS), f32),
            jax.ShapeDtypeStruct((SLOTS, 19, CELLS), f32),
            adj_t,
            ghost_t,
        ],
        input_output_aliases={6: 2, 7: 3},
        scratch_shapes=slots_in + [
            gx_t,
            pltpu.VMEM((20, ROWS_OWN, 128), f32),
            pltpu.VMEM((19 * ROWS_OWN, 128), f32),
            pltpu.VMEM((ROWS_OWN, 128), f32),
            pltpu.VMEM((SLOTS, CELLS), f32),
            pltpu.VMEM((SLOTS, 19, CELLS), f32),
            pltpu.SemaphoreType.DMA((1 + 2 * DZ,)),
        ],
        compiler_params=params(20),
    )(slot_column, moved, vmoved, mstore, across, r_across, adj, ghost_a)
    return grad, jnp.transpose(adjoint_out, (1, 0, 2))


def solution(mesh):
    return jax.shard_map(
        per_device,
        mesh=mesh,
        in_specs=(
            P(None, "blk", "gz"),
            P(None, "blk", "gz"),
            P("blk", "gz"),
            P("blk", "gz"),
            P("blk"),
        ),
        out_specs=(P("blk", "gz"), P(None, "blk", "gz")),
        check_vma=False,
    )
```

```python
import jax
import jax.numpy as jnp
from jax import lax
from jax.experimental import pallas as pl
from jax.experimental.pallas import tpu as pltpu
from jax.sharding import PartitionSpec as P

EDGE = 16
GY = 8
SLOTS = 5
DZ = 8
CELLS = DZ * EDGE * EDGE

VEL = (
    (0, 0, 0),
    (1, 0, 0), (-1, 0, 0), (0, 1, 0), (0, -1, 0), (0, 0, 1), (0, 0, -1),
    (1, 1, 0), (-1, -1, 0), (1, -1, 0), (-1, 1, 0),
    (1, 0, 1), (-1, 0, -1), (1, 0, -1), (-1, 0, 1),
    (0, 1, 1), (0, -1, -1), (0, 1, -1), (0, -1, 1),
)
OPP = (0, 2, 1, 4, 3, 6, 5, 8, 7, 10, 9, 12, 11, 14, 13, 16, 15, 18, 17)
T_SCALE = (3.0,) + (9.0,) * 18

NF = 38
ZI = 10
ROWS_STORE = ZI * 16
HALF = 56
ROWS_COMPACT = 2 * HALF
ROWS_OWN = 2 * DZ * 5
EDGE_LAYERS = 4


def place(zd):
    return {-1: 0, 0: 1, DZ - 1: 2, DZ: 3}.get(zd, zd + 3)


def place_of(zd):
    return jnp.where(zd < 1, zd + 1, jnp.where(zd > DZ - 2, zd - DZ + 3, zd + 3))


def vel(n):
    return VEL[n % 19]


def mirror(n, dim):
    v = list(vel(n))
    v[dim] = -v[dim]
    return n // 19 * 19 + VEL.index(tuple(v))


def planes(dim):
    out = []
    for n in range(NF):
        c = vel(n)[dim]
        if c == 0:
            out.append((n, True, True))
        elif c == 1:
            out.append((n, False, True))
            out.append((n, True, False))
    return out


ZP, XP = planes(2), planes(0)
NP = len(ZP)
ZROWS = 200
XROWS = 400
SLOT_ROWS = 24


def moments(f):
    m = {}

    def pair(a):
        return f[a] + f[a + 1], f[a] - f[a + 1]

    sx, dx = pair(1)
    sy, dy = pair(3)
    sz, dz = pair(5)
    for name, a, t1, t2 in (("xy", 7, "xyy", "xxy"), ("xz", 11, "xzz", "xxz"), ("yz", 15, "yzz", "yyz")):
        sa, da = pair(a)
        sb, db = pair(a + 2)
        m["Q" + name] = sa + sb
        m["P" + name] = sa - sb
        m["T" + t1] = da + db
        m["T" + t2] = da - db
    qa = m["Qxy"] + m["Qxz"]
    m["Pxx"] = sx + qa
    m["Pyy"] = sy + (m["Qxy"] + m["Qyz"])
    m["Pzz"] = sz + (m["Qxz"] + m["Qyz"])
    m["rho"] = (f[0] + sx) + (sy + sz) + (qa + m["Qyz"])
    m["jx"] = dx + (m["Txyy"] + m["Txzz"])
    m["jy"] = dy + (m["Txxy"] + m["Tyzz"])
    m["jz"] = dz + (m["Txxz"] + m["Tyyz"])
    return m


def defects(m):
    ux, uy, uz = m["jx"], m["jy"], m["jz"]
    xx, yy, zz = ux * ux, uy * uy, uz * uz
    third = m["rho"] * (1.0 / 3.0)
    ninth = m["rho"] * (1.0 / 9.0) - (xx + yy + zz) * (1.0 / 6.0)
    d = {}
    d["Pxx"] = third + xx - m["Pxx"]
    d["Pyy"] = third + yy - m["Pyy"]
    d["Pzz"] = third + zz - m["Pzz"]
    d["Pxy"] = ux * uy - m["Pxy"]
    d["Pxz"] = ux * uz - m["Pxz"]
    d["Pyz"] = uy * uz - m["Pyz"]
    d["Qxy"] = ninth + (xx + yy) * 0.5 - m["Qxy"]
    d["Qxz"] = ninth + (xx + zz) * 0.5 - m["Qxz"]
    d["Qyz"] = ninth + (yy + zz) * 0.5 - m["Qyz"]
    return d


P_NAMES = ("Pxx", "Pyy", "Pzz", "Pxy", "Pxz", "Pyz")
Q_NAMES = ("Qxy", "Qxz", "Qyz")
M_NAMES = ("rho", "jx", "jy", "jz") + P_NAMES + Q_NAMES + ("Txyy", "Txzz", "Txxy", "Tyzz", "Txxz", "Tyyz")
T_OF = {"x": ("Txyy", "Txzz"), "y": ("Txxy", "Tyzz"), "z": ("Txxz", "Tyyz")}


def collide(m, d, s, scaled=False):
    two, four, shift = (4.5, 2.25, 18.0) if scaled else (0.5, 0.25, None)
    h = 1.0 - s
    h16 = 1.6 * h
    t_keep = 0.8 * h - 1.0
    h04 = 0.4 * h
    j_keep = h - s
    o = {}
    for name in P_NAMES:
        o[name] = m[name] + h16 * d[name]
    for name in Q_NAMES:
        o[name] = m[name] + h * d[name]
    for axis in "xyz":
        j = m["j" + axis]
        o["j" + axis] = j_keep * j
        hj = h04 * j
        for name in T_OF[axis]:
            o[name] = t_keep * m[name] + hj
    f = [None] * 19
    qs = (o["Qxy"] + o["Qxz"]) + o["Qyz"]
    f[0] = (m["rho"] + qs) - ((o["Pxx"] + o["Pyy"]) + o["Pzz"])
    if scaled:
        f[0] = 3.0 * f[0] + 6.0
    for a, p, q1, q2, axis in ((1, "Pxx", "Qxy", "Qxz", "x"), (3, "Pyy", "Qxy", "Qyz", "y"), (5, "Pzz", "Qxz", "Qyz", "z")):
        s_ = (o[p] - (o[q1] + o[q2])) * two
        if scaled:
            s_ = s_ + shift
        d_ = (o["j" + axis] - (o[T_OF[axis][0]] + o[T_OF[axis][1]])) * two
        f[a] = s_ + d_
        f[a + 1] = s_ - d_
    for name, a, t1, t2 in (("xy", 7, "Txyy", "Txxy"), ("xz", 11, "Txzz", "Txxz"), ("yz", 15, "Tyzz", "Tyyz")):
        q = o["Q" + name] * four
        if scaled:
            q = q + shift
        p = o["P" + name] * four
        u = o[t1] * four
        w = o[t2] * four
        sa, sb, da, db = q + p, q - p, u + w, u - w
        f[a] = sa + da
        f[a + 1] = sa - da
        f[a + 2] = sb + db
        f[a + 3] = sb - db
    return f


def adjoint(m, d, s, q, scaled=False):
    by_two = (lambda x: x) if scaled else (lambda x: x * 0.5)
    by_four = (lambda x: x) if scaled else (lambda x: x * 0.25)
    h = 1.0 - s
    h16 = 1.6 * h
    t_keep = 0.8 * h - 1.0
    h04 = 0.4 * h
    j_keep = h - s
    t = {}
    half = {}
    for axis, a in (("x", 1), ("y", 3), ("z", 5)):
        half[axis] = by_two(q[a] + q[a + 1])
        t["j" + axis] = by_two(q[a] - q[a + 1])
        t["P" + axis + axis] = half[axis] - q[0]
    for name, a, t1, t2 in (("xy", 7, "Txyy", "Txxy"), ("xz", 11, "Txzz", "Txxz"), ("yz", 15, "Tyzz", "Tyyz")):
        sa, da = q[a] + q[a + 1], q[a] - q[a + 1]
        sb, db = q[a + 2] + q[a + 3], q[a + 2] - q[a + 3]
        t["Q" + name] = by_four(sa + sb) - half[name[0]] - t["P" + name[1] * 2]
        t["P" + name] = by_four(sa - sb)
        t[t1] = by_four(da + db) - t["j" + name[0]]
        t[t2] = by_four(da - db) - t["j" + name[1]]
    gp = t["Pxx"] * d["Pxx"]
    for name in P_NAMES[1:]:
        gp = gp + t[name] * d[name]
    gq = t["Qxy"] * d["Qxy"] + t["Qxz"] * d["Qxz"] + t["Qyz"] * d["Qyz"]
    gt = None
    gj = None
    tsum = {}
    for axis in "xyz":
        tsum[axis] = t[T_OF[axis][0]] + t[T_OF[axis][1]]
        term = t[T_OF[axis][0]] * m[T_OF[axis][0]] + t[T_OF[axis][1]] * m[T_OF[axis][1]]
        gt = term if gt is None else gt + term
        term = (2.0 * t["j" + axis] + 0.4 * tsum[axis]) * m["j" + axis]
        gj = term if gj is None else gj + term
    gs = -(1.6 * gp + gq + gj + 0.8 * gt)
    ux, uy, uz = m["jx"], m["jy"], m["jz"]
    p_keep = 1.0 - h16
    qsum = t["Qxy"] + t["Qxz"] + t["Qyz"]
    u = {}
    u["rho"] = q[0] + (h16 * (1.0 / 3.0)) * (t["Pxx"] + t["Pyy"] + t["Pzz"]) + (h * (1.0 / 9.0)) * qsum
    third = qsum * (1.0 / 3.0)
    w16 = {"x": t["Pxy"] * uy + t["Pxz"] * uz, "y": t["Pxy"] * ux + t["Pyz"] * uz, "z": t["Pxz"] * ux + t["Pyz"] * uy}
    other = {"x": "Qyz", "y": "Qxz", "z": "Qxy"}
    for axis, uu in (("x", ux), ("y", uy), ("z", uz)):
        quad = 2.0 * third - t[other[axis]]
        u["j" + axis] = (
            j_keep * t["j" + axis]
            + h04 * tsum[axis]
            + h16 * (w16[axis] + 2.0 * t["P" + axis + axis] * uu)
            + h * (quad * uu)
        )
    for name in P_NAMES:
        u[name] = p_keep * t[name]
    for name in Q_NAMES:
        u[name] = s * t[name]
    for axis in "xyz":
        for name in T_OF[axis]:
            u[name] = t_keep * t[name]
    a_ = [None] * 19
    a_[0] = u["rho"]
    for axis, a in (("x", 1), ("y", 3), ("z", 5)):
        e = u["rho"] + u["P" + axis + axis]
        a_[a] = e + u["j" + axis]
        a_[a + 1] = e - u["j" + axis]
    for name, a, t1, t2 in (("xy", 7, "Txyy", "Txxy"), ("xz", 11, "Txzz", "Txxz"), ("yz", 15, "Tyzz", "Tyyz")):
        e = u["rho"] + u["P" + name[0] * 2] + u["P" + name[1] * 2] + u["Q" + name]
        ea, eb = e + u["P" + name], e - u["P" + name]
        o1, o2 = u["j" + name[0]] + u[t1], u["j" + name[1]] + u[t2]
        oa, ob = o1 + o2, o1 - o2
        a_[a] = ea + oa
        a_[a + 1] = ea - oa
        a_[a + 2] = eb + ob
        a_[a + 3] = eb - ob
    return a_, gs


def misfit(c, arrived):
    return [jnp.where(arrived[OPP[i]] > 1.0, c[i] - arrived[OPP[i]], 0.0) for i in range(19)]


def iota(shape, dim):
    return lax.broadcasted_iota(jnp.int32, shape, dim)


def columns(slots, shape):
    row = iota(shape, 0)
    col = jnp.full(shape, -1, jnp.int32)
    for k in range(SLOTS):
        col = jnp.where(row == k, slots[k], col)
    return col


def load_all(copies):
    for c in copies:
        c.start()
    for c in copies:
        c.wait()


def unpack(f_raw, t_raw, s_raw, w_raw, f_rows, t_rows, frac, tiles):
    for t in range(tiles):
        lanes = pl.ds(t * 128, 128)
        for k in range(SLOTS):
            f_rows[t, pl.ds(k * SLOT_ROWS, 19), :] = f_raw[k, :, lanes]
            t_rows[t, pl.ds(k * SLOT_ROWS, 19), :] = t_raw[k, :, lanes].astype(jnp.float32)
        frac[pl.ds(0, SLOTS), lanes] = jnp.where(w_raw[:, lanes] == 1, 1.0, s_raw[:, lanes])


def fields_of(f_rows, t_rows, frac, valid, tile):
    f = [f_rows[tile, pl.ds(i, 8, stride=SLOT_ROWS), :] for i in range(19)]
    s = frac[:, pl.ds(pl.multiple_of(tile * 128, 128), 128)]
    m = moments(f)
    c = collide(m, defects(m), s)
    out = [jnp.where(valid, c[i], 0.0) for i in range(19)]
    for i in range(19):
        t = t_rows[tile, pl.ds(OPP[i], 8, stride=SLOT_ROWS), :]
        out.append(jnp.where(valid, T_SCALE[i] * t + 2.0 * T_SCALE[i], 0.0))
    return out, jnp.where(valid, s + 1.0, 0.0), m


def even(axis):
    return lax.rem(lax.axis_index(axis), 2) == 0


def border_kernel(slots_h, f_h, t_h, s_h, w_h, inside, across, slots, f_raw, t_raw, s_raw, w_raw, f_rows, t_rows, frac, sem):
    copies = [pltpu.make_async_copy(slots_h, slots, sem.at[0])]
    for e, lane in enumerate((0, CELLS - 512)):
        src, dst = pl.ds(lane, 512), pl.ds(e * 512, 512)
        copies += [
            pltpu.make_async_copy(f_h.at[:, :, src], f_raw.at[:, :, dst], sem.at[1 + e]),
            pltpu.make_async_copy(t_h.at[:, :, src], t_raw.at[:, :, dst], sem.at[3 + e]),
            pltpu.make_async_copy(s_h.at[:, src], s_raw.at[:, dst], sem.at[5 + e]),
            pltpu.make_async_copy(w_h.at[:, src], w_raw.at[:, dst], sem.at[7 + e]),
        ]
    load_all(copies)
    unpack(f_raw, t_raw, s_raw, w_raw, f_rows, t_rows, frac, 8)
    valid = columns(slots, (8, 128)) >= 0
    even_z = even("gz")
    for out, goes_up in ((inside, even_z), (across, jnp.logical_not(even_z))):
        for outer in (True, False):
            layer = jnp.where(goes_up, 3, 0) if outer else jnp.where(goes_up, 2, 1)
            for half in range(2):
                dst = pl.ds(half * 128, 128)
                fields, v, _ = fields_of(f_rows, t_rows, frac, valid, layer * 2 + half)
                for p, (n, src, _) in enumerate(ZP):
                    if src == outer:
                        m = mirror(n, 2)
                        val = fields[n] if m == n else jnp.where(goes_up, fields[n], fields[m])
                        out[pl.ds(p * SLOTS, SLOTS), dst] = val[0:SLOTS]
                if outer:
                    out[pl.ds(NP * SLOTS, SLOTS), dst] = v[0:SLOTS]


def fields_kernel(slots_h, f_h, t_h, s_h, w_h, store, vstore, mstore, moved, inside, across, slots, f_raw, t_raw, s_raw, w_raw, f_rows, t_rows, frac, sem):
    load_all([
        pltpu.make_async_copy(slots_h, slots, sem.at[0]),
        pltpu.make_async_copy(f_h, f_raw, sem.at[1]),
        pltpu.make_async_copy(t_h, t_raw, sem.at[2]),
        pltpu.make_async_copy(s_h, s_raw, sem.at[3]),
        pltpu.make_async_copy(w_h, w_raw, sem.at[4]),
    ])
    unpack(f_raw, t_raw, s_raw, w_raw, f_rows, t_rows, frac, 16)
    valid = columns(slots, (8, 128)) >= 0

    def body(z, carry):
        rows = {c: pl.multiple_of(place_of(z + c) * 16, 16) for c in (-1, 0, 1)}
        for half in range(2):
            fields, v, m = fields_of(f_rows, t_rows, frac, valid, z * 2 + half)
            for n in range(NF):
                store[n, pl.ds(rows[vel(n)[2]] + half * 8, 8), :] = fields[n]
            vstore[pl.ds(rows[0] + half * 8, 8), :] = v
            own = pl.ds(half * DZ * 5 + z * 5, SLOTS)
            for i, name in enumerate(M_NAMES):
                mstore[i, own, :] = m[name][0:SLOTS]
            mstore[19, own, :] = v[0:SLOTS]
        return carry

    lax.fori_loop(0, DZ, body, 0, unroll=2)
    side_planes(slots, store, vstore, inside, across, EDGE_LAYERS, ZI)
    shift_layers(slots, store, moved, EDGE_LAYERS, ZI)


def side_planes(slots, store, vstore, inside, across, first, last):
    count = last - first
    group = iota((count, 128), 1) // EDGE
    masks = [group == slots[k] for k in range(SLOTS)]
    even_x = even("blk")
    for out, right in ((inside, even_x), (across, jnp.logical_not(even_x))):
        if out is None:
            continue
        half = jnp.where(right, 1, 0)
        outer_x, inner_x = jnp.where(right, 7, 0), jnp.where(right, 6, 1)
        shifts = {
            outer: [lax.rem((slots[k] - (outer_x if outer else inner_x) + 16) * EDGE, 128) for k in range(SLOTS)]
            for outer in (True, False)
        }
        for p, (n, outer, _) in enumerate(XP + [(None, True, None)]):
            if n is not None:
                m = mirror(n, 0)
                field = n if m == n else jnp.where(right, n, m)
            acc = jnp.zeros((count, 128), jnp.float32)
            for k in range(SLOTS):
                rows = pl.ds(first * 16 + half * 8 + k, count, stride=16)
                v = vstore[rows, :] if n is None else store[field, rows, :]
                acc = jnp.where(masks[k], pltpu.roll(v, shifts[outer][k], 1), acc)
            out[pl.ds(p * ZI + first, count), :] = acc


def side_kernel(slots_h, store_in, vstore_in, across_in, inside_in, r_inside, r_across, store, vstore, across, inside, slots, sem):
    del store_in, vstore_in, across_in, inside_in
    fetch = pltpu.make_async_copy(slots_h, slots, sem.at[0])
    fetch.start()
    even_z, alone = even("gz"), at_end("gz")
    for r, below in ((r_inside, jnp.logical_not(even_z)), (r_across, even_z)):
        ghost = jnp.where(below, place(-1), place(DZ)) * 16
        first = jnp.where(below, place(0), place(DZ - 1)) * 16
        for half in range(2):
            src = pl.ds(half * 128, 128)
            for p, (n, _, is_ghost) in enumerate(ZP):
                m = mirror(n, 2)
                field = n if m == n else jnp.where(below, n, m)
                row = ghost if is_ghost else first
                t = r[pl.ds(p * SLOTS, SLOTS), src]
                if r is r_across and not is_ghost:
                    t = jnp.where(alone, 0.0, t)
                store[field, pl.ds(row + half * 8, SLOTS), :] = t
            t = r[pl.ds(NP * SLOTS, SLOTS), src]
            if r is r_across:
                t = jnp.where(alone, 0.0, t)
            vstore[pl.ds(ghost + half * 8, SLOTS), :] = t
    fetch.wait()
    side_planes(slots, store, vstore, inside, across, 0, EDGE_LAYERS)


def shifter(slots):
    lane = iota((8, 128), 1)
    y = lax.rem(lane, EDGE)
    row = iota((8, 128), 0)
    col = columns(slots, (8, 128))
    prev = pltpu.roll(col, 1, 0)
    nxt = pltpu.roll(col, 7, 0)
    edge = {1: y == 0, -1: y == EDGE - 1}
    conn = {
        1: edge[1] & (row >= 1) & (col >= 0) & (prev == col - 1),
        -1: edge[-1] & (row < SLOTS - 1) & (nxt >= 0) & (nxt == col + 1),
    }
    low, high = lane < EDGE, lane >= 128 - EDGE

    def yshift(t, cy):
        if cy == 0:
            return t
        a = pltpu.roll(t, cy % 128, 1)
        b = pltpu.roll(pltpu.roll(t, (-15 * cy) % 128, 1), cy % 8, 0)
        return jnp.where(conn[cy], b, jnp.where(edge[cy], 0.0, a))

    def xyshift(t0, t1, v, ghost):
        t0, t1 = yshift(t0, v[1]), yshift(t1, v[1])
        if v[0] == 1:
            r0, r1 = pltpu.roll(t0, EDGE, 1), pltpu.roll(t1, EDGE, 1)
            return jnp.where(low, ghost, r0), jnp.where(low, r0, r1)
        if v[0] == -1:
            r0, r1 = pltpu.roll(t0, 128 - EDGE, 1), pltpu.roll(t1, 128 - EDGE, 1)
            return jnp.where(high, r1, r0), jnp.where(high, ghost, r1)
        return t0, t1

    return xyshift, yshift


def shift_layers(slots, store, moved, first, last):
    xyshift, _ = shifter(slots)

    def body(at, carry):
        r0, r1 = pl.multiple_of(at * 16, 8), pl.multiple_of(at * 16 + 8, 8)
        for n in range(NF):
            t0, t1 = xyshift(store[n, pl.ds(r0, 8), :], store[n, pl.ds(r1, 8), :], vel(n), 0.0)
            moved[n, pl.ds(at * 5, SLOTS), :] = t0[0:SLOTS]
            moved[n, pl.ds(HALF + at * 5, SLOTS), :] = t1[0:SLOTS]
        return carry

    lax.fori_loop(first, last, body, 0)


def shift_kernel(slots_h, store, vstore, moved_in, moved, vmoved, slots, sem):
    del moved_in
    fetch = pltpu.make_async_copy(slots_h, slots, sem.at[0])
    fetch.start()
    for at in range(ZI):
        for half in range(2):
            vmoved[pl.ds(half * HALF + at * 5, SLOTS), :] = vstore[pl.ds(at * 16 + half * 8, SLOTS), :]
    fetch.wait()
    shift_layers(slots, store, moved, 0, EDGE_LAYERS)


def one_side(left, absent, slots, fetch, own, recv, moved, vmoved, gx, ghost_a, adj):
    lane16 = iota((16, 128), 1)
    first, last = lane16 == 0, lane16 == 127

    def yshift_dense(t, cy):
        if cy == 0:
            return t
        a = pltpu.roll(t, cy % 128, 1)
        return jnp.where(first if cy == 1 else last, 0.0, a)

    ghost = [None] * NF
    packs = []
    for p, (n, _, is_ghost) in enumerate(XP + [(None, None, True)]):
        rows = pl.ds(p * ZI, 16)
        t = recv[rows, :]
        if absent is not None and (n is None or not is_ghost):
            t = jnp.where(absent, 0.0, t)
        if n is None:
            v = t
        elif is_ghost:
            ghost[n] = yshift_dense(t, vel(n)[1])
        else:
            packs.append((yshift_dense(t, vel(n)[1]), gx, n))
            ghost[mirror(n, 0)] = yshift_dense(own[rows, :], vel(n)[1])
    m = moments(ghost[:19])
    d = defects(m)
    s = v - 1.0
    a, _ = adjoint(m, d, s, misfit(collide(m, d, s, True), ghost[19:]), True)
    for n in range(19):
        if VEL[n][0] == 1:
            t = jnp.where(v > 0.5, a[OPP[n]], 0.0)
            packs.append((yshift_dense(t, VEL[n][1]), ghost_a, n))
    fetch.wait()
    shifts = [lax.rem((jnp.where(left, 0, 7) - slots[k] + 16) * EDGE, 128) for k in range(SLOTS)]
    for t, dst, n in packs:
        field = jnp.where(left, n, mirror(n, 0))
        for k in range(SLOTS):
            r = pltpu.roll(t, shifts[k], 1)
            dst[field, pl.ds(k, 8, stride=5), :] = r[0:8]
            dst[field, pl.ds(40 + k, ZI - 8, stride=5), :] = r[8:ZI]

    lane = iota((8, 128), 1)
    entry = {1: (lane < EDGE) & left, -1: (lane >= 128 - EDGE) & jnp.logical_not(left)}
    base = jnp.where(left, 0, HALF)

    def advance(i, carry):
        r = pl.ds(pl.multiple_of(base + i * 8, 8), 8)
        f = []
        for n in range(NF):
            t = moved[n, r, :]
            if vel(n)[0]:
                t = jnp.where(entry[vel(n)[0]], gx[n, pl.ds(pl.multiple_of(i * 8, 8), 8), :], t)
            f.append(t)
        v = vmoved[r, :]
        s = v - 1.0
        m = moments(f[:19])
        d = defects(m)
        a, gs = adjoint(m, d, s, misfit(collide(m, d, s, True), f[19:]), True)
        listed = v > 0.5
        for n in range(19):
            adj[n, r, :] = jnp.where(listed, a[OPP[n]], 0.0)
        adj[19, r, :] = gs
        return carry

    lax.fori_loop(0, HALF // 8, advance, 0, unroll=7)


def entry_lanes(left):
    lane = iota((8, 128), 1)
    return ((lane < EDGE) & left) | ((lane >= 128 - EDGE) & jnp.logical_not(left))


def near_kernel(slots_h, moved, vmoved, own, recv, adj, ghost_a, back, slots, gx, sem):
    fetch = pltpu.make_async_copy(slots_h, slots, sem.at[0])
    fetch.start()
    left = jnp.logical_not(even("blk"))
    one_side(left, None, slots, fetch, own, recv, moved, vmoved, gx, ghost_a, adj)
    yshift = shifter(slots)[1]
    base, own_base = jnp.where(left, 0, HALF), jnp.where(left, 0, DZ * 5)
    turn, entry = jnp.where(left, EDGE, 128 - EDGE), entry_lanes(left)

    def pull(z, carry):
        rows = {c: place_of(z + c) * 5 for c in (-1, 0, 1)}
        dst = pl.ds(own_base + z * 5, SLOTS)
        for n in range(19):
            cx, cy, cz = VEL[n]
            if cx < 0:
                continue
            field = jnp.where(left, n, mirror(n, 0)) if cx else n
            t = yshift(adj[field, pl.ds(base + rows[-cz], 8), :], cy)
            if cx:
                t = jnp.where(entry, ghost_a[field, pl.ds(rows[-cz], 8), :], pltpu.roll(t, turn, 1))
            back[field, dst, :] = t[0:SLOTS]
        back[19, dst, :] = adj[19, pl.ds(base + rows[0], SLOTS), :]
        return carry

    lax.fori_loop(0, DZ, pull, 0, unroll=2)


def final_kernel(slots_h, moved, vmoved, mstore, own, recv, adj_in, ghost_in, back_in, grad_h, out_h, adj, ghost_a,
                 back, slots, gx, a0, g0, grad, out, sem):
    del adj_in, ghost_in, back_in
    fetch = pltpu.make_async_copy(slots_h, slots, sem.at[0])
    fetch.start()
    left = even("blk")
    one_side(left, at_end("blk"), slots, fetch, own, recv, moved, vmoved, gx, ghost_a, adj)
    yshift = shifter(slots)[1]
    far, near = jnp.where(left, 0, HALF), jnp.where(left, HALF, 0)
    own_far, own_near = jnp.where(left, 0, DZ * 5), jnp.where(left, DZ * 5, 0)
    turn, other_turn = jnp.where(left, EDGE, 128 - EDGE), jnp.where(left, 128 - EDGE, EDGE)
    entry, other_entry = entry_lanes(left), entry_lanes(jnp.logical_not(left))

    def writes(z):
        lanes = pl.ds(pl.multiple_of(z * 256, 256), 256)
        return (
            pltpu.make_async_copy(out.at[:, :, lanes], out_h.at[:, :, lanes], sem.at[1 + z]),
            pltpu.make_async_copy(grad.at[:, lanes], grad_h.at[:, lanes], sem.at[1 + DZ + z]),
        )

    def pull(z, carry):
        rows = {c: place_of(z + c) * 5 for c in (-1, 0, 1)}
        dst = pl.ds(own_far + z * 5, SLOTS)
        for n in range(19):
            cx, cy, cz = VEL[n]
            src = rows[-cz]
            field = jnp.where(left, n, mirror(n, 0)) if cx else n
            t = yshift(adj[field, pl.ds(far + src, 8), :], cy)
            if cx:
                o = yshift(adj[field, pl.ds(near + src, 8), :], cy)
            if cx == 1:
                t = pltpu.roll(t, turn, 1)
                o = jnp.where(entry, t, pltpu.roll(o, turn, 1))
                back[field, pl.ds(own_near + z * 5, SLOTS), :] = o[0:SLOTS]
                t = jnp.where(entry, ghost_a[field, pl.ds(src, 8), :], t)
            elif cx == -1:
                t = jnp.where(other_entry, pltpu.roll(o, other_turn, 1), pltpu.roll(t, other_turn, 1))
            back[field, dst, :] = t[0:SLOTS]
        back[19, dst, :] = adj[19, pl.ds(far + rows[0], SLOTS), :]
        return carry

    def retreat(i, carry):
        for half in range(2):
            r = pl.ds(pl.multiple_of(half * DZ * 5 + i * 8, 8), 8)
            m = {name: mstore[j, r, :] for j, name in enumerate(M_NAMES)}
            v = mstore[19, r, :]
            listed = v > 0.5
            s = v - 1.0
            a, gs = adjoint(m, defects(m), s, [back[OPP[j], r, :] for j in range(19)])
            for j in range(19):
                a0[pl.ds(pl.multiple_of(j * ROWS_OWN + half * DZ * 5 + i * 8, 8), 8), :] = jnp.where(listed, a[j], 0.0)
            g0[r, :] = jnp.where(listed & (v < 1.75), gs + back[19, r, :], 0.0)
        return carry

    def send(z, carry):
        for half in range(2):
            lanes = pl.ds(pl.multiple_of(z * 256 + half * 128, 128), 128)
            base = half * DZ * 5 + z * 5
            for k in range(SLOTS):
                out[k, :, lanes] = a0[pl.ds(base + k, 19, stride=ROWS_OWN), :]
            grad[:, lanes] = g0[pl.ds(base, SLOTS), :]
        for c in writes(z):
            c.start()
        return carry

    lax.fori_loop(0, DZ, pull, 0, unroll=2)
    lax.fori_loop(0, 3, retreat, 0)
    lax.fori_loop(0, 4, send, 0)
    lax.fori_loop(3, DZ * 5 // 8, retreat, 0)
    lax.fori_loop(4, DZ, send, 0)

    def finish(z, carry):
        for c in writes(z):
            c.wait()
        return carry

    lax.fori_loop(0, DZ, finish, 0)


HBM = pl.BlockSpec(memory_space=pltpu.HBM)
VMEM = pl.BlockSpec(memory_space=pltpu.VMEM)


def exchange(inside, across, axis):
    rows, depth = lax.axis_size("blk"), lax.axis_size("gz")
    along_gz = axis == "gz"
    count = depth if along_gz else rows
    index = (lambda at, other: other * depth + at) if along_gz else (lambda at, other: at * depth + other)
    second = []
    for other in range(rows if along_gz else depth):
        for at in range(1, count - 1, 2):
            second += [(index(at, other), index(at + 1, other)), (index(at + 1, other), index(at, other))]
        second += [(index(at, other), index(at, other ^ 1)) for at in (0, count - 1)]
    first = [(i, i ^ 1) for i in range(count)]
    if inside is not None:
        inside = lax.ppermute(inside, axis, first)
    if across is not None:
        across = lax.ppermute(across, ("blk", "gz"), second)
    return inside, across


def at_end(axis):
    at = lax.axis_index(axis)
    return (at == 0) | (at == lax.axis_size(axis) - 1)


def per_device(populations, target, solid_frac, wall_mask, slot_column):
    f32 = jnp.float32
    populations = jnp.transpose(populations, (1, 0, 2))
    target = jnp.transpose(target, (1, 0, 2))
    populations, target, solid_frac, wall_mask, slot_column = (
        pltpu.with_memory_space_constraint(x, pltpu.HBM) for x in (populations, target, solid_frac, wall_mask, slot_column)
    )

    def params(mib):
        return pltpu.CompilerParams(vmem_limit_bytes=mib << 20)

    def inputs(cells):
        return [
            pltpu.SMEM((SLOTS,), jnp.int32),
            pltpu.VMEM((SLOTS, 19, cells), f32),
            pltpu.VMEM((SLOTS, 19, cells), jnp.bfloat16),
            pltpu.VMEM((SLOTS, cells), f32),
            pltpu.VMEM((SLOTS, cells), jnp.int32),
            pltpu.VMEM((cells // 128, 8 * SLOT_ROWS, 128), f32),
            pltpu.VMEM((cells // 128, 8 * SLOT_ROWS, 128), f32),
            pltpu.VMEM((8, cells), f32),
            pltpu.SemaphoreType.DMA((9,)),
        ]

    slots_in = [pltpu.SMEM((SLOTS,), jnp.int32)]
    zbuf = jax.ShapeDtypeStruct((ZROWS, 256), f32)
    inside, across = pl.pallas_call(
        border_kernel,
        in_specs=[HBM] * 5,
        out_specs=[VMEM] * 2,
        out_shape=[zbuf, zbuf],
        scratch_shapes=inputs(1024),
        compiler_params=params(8),
    )(slot_column, populations, target, solid_frac, wall_mask)
    r_inside, r_across = exchange(inside, across, "gz")
    store_t = jax.ShapeDtypeStruct((NF, ROWS_STORE, 128), f32)
    vstore_t = jax.ShapeDtypeStruct((ROWS_STORE, 128), f32)
    xbuf = jax.ShapeDtypeStruct((XROWS, 128), f32)
    xbuf2 = jax.ShapeDtypeStruct((XROWS + 8, 128), f32)
    moved_t = jax.ShapeDtypeStruct((NF, ROWS_COMPACT, 128), f32)
    store, vstore, mstore, moved, inside, across = pl.pallas_call(
        fields_kernel,
        in_specs=[HBM] * 5,
        out_specs=[VMEM] * 6,
        out_shape=[store_t, vstore_t, jax.ShapeDtypeStruct((20, ROWS_OWN, 128), f32), moved_t, xbuf, xbuf2],
        scratch_shapes=inputs(CELLS),
        compiler_params=params(12),
    )(slot_column, populations, target, solid_frac, wall_mask)
    store, vstore, across, inside = pl.pallas_call(
        side_kernel,
        in_specs=[HBM] + [VMEM] * 6,
        out_specs=[VMEM] * 4,
        out_shape=[store_t, vstore_t, xbuf2, xbuf],
        input_output_aliases={1: 0, 2: 1, 3: 2, 4: 3},
        scratch_shapes=slots_in + [pltpu.SemaphoreType.DMA((1,))],
        compiler_params=params(12),
    )(slot_column, store, vstore, across, inside, r_inside, r_across)
    _, r_across = exchange(None, across, "blk")
    r_inside, _ = exchange(inside, None, "blk")
    moved, vmoved = pl.pallas_call(
        shift_kernel,
        in_specs=[HBM] + [VMEM] * 3,
        out_specs=[VMEM] * 2,
        out_shape=[moved_t, jax.ShapeDtypeStruct((ROWS_COMPACT, 128), f32)],
        input_output_aliases={3: 0},
        scratch_shapes=slots_in + [pltpu.SemaphoreType.DMA((1,))],
        compiler_params=params(12),
    )(slot_column, store, vstore, moved)
    gx_t = pltpu.VMEM((NF, HALF, 128), f32)
    adj_t = jax.ShapeDtypeStruct((20, ROWS_COMPACT, 128), f32)
    ghost_t = jax.ShapeDtypeStruct((19, HALF, 128), f32)
    back_t = jax.ShapeDtypeStruct((20, ROWS_OWN, 128), f32)
    adj, ghost_a, back = pl.pallas_call(
        near_kernel,
        in_specs=[HBM] + [VMEM] * 4,
        out_specs=[VMEM] * 3,
        out_shape=[adj_t, ghost_t, back_t],
        scratch_shapes=slots_in + [gx_t, pltpu.SemaphoreType.DMA((1,))],
        compiler_params=params(12),
    )(slot_column, moved, vmoved, inside, r_inside)
    grad, adjoint_out, _, _, _ = pl.pallas_call(
        final_kernel,
        in_specs=[HBM] + [VMEM] * 8,
        out_specs=[HBM, HBM, VMEM, VMEM, VMEM],
        out_shape=[
            jax.ShapeDtypeStruct((SLOTS, CELLS), f32),
            jax.ShapeDtypeStruct((SLOTS, 19, CELLS), f32),
            adj_t,
            ghost_t,
            back_t,
        ],
        input_output_aliases={6: 2, 7: 3, 8: 4},
        scratch_shapes=slots_in + [
            gx_t,
            pltpu.VMEM((19 * ROWS_OWN, 128), f32),
            pltpu.VMEM((ROWS_OWN, 128), f32),
            pltpu.VMEM((SLOTS, CELLS), f32),
            pltpu.VMEM((SLOTS, 19, CELLS), f32),
            pltpu.SemaphoreType.DMA((1 + 2 * DZ,)),
        ],
        compiler_params=params(20),
    )(slot_column, moved, vmoved, mstore, across, r_across, adj, ghost_a, back)
    return grad, jnp.transpose(adjoint_out, (1, 0, 2))


def solution(mesh):
    return jax.shard_map(
        per_device,
        mesh=mesh,
        in_specs=(
            P(None, "blk", "gz"),
            P(None, "blk", "gz"),
            P("blk", "gz"),
            P("blk", "gz"),
            P("blk"),
        ),
        out_specs=(P("blk", "gz"), P(None, "blk", "gz")),
        check_vma=False,
    )
```
